128 devices in a mesh: batch: 8 (over x, core), ctx: 16 (over y, z).
Axes of the slice: x: 4, y: 4, z: 4, core: 2. Of those that a mesh axis runs over, the one named last changes fastest.
Arguments:
- event_rows: bfloat16 [8, 4096, 256], P('batch', 'ctx'), may hold values from -6 to 6
- event_index: int32 [8, 4096], P('batch', 'ctx'), may hold values from 0 to 65535, as said below
- decay: float32 [8, 16, 4096], P('batch', None, 'ctx'), may hold values from 0.15 to 1
- saved_state: float32 [8, 16, 16, 128, 64], P('batch', 'ctx'), may hold values from -6 to 6
- dout: bfloat16 [8, 4096, 512], P('batch', 'ctx'), may hold values from -0.29882812 to 0.29882812
- w_up: bfloat16 [256, 512], replicated, may hold values from -0.375 to 0.375
- w_in: bfloat16 [512, 1280], replicated, may hold values from -0.25 to 0.25
- w_out: bfloat16 [1024, 512], replicated, may hold values from -0.1875 to 0.1875
- skip: float32 [16], replicated, may hold values from 0.5 to 2
Outputs:
- grad_up: float32 [256, 512], replicated
- grad_in: float32 [512, 1280], replicated
- grad_out: float32 [1024, 512], replicated
- grad_skip: float32 [16], replicated
- grad_table: float32 [65536, 256], P(('batch', 'ctx'))
The draws below stay inside these ranges and needn't reach their ends.
Inputs may be any that keep to these rules, and one draw needn't show every extreme that they name: `event_index`: rows are in blocks of 512; block k is held by device k of batch+ctx. The 256 events of one device name rows of at most 4 events in any one block, and in every draw some block is named by exactly 4 events of every device.
All inputs are finite; a program needn't handle non-finite values.
Results may differ from the reference program's by a relative error of at most 0.011.
Values may be sent and summed in bfloat16 or wider, within the bound.
No kernel may reach another device: no remote copies, remote signals or barrier semaphores. Data moves between devices by JAX's collectives and lax.ppermute only.
A program may use at most 128 MiB of HBM per device.

```python
from functools import partial
import jax
import jax.numpy as jnp
from jax import lax

D = 512
E = 256
HEADS = 16
HEAD = 64
STATE = 128
CH = 256
TOK_DEV = 256
ROWS_DEV = 512
INNER = 1024
PROJ = 1280
BATCH = 8
CTX_SHARDS = 16
SEQ = 4096
ROWS = 65536
CAP = 4
DEVICES = 128


def draw_decay(key, part):
    key_fast, key_rough, key_piece, key_spot, key_depth = jax.random.split(key, 5)
    is_fast = jax.random.randint(key_fast, (BATCH, HEADS, 1), 0, 2) == 0
    baseline_intensity = jnp.where(is_fast, 1.0 / 40.0, 0.3 / SEQ)
    coarse_estimate = jnp.exp(jax.random.uniform(key_rough, (BATCH, HEADS, SEQ), minval=-0.7, maxval=0.7))
    segment_multiplier = jnp.exp(jax.random.uniform(key_piece, (BATCH, HEADS, CTX_SHARDS, 1), minval=-0.7, maxval=0.7))
    segment_multiplier = jnp.broadcast_to(segment_multiplier, (BATCH, HEADS, CTX_SHARDS, TOK_DEV)).reshape(BATCH, HEADS, SEQ)
    marked_places = jax.random.randint(key_spot, (BATCH, 1, 3, 1), 0, SEQ)
    nesting_level = jax.random.uniform(key_depth, (BATCH, 1, 3, 1), minval=0.22, maxval=0.5)
    event_location = jnp.arange(SEQ, dtype=jnp.int32)[None, None, None, :]
    excitation_jump = jnp.sum(jnp.where(marked_places == event_location, nesting_level, 0.0), axis=2)
    return jnp.exp(-baseline_intensity * coarse_estimate * segment_multiplier - excitation_jump).astype(jnp.float32)


def draw_event_index(key, part):
    key_full, key_rank, key_score, key_order, key_row = jax.random.split(key, 5)
    owner_total = DEVICES
    full_owner = jax.random.randint(key_full, (), 0, owner_total)
    owner_rank = jax.random.permutation(key_rank, owner_total).astype(jnp.int32)
    owner_of_slot = jnp.repeat(jnp.arange(owner_total, dtype=jnp.int32), CAP)
    score = jax.random.randint(key_score, (BATCH, CTX_SHARDS, owner_total * CAP), 0, 65536) + owner_rank[owner_of_slot] * 1024
    score = jnp.where(owner_of_slot == full_owner, -1, score)
    chosen = jnp.argsort(score, axis=-1, stable=True)[..., :TOK_DEV]
    owners = owner_of_slot[chosen]
    order = jnp.argsort(jax.random.randint(key_order, (BATCH, CTX_SHARDS, TOK_DEV), 0, 1 << 30), axis=-1, stable=True)
    owners = jnp.take_along_axis(owners, order, axis=-1)
    local_row = jax.random.randint(key_row, (BATCH, CTX_SHARDS, TOK_DEV), 0, ROWS_DEV)
    return (owners * ROWS_DEV + local_row).reshape(BATCH, SEQ).astype(jnp.int32)


def shard_levels(own_key, extent, shards, low, high):
    level = 1.0
    for dim, shards_of in shards:
        steps = jax.random.uniform(jax.random.fold_in(jax.random.fold_in(own_key, 6), dim), (shards_of,), jnp.float32, low / len(shards), high / len(shards))
        level = level * jnp.repeat(jnp.exp(steps), extent[dim] // shards_of).reshape((-1,) + (1,) * (len(extent) - 1 - dim))
    return level


def gaussian(rng, shape, width, most, cuts=(), held_as=jnp.bfloat16):
    values = width * jax.random.normal(rng, shape, jnp.float32)
    if cuts:
        values = values * shard_levels(rng, shape, cuts, -0.22, 0.18)
    return jnp.clip(values, -most, most).astype(held_as)


def setup_inputs(seed: int = 0) -> dict:
    streams_of = jax.random.split(jax.random.key(seed), 10)
    return {
        "event_rows": gaussian(streams_of[0], (BATCH, SEQ, E), 1.0, 6.0, ((0, 8), (1, 16))),
        "event_index": draw_event_index(jax.random.fold_in(streams_of[9], 71), 0),
        "decay": draw_decay(jax.random.fold_in(streams_of[9], 71), 0),
        "saved_state": gaussian(streams_of[3], (BATCH, CTX_SHARDS, HEADS, STATE, HEAD), 1.0, 6.0, ((0, 8), (1, 16)), jnp.float32),
        "dout": gaussian(streams_of[4], (BATCH, SEQ, D), 0.05, 0.29882812, ((0, 8), (1, 16))),
        "w_up": gaussian(streams_of[5], (E, D), E ** -0.5, 0.375),
        "w_in": gaussian(streams_of[6], (D, PROJ), D ** -0.5, 0.25),
        "w_out": gaussian(streams_of[7], (INNER, D), INNER ** -0.5, 0.1875),
        "skip": jnp.clip(jax.random.uniform(streams_of[8], (HEADS,), jnp.float32, 0.5, 2.0), 0.5, 2.0),
    }


STEP_SIZE = 0.0625
exact_sum = partial(jnp.einsum, precision=lax.Precision.HIGHEST)


def block_parts(log_decay):
    cum_log = jnp.cumsum(log_decay, axis=1)
    length = log_decay.shape[1]
    causal = jnp.arange(length)[:, None] >= jnp.arange(length)[None, :]
    log_gap = cum_log[:, :, None] - cum_log[:, None, :]
    decay_mask = jnp.where(causal[None], jnp.exp(jnp.where(causal[None], log_gap, 0.0)), 0.0)
    return cum_log, decay_mask


def forward_block(h_start, x_part, b_part, c_part, log_decay, skip):
    state_scale = c_part.shape[1] ** -0.5
    cum_log, decay_mask = block_parts(log_decay)
    start_decay = jnp.exp(cum_log)
    c_dot_b = exact_sum("tn,sn->ts", c_part, b_part)
    within = STEP_SIZE * exact_sum("hts,ts,shp->thp", decay_mask, c_dot_b, x_part)
    from_start = exact_sum("tn,hnp->thp", c_part, h_start) * start_decay.T[:, :, None]
    y_out = state_scale * (from_start + within) + skip[None, :, None] * x_part
    tail_decay = jnp.exp(cum_log[:, -1:] - cum_log)
    h_end = jnp.exp(cum_log[:, -1])[:, None, None] * h_start + STEP_SIZE * exact_sum("hs,sn,shp->hnp", tail_decay, b_part, x_part)
    return y_out, h_end


def block_summary(c_part, dy_part, log_decay):
    state_scale = c_part.shape[1] ** -0.5
    cum_log = jnp.cumsum(log_decay, axis=1)
    amount = jnp.exp(cum_log[:, -1])
    block_sums = state_scale * exact_sum("ht,tn,thp->hnp", jnp.exp(cum_log), c_part, dy_part)
    return amount, block_sums


def backward_block(carry_in, h_start, x_part, b_part, c_part, dy_part, log_decay, skip):
    state_scale = c_part.shape[1] ** -0.5
    cum_log, decay_mask = block_parts(log_decay)
    start_decay = jnp.exp(cum_log)
    tail_decay = jnp.exp(cum_log[:, -1:] - cum_log)
    mask_back = jnp.swapaxes(decay_mask, 1, 2)
    b_dot_c = exact_sum("tn,sn->ts", b_part, c_part)
    x_dot_dy = exact_sum("thp,shp->hts", x_part, dy_part)
    dy_dot_x = jnp.swapaxes(x_dot_dy, 1, 2)
    dx_part = STEP_SIZE * (state_scale * exact_sum("hts,ts,shp->thp", mask_back, b_dot_c, dy_part)
                           + tail_decay.T[:, :, None] * exact_sum("tn,hnp->thp", b_part, carry_in)) + skip[None, :, None] * dy_part
    db_part = STEP_SIZE * (state_scale * exact_sum("hts,sn->tn", mask_back * x_dot_dy, c_part)
                           + exact_sum("ht,hnp,thp->tn", tail_decay, carry_in, x_part))
    dc_part = state_scale * (exact_sum("ht,hnp,thp->tn", start_decay, h_start, dy_part)
                             + STEP_SIZE * exact_sum("hts,sn->tn", decay_mask * dy_dot_x, b_part))
    dskip_part = exact_sum("thp,thp->h", x_part, dy_part)
    return dx_part, db_part, dc_part, dskip_part


def one_history(history_rows, history_index, history_decay, saved_blocks, history_dout, w_up, w_in, w_out, skip):
    length = history_rows.shape[0]
    inner_width = w_out.shape[0]
    head_count = skip.shape[0]
    head_size = inner_width // head_count
    state_width = (w_in.shape[1] - inner_width) // 2
    block_count = length // CH
    per_piece = TOK_DEV // CH
    u_rows = jnp.dot(history_rows, w_up, preferred_element_type=jnp.float32).astype(jnp.bfloat16)
    projected = jnp.dot(u_rows, w_in, preferred_element_type=jnp.float32).astype(jnp.bfloat16)
    dy_rows = jnp.dot(history_dout, w_out.T, preferred_element_type=jnp.float32).astype(jnp.bfloat16)
    x_all = projected[:, :inner_width].astype(jnp.float32).reshape(block_count, CH, head_count, head_size)
    b_all = projected[:, inner_width:inner_width + state_width].astype(jnp.float32).reshape(block_count, CH, state_width)
    c_all = projected[:, inner_width + state_width:].astype(jnp.float32).reshape(block_count, CH, state_width)
    dy_all = dy_rows.astype(jnp.float32).reshape(block_count, CH, head_count, head_size)
    log_all = jnp.log(history_decay).reshape(head_count, block_count, CH).transpose(1, 0, 2)

    def forward_step(h_state, block):
        x_part, b_part, c_part, log_decay, block_number = block
        saved_here = lax.dynamic_index_in_dim(saved_blocks, (block_number // per_piece).astype(jnp.int32), 0, keepdims=False)
        h_start = jnp.where(block_number % per_piece == 0, saved_here, h_state)
        y_out, h_end = forward_block(h_start, x_part, b_part, c_part, log_decay, skip)
        return h_end, (y_out, h_start)

    zero_state = jnp.zeros((head_count, state_width, head_size), jnp.float32)
    _, (y_blocks, starts) = lax.scan(forward_step, zero_state,
                                     (x_all, b_all, c_all, log_all, jnp.arange(block_count, dtype=jnp.int32)))
    y_rows = y_blocks.reshape(length, inner_width).astype(jnp.bfloat16)

    def backward_step(carried, block):
        h_start, x_part, b_part, c_part, dy_part, log_decay = block
        grads = backward_block(carried, h_start, x_part, b_part, c_part, dy_part, log_decay, skip)
        amount, block_sums = block_summary(c_part, dy_part, log_decay)
        return block_sums + amount[:, None, None] * carried, grads

    _, (dx_all, db_all, dc_all, dskip_all) = lax.scan(backward_step, zero_state,
                                                      (starts, x_all, b_all, c_all, dy_all, log_all), reverse=True)
    dprojected = jnp.concatenate([dx_all.reshape(length, inner_width), db_all.reshape(length, state_width),
                                  dc_all.reshape(length, state_width)], axis=1).astype(jnp.bfloat16)
    grad_out = jnp.dot(y_rows.T, history_dout, preferred_element_type=jnp.float32)
    grad_in = jnp.dot(u_rows.T, dprojected, preferred_element_type=jnp.float32)
    du_rows = jnp.dot(dprojected, w_in.T, preferred_element_type=jnp.float32).astype(jnp.bfloat16)
    grad_up = jnp.dot(history_rows.T, du_rows, preferred_element_type=jnp.float32)
    de_rows = jnp.dot(du_rows, w_up.T, preferred_element_type=jnp.float32).astype(jnp.bfloat16)
    grad_table = jax.ops.segment_sum(de_rows.astype(jnp.float32), history_index, num_segments=ROWS)
    return grad_up, grad_in, grad_out, jnp.sum(dskip_all, axis=0), grad_table


def reference(event_rows, event_index, decay, saved_state, dout, w_up, w_in, w_out, skip):
    def accumulate(totals, item):
        history_rows, history_index, history_decay, saved_blocks, history_dout = item
        parts = one_history(history_rows, history_index, history_decay, saved_blocks, history_dout, w_up, w_in, w_out, skip)
        return tuple(total + part for total, part in zip(totals, parts)), None

    initial = (jnp.zeros(w_up.shape, jnp.float32), jnp.zeros(w_in.shape, jnp.float32),
               jnp.zeros(w_out.shape, jnp.float32), jnp.zeros(skip.shape, jnp.float32),
               jnp.zeros((ROWS, event_rows.shape[2]), jnp.float32))
    totals, _ = lax.scan(accumulate, initial, (event_rows, event_index, decay, saved_state, dout))
    return totals[0], totals[1], totals[2], totals[3], totals[4]
```

```python
from functools import partial

import jax
import jax.numpy as jnp
from jax import lax
from jax.experimental import pallas as pl
from jax.experimental.pallas import tpu as pltpu
from jax.sharding import PartitionSpec as P

T = 256
E = 256
D = 512
H = 16
HP = 64
N = 128
INNER = H * HP
PROJ = INNER + 2 * N
ROWS_DEV = 512
CAP = 4
DEV = 128
CTX = 16
SROWS = 80

DT = 0.0625
SC = 128.0**-0.5
F32 = jnp.float32
BF = jnp.bfloat16
NN = (((1,), (0,)), ((), ()))
NT = (((1,), (1,)), ((), ()))
TN = (((0,), (0,)), ((), ()))
MB = 1 << 20


def dot(a, b, dims=NN):
    return lax.dot_general(a, b, dims, preferred_element_type=F32)


def split3(v):
    hi = v.astype(BF)
    rest = v - hi.astype(F32)
    mid = rest.astype(BF)
    return hi, mid, (rest - mid.astype(F32)).astype(BF)


def call(kernel, outs, vmem, flops, nbytes, **kw):
    return pl.pallas_call(
        kernel,
        out_shape=tuple(jax.ShapeDtypeStruct(s, d) for s, d in outs),
        compiler_params=pltpu.CompilerParams(vmem_limit_bytes=vmem * MB),
        cost_estimate=pl.CostEstimate(flops=flops, bytes_accessed=nbytes, transcendentals=0),
        **kw,
    )


VM = pl.BlockSpec(memory_space=pltpu.VMEM)
SM = pl.BlockSpec(memory_space=pltpu.SMEM)


def project_kernel(rows_ref, dout_ref, decay_ref, w_up_ref, w_in_ref, w_out_ref,
                   proj_ref, dy_ref, cum_ref, cumt_ref, send_ref):
    u = dot(rows_ref[...], w_up_ref[...]).astype(BF)
    proj_ref[...] = dot(u, w_in_ref[...]).astype(BF)
    dy_ref[...] = dot(w_out_ref[...], dout_ref[...], NT).astype(BF)
    logs = split3(jnp.log(decay_ref[...]))
    r = lax.broadcasted_iota(jnp.int32, (T, T), 0)
    c = lax.broadcasted_iota(jnp.int32, (T, T), 1)
    upper = (r <= c).astype(F32).astype(BF)
    lower = (c <= r).astype(F32).astype(BF)
    cum = sum(dot(p, upper) for p in logs)
    cum_ref[...] = cum
    cumt_ref[...] = sum(dot(lower, p, NT) for p in logs)
    start = jnp.exp(cum)
    c_nat = proj_ref[:, INNER + N :]
    scaled = jnp.concatenate(
        [
            (dy_ref[h * HP : (h + 1) * HP, :].astype(F32) * (SC * start[h : h + 1, :])).astype(BF)
            for h in range(H)
        ],
        axis=0,
    )
    sums = dot(scaled, c_nat).astype(BF)
    amount = jnp.exp(cum[:, T - 1 : T])
    parts = [jnp.broadcast_to(p.astype(F32), (H, N)) for p in split3(amount)]
    row = lax.broadcasted_iota(jnp.int32, (SROWS - HP, N), 0)
    for h in range(H):
        send_ref[h, 0:HP, :] = sums[h * HP : (h + 1) * HP, :]
        tail = jnp.where(
            row == 0,
            parts[0][h : h + 1, :],
            jnp.where(row == 1, parts[1][h : h + 1, :], jnp.where(row == 2, parts[2][h : h + 1, :], 0.0)),
        )
        send_ref[h, HP:SROWS, :] = tail.astype(BF)


def scan_kernel(got_ref, out_ref):
    carry = jnp.zeros((HP, N), F32)
    for j in range(CTX - 1, -1, -1):
        out_ref[j, :, :] = carry.astype(BF)
        if j:
            tail = got_ref[j, HP:SROWS, :].astype(F32)
            amount = tail[0:1, :] + tail[1:2, :] + tail[2:3, :]
            carry = got_ref[j, 0:HP, :].astype(F32) + amount * carry


def local_kernel(proj_ref, dy_ref, cum_ref, cumt_ref, h0_ref, dout_ref, index_ref, skip_ref,
                 gout_ref, dx_ref, dbt_ref, dct_ref, misc_ref, hits_ref, y_ref, sdy_ref, h0t_ref, sum_ref):
    proj_t = jnp.transpose(proj_ref[...])
    bt = proj_t[INNER : INNER + N, :]
    ct = proj_t[INNER + N :, :]
    b_nat = proj_ref[:, INNER : INNER + N]
    c_nat = proj_ref[:, INNER + N :]
    pair = (SC * DT) * dot(b_nat, c_nat, NT)
    r = lax.broadcasted_iota(jnp.int32, (N, N), 0)
    c = lax.broadcasted_iota(jnp.int32, (N, N), 1)
    causal = r <= c
    cum = cum_ref[...]
    cumt = cumt_ref[...]
    start = jnp.exp(cum)
    for h in range(H):
        h0t_ref[h * HP : (h + 1) * HP, :] = jnp.transpose(h0_ref[h]).astype(BF)
    y_ref[...] = dot(h0t_ref[...], ct)
    skip_sums = []
    a00 = jnp.zeros((N, N), F32)
    a01 = jnp.zeros((N, N), F32)
    a11 = jnp.zeros((N, N), F32)
    zero = jnp.zeros((N, N), BF)
    zrow = jnp.zeros((HP, T), BF)
    for h in range(H):
        lo, hi = h * HP, (h + 1) * HP
        row0, row1 = cum[h : h + 1, :N], cum[h : h + 1, N:]
        col0, col1 = cumt[:N, h : h + 1], cumt[N:, h : h + 1]
        m00 = jnp.exp(jnp.where(causal, row0 - col0, -1e30))
        m01 = jnp.exp(row1 - col0)
        m11 = jnp.exp(jnp.where(causal, row1 - col1, -1e30))
        weights = jnp.concatenate(
            [
                jnp.concatenate([(m00 * pair[:N, :N]).astype(BF), (m01 * pair[:N, N:]).astype(BF)], axis=1),
                jnp.concatenate([zero, (m11 * pair[N:, N:]).astype(BF)], axis=1),
            ],
            axis=0,
        )
        x_h = proj_t[lo:hi, :]
        dy_h = dy_ref[lo:hi, :]
        x_f, dy_f = x_h.astype(F32), dy_h.astype(F32)
        st = start[h : h + 1, :]
        skip = skip_ref[h]
        y_ref[lo:hi, :] = dot(x_h, weights) + SC * st * y_ref[lo:hi, :] + skip * x_f
        dx_ref[lo:hi, :] = dot(dy_h, weights, NT) + skip * dy_f
        sdy_ref[lo:hi, :] = (st * dy_f).astype(BF)
        x_pair = proj_ref[:, (h // 2) * N : (h // 2 + 1) * N]
        dy_z = jnp.concatenate([dy_h, zrow] if h % 2 == 0 else [zrow, dy_h], axis=0)
        q0 = dot(x_pair[:N, :], dy_z)
        q11 = dot(x_pair[N:, :], dy_z[:, N:])
        a00 += m00 * q0[:, :N]
        a01 += m01 * q0[:, N:]
        a11 += m11 * q11
        skip_sums.append(jnp.sum(x_f * dy_f, keepdims=True))
    gout_ref[...] = dot(y_ref[...].astype(BF), dout_ref[...]).astype(BF)
    sum_ref[:N, :N] = a00.astype(BF)
    sum_ref[:N, N:] = a01.astype(BF)
    sum_ref[N:, :N] = zero
    sum_ref[N:, N:] = a11.astype(BF)
    a = sum_ref[...]
    dct_ref[...] = (SC * (DT * dot(bt, a) + dot(h0t_ref[...], sdy_ref[...], TN))).astype(BF)
    dbt_ref[...] = (DT * SC) * dot(ct, a, NT)
    index = index_ref[...]
    owner_row = lax.shift_right_logical(index, 9)
    rr = lax.broadcasted_iota(jnp.int32, (T, T), 0)
    cc = lax.broadcasted_iota(jnp.int32, (T, T), 1)
    index_col = jnp.sum(jnp.where(rr == cc, index.astype(F32), 0.0), axis=1, keepdims=True)
    index_col = index_col.astype(jnp.int32)
    owner_col = lax.shift_right_logical(index_col, 9)
    same = owner_col == owner_row
    rank_row = jnp.sum(jnp.where(same & (rr < cc), 1.0, 0.0), axis=0, keepdims=True).astype(jnp.int32)
    rank_col = jnp.sum(jnp.where(same & (cc < rr), 1.0, 0.0), axis=1, keepdims=True).astype(jnp.int32)
    local_col = index_col - owner_col * ROWS_DEV
    id_hi = lax.shift_right_logical(local_col, 1)
    id_lo = local_col - 2 * id_hi
    v = jnp.where(cc == rank_col, id_hi, jnp.where(cc == rank_col + 64, id_lo, 0))
    row_id = lax.broadcasted_iota(jnp.int32, (8 * DEV, T), 0)
    hits_ref[...] = jnp.where(row_id == owner_row * 8 + 2 + rank_row, 1.0, 0.0).astype(BF)
    heads = jnp.where(row_id == owner_row * 8 + 6, 1.0, 0.0).astype(BF)
    lane = lax.broadcasted_iota(jnp.int32, (1, T), 1)
    extra = jnp.zeros((1, T), F32)
    for h in range(H):
        whole = skip_sums[h]
        top = whole.astype(BF).astype(F32)
        extra = extra + jnp.where(lane == 128 + h, top, 0.0) + jnp.where(lane == 160 + h, whole - top, 0.0)
    misc = dot(heads, v.astype(F32).astype(BF))
    misc_ref[...] = misc + jnp.where((row_id & 7) == 6, extra, 0.0)


def finish_kernel(carry_ref, proj_ref, cum_ref, dx_ref, dbt_ref, dct_ref, misc_ref, hits_ref, rows_ref,
                  w_in_ref, w_up_ref, out_ref, d_ref, tx_ref):
    proj_t = jnp.transpose(proj_ref[...])
    bt = proj_t[INNER : INNER + N, :]
    cum = cum_ref[...]
    tail = DT * jnp.exp(cum[:, T - 1 : T] - cum)
    carry = carry_ref[...]
    entering = dot(carry, bt)
    for h in range(H):
        lo, hi = h * HP, (h + 1) * HP
        tl = tail[h : h + 1, :]
        d_ref[lo:hi, :] = (dx_ref[lo:hi, :] + tl * entering[lo:hi, :]).astype(BF)
        tx_ref[lo:hi, :] = (tl * proj_t[lo:hi, :].astype(F32)).astype(BF)
    d_ref[INNER : INNER + N, :] = (dbt_ref[...] + dot(carry, tx_ref[...], TN)).astype(BF)
    d_ref[INNER + N :, :] = dct_ref[...]
    d = d_ref[...]
    g = dot(d, rows_ref[...]).astype(BF)
    out_ref[:, :E] = g[:INNER, :]
    du = dot(w_in_ref[...], d).astype(BF)
    de = dot(w_up_ref[...], du).astype(BF)
    r = lax.broadcasted_iota(jnp.int32, (8 * DEV, 2 * N), 0)
    j = lax.broadcasted_iota(jnp.int32, (1, 2 * N), 1)
    place = jnp.where(r == 8 * lax.shift_right_logical(j, 1) + (j & 1), 1.0, 0.0).astype(BF)
    misc = misc_ref[...] + dot(hits_ref[...], de, NT) + dot(place, g[INNER:, :])
    out_ref[:, E:] = misc.astype(BF)


def sum_kernel(got_ref, go_ref, chunk_ref, skip_ref):
    a = jnp.sum(got_ref[...].astype(F32), axis=0)
    b = jnp.sum(go_ref[...].astype(F32), axis=0)
    chunk = jnp.concatenate([a, b], axis=1)
    chunk_ref[...] = jnp.broadcast_to(chunk[None], chunk_ref.shape).astype(BF)
    skip_ref[...] = a[6:7, E + 128 : E + 256]


def table_kernel(got_ref, table_ref):
    misc = got_ref[:, :, E:]
    ids = misc[:, 6:7, 0:128].astype(F32)
    sub = lax.broadcasted_iota(jnp.int32, (DEV, 8, 128), 1) - 2
    lane = lax.broadcasted_iota(jnp.int32, (DEV, 8, 128), 2)
    want = jnp.where(lane == sub, 2.0, jnp.where(lane == sub + 64, 1.0, 0.0))
    row = jnp.sum(ids * want, axis=2, keepdims=True)
    row = jnp.where((sub[:, :, :1] >= 0) & (sub[:, :, :1] < CAP), row, -1.0)
    rid = lax.broadcasted_iota(jnp.int32, (DEV, 8, ROWS_DEV), 2).astype(F32)
    hits = jnp.where(rid == row, 1.0, 0.0).reshape(DEV * 8, ROWS_DEV).astype(BF)
    table_ref[...] = dot(hits, got_ref[...].reshape(DEV * 8, 2 * E)[:, E:], TN)


def last_kernel(got_ref, w_up_ref, w_in_ref, up_ref, in_ref, out_ref):
    got = got_ref[...].reshape(DEV * 8, 4 * E)
    out_ref[...] = got[:, 2 * E :].astype(F32)
    j = lax.broadcasted_iota(jnp.int32, (2 * N, 8 * DEV), 0)
    r = lax.broadcasted_iota(jnp.int32, (2 * N, 8 * DEV), 1)
    pick = jnp.where(r == 8 * lax.shift_right_logical(j, 1) + (j & 1), 1.0, 0.0).astype(BF)
    g = jnp.concatenate([got[:, :E], dot(pick, got[:, E : 2 * E]).astype(BF)], axis=0)
    in_ref[...] = lax.dot_general(w_up_ref[...], g, (((0,), (1,)), ((), ())), preferred_element_type=F32)
    up_ref[...] = jnp.transpose(dot(w_in_ref[...], g))


def local(event_rows, event_index, decay, saved_state, dout, w_up, w_in, w_out, skip):
    every = ("batch", "ctx")
    rows, d_out = event_rows[0], dout[0]
    proj, dy, cum, cumt, send = call(
        project_kernel,
        [((T, PROJ), BF), ((INNER, T), BF), ((H, T), F32), ((T, H), F32), ((H, SROWS, N), BF)],
        32, 750_000_000, 4_500_000,
        in_specs=[VM] * 6, out_specs=(VM,) * 5,
    )(rows, d_out, decay[0], w_up, w_in, w_out)
    got = lax.all_to_all(send, "ctx", 0, 0, tiled=True)
    gout, dx, dbt, dct, misc, hits = call(
        local_kernel,
        [((INNER, D), BF), ((INNER, T), F32), ((N, T), F32), ((N, T), BF), ((8 * DEV, E), F32), ((8 * DEV, T), BF)],
        40, 2_500_000_000, 6_000_000,
        in_specs=[VM] * 7 + [SM], out_specs=(VM,) * 6,
        scratch_shapes=[
            pltpu.VMEM((INNER, T), F32), pltpu.VMEM((INNER, T), BF),
            pltpu.VMEM((INNER, N), BF), pltpu.VMEM((T, T), BF),
        ],
    )(proj, dy, cum, cumt, saved_state[0, 0], d_out, event_index, skip)
    (carries,) = call(
        scan_kernel, [((CTX, HP, N), BF)], 8, 4_000_000, 600_000, in_specs=[VM], out_specs=(VM,)
    )(got)
    carry = lax.all_to_all(carries, "ctx", 0, 0, tiled=True)
    go_got = lax.all_to_all(gout.reshape(DEV, 8, D), every, 0, 0, tiled=True)
    (pay,) = call(
        finish_kernel, [((8 * DEV, 2 * E), BF)], 32, 1_400_000_000, 6_000_000,
        in_specs=[VM] * 11, out_specs=(VM,),
        scratch_shapes=[pltpu.VMEM((PROJ, T), BF), pltpu.VMEM((INNER, T), BF)],
    )(carry.reshape(INNER, N), proj, cum, dx, dbt, dct, misc, hits, rows, w_in, w_up)
    pay_got = lax.all_to_all(pay.reshape(DEV, 8, 2 * E), every, 0, 0, tiled=True)
    chunk, skip_sum = call(
        sum_kernel, [((DEV, 8, 4 * E), BF), ((1, 128), F32)], 24, 2_000_000, 4_000_000,
        in_specs=[VM] * 2, out_specs=(VM,) * 2,
    )(pay_got, go_got)
    whole = lax.all_to_all(chunk, every, 0, 0, tiled=True)
    (table,) = call(
        table_kernel, [((ROWS_DEV, E), F32)], 24, 400_000_000, 2_000_000, in_specs=[VM], out_specs=(VM,)
    )(pay_got)
    grad_up, grad_in, grad_out = call(
        last_kernel, [((E, D), F32), ((D, PROJ), F32), ((INNER, D), F32)], 40, 700_000_000, 9_000_000,
        in_specs=[VM] * 3, out_specs=(VM,) * 3,
    )(whole, w_up, w_in)
    grad_skip = skip_sum[0, :H] + skip_sum[0, 32 : 32 + H]
    return (grad_up, grad_in, grad_out, grad_skip, table)


def solution(mesh):
    in_specs = (
        P("batch", "ctx", None),
        P("batch", "ctx"),
        P("batch", None, "ctx"),
        P("batch", "ctx", None, None, None),
        P("batch", "ctx", None),
        P(),
        P(),
        P(),
        P(),
    )
    out_specs = (P(), P(), P(), P(), P(("batch", "ctx"), None))
    return jax.shard_map(local, mesh=mesh, in_specs=in_specs, out_specs=out_specs, check_vma=False)
```

```python
from functools import partial

import jax
import jax.numpy as jnp
from jax import lax
from jax.experimental import pallas as pl
from jax.experimental.pallas import tpu as pltpu
from jax.sharding import PartitionSpec as P

T = 256
E = 256
D = 512
H = 16
HP = 64
N = 128
INNER = H * HP
PROJ = INNER + 2 * N
ROWS_DEV = 512
CAP = 4
DEV = 128
CTX = 16
SROWS = 80

DT = 0.0625
SC = 128.0**-0.5
F32 = jnp.float32
BF = jnp.bfloat16
NN = (((1,), (0,)), ((), ()))
NT = (((1,), (1,)), ((), ()))
TN = (((0,), (0,)), ((), ()))
MB = 1 << 20
BIG = 60


def dot(a, b, dims=NN):
    return lax.dot_general(a, b, dims, preferred_element_type=F32)


def split3(v):
    hi = v.astype(BF)
    rest = v - hi.astype(F32)
    mid = rest.astype(BF)
    return hi, mid, (rest - mid.astype(F32)).astype(BF)


def call(kernel, outs, vmem, flops, nbytes, **kw):
    return pl.pallas_call(
        kernel,
        out_shape=tuple(jax.ShapeDtypeStruct(s, d) for s, d in outs),
        compiler_params=pltpu.CompilerParams(vmem_limit_bytes=vmem * MB),
        cost_estimate=pl.CostEstimate(flops=flops, bytes_accessed=nbytes, transcendentals=0),
        **kw,
    )


VM = pl.BlockSpec(memory_space=pltpu.VMEM)
HBM = pl.BlockSpec(memory_space=pltpu.HBM)
SM = pl.BlockSpec(memory_space=pltpu.SMEM)


def project_kernel(rows_hbm, dout_hbm, decay_hbm, w_up_hbm, w_in_hbm, w_out_hbm,
                   proj_ref, dy_ref, cum_ref, cumt_ref, send_ref,
                   rows_ref, dout_ref, decay_ref, w_up_ref, w_in_ref, w_out_ref, sems):
    pairs = (
        (rows_hbm, rows_ref), (w_up_hbm, w_up_ref), (w_in_hbm, w_in_ref),
        (dout_hbm, dout_ref), (w_out_hbm, w_out_ref), (decay_hbm, decay_ref),
    )
    copies = [pltpu.make_async_copy(a, b, sems.at[i]) for i, (a, b) in enumerate(pairs)]
    for copy in copies:
        copy.start()
    copies[0].wait()
    copies[1].wait()
    u = dot(rows_ref[...], w_up_ref[...]).astype(BF)
    copies[2].wait()
    proj_ref[...] = dot(u, w_in_ref[...]).astype(BF)
    copies[3].wait()
    copies[4].wait()
    dy_ref[...] = dot(w_out_ref[...], dout_ref[...], NT).astype(BF)
    copies[5].wait()
    logs = split3(jnp.log(decay_ref[...]))
    r = lax.broadcasted_iota(jnp.int32, (T, T), 0)
    c = lax.broadcasted_iota(jnp.int32, (T, T), 1)
    upper = (r <= c).astype(F32).astype(BF)
    lower = (c <= r).astype(F32).astype(BF)
    cum = sum(dot(p, upper) for p in logs)
    cum_ref[...] = cum
    cumt_ref[...] = sum(dot(lower, p, NT) for p in logs)
    start = jnp.exp(cum)
    c_nat = proj_ref[:, INNER + N :]
    scaled = jnp.concatenate(
        [
            (dy_ref[h * HP : (h + 1) * HP, :].astype(F32) * (SC * start[h : h + 1, :])).astype(BF)
            for h in range(H)
        ],
        axis=0,
    )
    sums = dot(scaled, c_nat).astype(BF)
    amount = jnp.exp(cum[:, T - 1 : T])
    parts = [jnp.broadcast_to(p.astype(F32), (H, N)) for p in split3(amount)]
    row = lax.broadcasted_iota(jnp.int32, (SROWS - HP, N), 0)
    for h in range(H):
        send_ref[h, 0:HP, :] = sums[h * HP : (h + 1) * HP, :]
        tail = jnp.where(
            row == 0,
            parts[0][h : h + 1, :],
            jnp.where(row == 1, parts[1][h : h + 1, :], jnp.where(row == 2, parts[2][h : h + 1, :], 0.0)),
        )
        send_ref[h, HP:SROWS, :] = tail.astype(BF)


def scan_kernel(got_ref, out_ref):
    carry = jnp.zeros((HP, N), F32)
    for j in range(CTX - 1, -1, -1):
        out_ref[j, :, :] = carry.astype(BF)
        if j:
            tail = got_ref[j, HP:SROWS, :].astype(F32)
            amount = tail[0:1, :] + tail[1:2, :] + tail[2:3, :]
            carry = got_ref[j, 0:HP, :].astype(F32) + amount * carry


def local_kernel(proj_ref, dy_ref, cum_ref, cumt_ref, h0_ref, dout_ref, index_ref, skip_ref,
                 gout_ref, dx_ref, dbt_ref, dct_ref, misc_ref, hits_ref, y_ref, sdy_ref, h0t_ref, sum_ref):
    proj_t = jnp.transpose(proj_ref[...])
    bt = proj_t[INNER : INNER + N, :]
    ct = proj_t[INNER + N :, :]
    b_nat = proj_ref[:, INNER : INNER + N]
    c_nat = proj_ref[:, INNER + N :]
    pair = (SC * DT) * dot(b_nat, c_nat, NT)
    r = lax.broadcasted_iota(jnp.int32, (N, N), 0)
    c = lax.broadcasted_iota(jnp.int32, (N, N), 1)
    causal = r <= c
    cum = cum_ref[...]
    cumt = cumt_ref[...]
    start = jnp.exp(cum)
    h0t_ref[...] = h0_ref[...].astype(BF)
    y_ref[...] = dot(h0t_ref[...], ct)
    skip_sums = []
    a00 = jnp.zeros((N, N), F32)
    a01 = jnp.zeros((N, N), F32)
    a11 = jnp.zeros((N, N), F32)
    zero = jnp.zeros((N, N), BF)
    zrow = jnp.zeros((HP, T), BF)
    for h in range(H):
        lo, hi = h * HP, (h + 1) * HP
        row0, row1 = cum[h : h + 1, :N], cum[h : h + 1, N:]
        col0, col1 = cumt[:N, h : h + 1], cumt[N:, h : h + 1]
        m00 = jnp.exp(jnp.where(causal, row0 - col0, -1e30))
        m01 = jnp.exp(row1 - col0)
        m11 = jnp.exp(jnp.where(causal, row1 - col1, -1e30))
        weights = jnp.concatenate(
            [
                jnp.concatenate([(m00 * pair[:N, :N]).astype(BF), (m01 * pair[:N, N:]).astype(BF)], axis=1),
                jnp.concatenate([zero, (m11 * pair[N:, N:]).astype(BF)], axis=1),
            ],
            axis=0,
        )
        x_h = proj_t[lo:hi, :]
        dy_h = dy_ref[lo:hi, :]
        x_f, dy_f = x_h.astype(F32), dy_h.astype(F32)
        st = start[h : h + 1, :]
        skip = skip_ref[h]
        y_ref[lo:hi, :] = dot(x_h, weights) + SC * st * y_ref[lo:hi, :] + skip * x_f
        dx_ref[lo:hi, :] = dot(dy_h, weights, NT) + skip * dy_f
        sdy_ref[lo:hi, :] = (st * dy_f).astype(BF)
        x_pair = proj_ref[:, (h // 2) * N : (h // 2 + 1) * N]
        dy_z = jnp.concatenate([dy_h, zrow] if h % 2 == 0 else [zrow, dy_h], axis=0)
        q0 = dot(x_pair[:N, :], dy_z)
        q11 = dot(x_pair[N:, :], dy_z[:, N:])
        a00 += m00 * q0[:, :N]
        a01 += m01 * q0[:, N:]
        a11 += m11 * q11
        skip_sums.append(jnp.sum(x_f * dy_f, keepdims=True))
    gout_ref[...] = dot(y_ref[...].astype(BF), dout_ref[...]).astype(BF)
    sum_ref[:N, :N] = a00.astype(BF)
    sum_ref[:N, N:] = a01.astype(BF)
    sum_ref[N:, :N] = zero
    sum_ref[N:, N:] = a11.astype(BF)
    a = sum_ref[...]
    dct_ref[...] = (SC * (DT * dot(bt, a) + dot(h0t_ref[...], sdy_ref[...], TN))).astype(BF)
    dbt_ref[...] = (DT * SC) * dot(ct, a, NT)
    index = index_ref[...]
    owner_row = lax.shift_right_logical(index, 9)
    rr = lax.broadcasted_iota(jnp.int32, (T, T), 0)
    cc = lax.broadcasted_iota(jnp.int32, (T, T), 1)
    index_col = jnp.sum(jnp.where(rr == cc, index.astype(F32), 0.0), axis=1, keepdims=True)
    index_col = index_col.astype(jnp.int32)
    owner_col = lax.shift_right_logical(index_col, 9)
    same = owner_col == owner_row
    rank_row = jnp.sum(jnp.where(same & (rr < cc), 1.0, 0.0), axis=0, keepdims=True).astype(jnp.int32)
    rank_col = jnp.sum(jnp.where(same & (cc < rr), 1.0, 0.0), axis=1, keepdims=True).astype(jnp.int32)
    local_col = index_col - owner_col * ROWS_DEV
    id_hi = lax.shift_right_logical(local_col, 1)
    id_lo = local_col - 2 * id_hi
    v = jnp.where(cc == rank_col, id_hi, jnp.where(cc == rank_col + 64, id_lo, 0))
    row_id = lax.broadcasted_iota(jnp.int32, (8 * DEV, T), 0)
    hits_ref[...] = jnp.where(row_id == owner_row * 8 + 2 + rank_row, 1.0, 0.0).astype(BF)
    heads = jnp.where(row_id == owner_row * 8 + 6, 1.0, 0.0).astype(BF)
    lane = lax.broadcasted_iota(jnp.int32, (1, T), 1)
    extra = jnp.zeros((1, T), F32)
    for h in range(H):
        whole = skip_sums[h]
        top = whole.astype(BF).astype(F32)
        extra = extra + jnp.where(lane == 128 + h, top, 0.0) + jnp.where(lane == 160 + h, whole - top, 0.0)
    misc = dot(heads, v.astype(F32).astype(BF))
    misc_ref[...] = misc + jnp.where((row_id & 7) == 6, extra, 0.0)


def finish_kernel(carry_ref, proj_ref, cum_ref, dx_ref, dbt_ref, dct_ref, misc_ref, hits_ref, gout_ref, rows_ref,
                  w_in_ref, w_up_ref, out_ref, d_ref, tx_ref):
    proj_t = jnp.transpose(proj_ref[...])
    bt = proj_t[INNER : INNER + N, :]
    cum = cum_ref[...]
    tail = DT * jnp.exp(cum[:, T - 1 : T] - cum)
    carry = carry_ref[...]
    entering = dot(carry, bt)
    for h in range(H):
        lo, hi = h * HP, (h + 1) * HP
        tl = tail[h : h + 1, :]
        d_ref[lo:hi, :] = (dx_ref[lo:hi, :] + tl * entering[lo:hi, :]).astype(BF)
        tx_ref[lo:hi, :] = (tl * proj_t[lo:hi, :].astype(F32)).astype(BF)
    d_ref[INNER : INNER + N, :] = (dbt_ref[...] + dot(carry, tx_ref[...], TN)).astype(BF)
    d_ref[INNER + N :, :] = dct_ref[...]
    d = d_ref[...]
    g = dot(d, rows_ref[...]).astype(BF)
    out_ref[:, :E] = g[:INNER, :]
    du = dot(w_in_ref[...], d).astype(BF)
    de = dot(w_up_ref[...], du).astype(BF)
    r = lax.broadcasted_iota(jnp.int32, (8 * DEV, 2 * N), 0)
    j = lax.broadcasted_iota(jnp.int32, (1, 2 * N), 1)
    place = jnp.where(r == 8 * lax.shift_right_logical(j, 1) + (j & 1), 1.0, 0.0).astype(BF)
    misc = misc_ref[...] + dot(hits_ref[...], de, NT) + dot(place, g[INNER:, :])
    out_ref[:, E : 2 * E] = misc.astype(BF)
    out_ref[:, 2 * E :] = gout_ref[...]


def sum_kernel(got_ref, chunk_ref, skip_ref):
    total = jnp.sum(got_ref[...].astype(F32), axis=0)
    chunk_ref[...] = jnp.broadcast_to(total[None], chunk_ref.shape).astype(BF)
    skip_ref[...] = total[6:7, E + 128 : E + 256]


def table_kernel(got_ref, table_ref):
    misc = got_ref[:, :, E : 2 * E]
    ids = misc[:, 6:7, 0:128].astype(F32)
    sub = lax.broadcasted_iota(jnp.int32, (DEV, 8, 128), 1) - 2
    lane = lax.broadcasted_iota(jnp.int32, (DEV, 8, 128), 2)
    want = jnp.where(lane == sub, 2.0, jnp.where(lane == sub + 64, 1.0, 0.0))
    row = jnp.sum(ids * want, axis=2, keepdims=True)
    row = jnp.where((sub[:, :, :1] >= 0) & (sub[:, :, :1] < CAP), row, -1.0)
    rid = lax.broadcasted_iota(jnp.int32, (DEV, 8, ROWS_DEV), 2).astype(F32)
    hits = jnp.where(rid == row, 1.0, 0.0).reshape(DEV * 8, ROWS_DEV).astype(BF)
    table_ref[...] = dot(hits, misc.reshape(DEV * 8, E), TN)


def last_kernel(got_ref, w_up_ref, w_in_ref, up_ref, in_ref, out_ref):
    got = got_ref[...].reshape(DEV * 8, 4 * E)
    out_ref[...] = got[:, 2 * E :].astype(F32)
    j = lax.broadcasted_iota(jnp.int32, (2 * N, 8 * DEV), 0)
    r = lax.broadcasted_iota(jnp.int32, (2 * N, 8 * DEV), 1)
    pick = jnp.where(r == 8 * lax.shift_right_logical(j, 1) + (j & 1), 1.0, 0.0).astype(BF)
    g = jnp.concatenate([got[:, :E], dot(pick, got[:, E : 2 * E]).astype(BF)], axis=0)
    in_ref[...] = lax.dot_general(w_up_ref[...], g, (((0,), (1,)), ((), ())), preferred_element_type=F32)
    up_ref[...] = jnp.transpose(dot(w_in_ref[...], g))


def local(event_rows, event_index, decay, saved_state, dout, w_up, w_in, w_out, skip):
    every = ("batch", "ctx")
    rows, d_out = event_rows[0], dout[0]
    proj, dy, cum, cumt, send = call(
        project_kernel,
        [((T, PROJ), BF), ((INNER, T), BF), ((H, T), F32), ((T, H), F32), ((H, SROWS, N), BF)],
        BIG, 750_000_000, 4_500_000,
        in_specs=[HBM] * 6, out_specs=(VM,) * 5,
        scratch_shapes=[
            pltpu.VMEM((T, E), BF), pltpu.VMEM((T, D), BF), pltpu.VMEM((H, T), F32),
            pltpu.VMEM((E, D), BF), pltpu.VMEM((D, PROJ), BF), pltpu.VMEM((INNER, D), BF),
            pltpu.SemaphoreType.DMA((6,)),
        ],
    )(rows, d_out, decay[0], w_up, w_in, w_out)
    got = lax.all_to_all(send, "ctx", 0, 0, tiled=True)
    gout, dx, dbt, dct, misc, hits = call(
        local_kernel,
        [((INNER, D), BF), ((INNER, T), F32), ((N, T), F32), ((N, T), BF), ((8 * DEV, E), F32), ((8 * DEV, T), BF)],
        BIG, 2_500_000_000, 6_000_000,
        in_specs=[VM] * 7 + [SM], out_specs=(VM,) * 6,
        scratch_shapes=[
            pltpu.VMEM((INNER, T), F32), pltpu.VMEM((INNER, T), BF),
            pltpu.VMEM((INNER, N), BF), pltpu.VMEM((T, T), BF),
        ],
    )(proj, dy, cum, cumt, jnp.swapaxes(saved_state[0, 0], 1, 2).reshape(INNER, N), d_out, event_index, skip)
    got, dct = lax.optimization_barrier((got, dct))
    (carries,) = call(
        scan_kernel, [((CTX, HP, N), BF)], 8, 4_000_000, 600_000, in_specs=[VM], out_specs=(VM,)
    )(got)
    carry = lax.all_to_all(carries, "ctx", 0, 0, tiled=True)
    (pay,) = call(
        finish_kernel, [((8 * DEV, 4 * E), BF)], BIG, 1_400_000_000, 6_000_000,
        in_specs=[VM] * 12, out_specs=(VM,),
        scratch_shapes=[pltpu.VMEM((PROJ, T), BF), pltpu.VMEM((INNER, T), BF)],
    )(carry.reshape(INNER, N), proj, cum, dx, dbt, dct, misc, hits, gout, rows, w_in, w_up)
    pay_got = lax.all_to_all(pay.reshape(DEV, 8, 4 * E), every, 0, 0, tiled=True)
    chunk, skip_sum = call(
        sum_kernel, [((DEV, 8, 4 * E), BF), ((1, 128), F32)], 12, 2_000_000, 4_000_000,
        in_specs=[VM], out_specs=(VM,) * 2,
    )(pay_got)
    whole = lax.all_to_all(chunk, every, 0, 0, tiled=True)
    (table,) = call(
        table_kernel, [((ROWS_DEV, E), F32)], 12, 400_000_000, 2_000_000, in_specs=[VM], out_specs=(VM,)
    )(pay_got)
    grad_up, grad_in, grad_out = call(
        last_kernel, [((E, D), F32), ((D, PROJ), F32), ((INNER, D), F32)], 20, 700_000_000, 9_000_000,
        in_specs=[VM] * 3, out_specs=(VM,) * 3,
    )(whole, w_up, w_in)
    grad_skip = skip_sum[0, :H] + skip_sum[0, 32 : 32 + H]
    return (grad_up, grad_in, grad_out, grad_skip, table)


def solution(mesh):
    in_specs = (
        P("batch", "ctx", None),
        P("batch", "ctx"),
        P("batch", None, "ctx"),
        P("batch", "ctx", None, None, None),
        P("batch", "ctx", None),
        P(),
        P(),
        P(),
        P(),
    )
    out_specs = (P(), P(), P(), P(), P(("batch", "ctx"), None))
    return jax.shard_map(local, mesh=mesh, in_specs=in_specs, out_specs=out_specs, check_vma=False)
```

```python
from functools import partial

import jax
import jax.numpy as jnp
from jax import lax
from jax.experimental import pallas as pl
from jax.experimental.pallas import tpu as pltpu
from jax.sharding import PartitionSpec as P

T = 256
E = 256
D = 512
H = 16
HP = 64
N = 128
INNER = H * HP
PROJ = INNER + 2 * N
ROWS_DEV = 512
CAP = 4
DEV = 128
CTX = 16
SROWS = 80

DT = 0.0625
SC = 128.0**-0.5
F32 = jnp.float32
BF = jnp.bfloat16
NN = (((1,), (0,)), ((), ()))
NT = (((1,), (1,)), ((), ()))
TN = (((0,), (0,)), ((), ()))
MB = 1 << 20
BIG = 60


def dot(a, b, dims=NN):
    return lax.dot_general(a, b, dims, preferred_element_type=F32)


def split3(v):
    hi = v.astype(BF)
    rest = v - hi.astype(F32)
    mid = rest.astype(BF)
    return hi, mid, (rest - mid.astype(F32)).astype(BF)


def call(kernel, outs, vmem, flops, nbytes, **kw):
    return pl.pallas_call(
        kernel,
        out_shape=tuple(jax.ShapeDtypeStruct(s, d) for s, d in outs),
        compiler_params=pltpu.CompilerParams(vmem_limit_bytes=vmem * MB),
        cost_estimate=pl.CostEstimate(flops=flops, bytes_accessed=nbytes, transcendentals=0),
        **kw,
    )


VM = pl.BlockSpec(memory_space=pltpu.VMEM)
HBM = pl.BlockSpec(memory_space=pltpu.HBM)
SM = pl.BlockSpec(memory_space=pltpu.SMEM)


def project_kernel(rows_hbm, dout_hbm, decay_hbm, w_up_hbm, w_in_hbm, w_out_hbm,
                   proj_ref, dy_ref, cum_ref, cumt_ref, send_ref,
                   rows_ref, dout_ref, decay_ref, w_up_ref, w_in_ref, w_out_ref, sems):
    pairs = (
        (rows_hbm, rows_ref), (w_up_hbm, w_up_ref), (w_in_hbm, w_in_ref),
        (dout_hbm, dout_ref), (w_out_hbm, w_out_ref), (decay_hbm, decay_ref),
    )
    copies = [pltpu.make_async_copy(a, b, sems.at[i]) for i, (a, b) in enumerate(pairs)]
    for copy in copies:
        copy.start()
    copies[0].wait()
    copies[1].wait()
    u = dot(rows_ref[...], w_up_ref[...]).astype(BF)
    copies[2].wait()
    proj_ref[...] = dot(u, w_in_ref[...]).astype(BF)
    copies[3].wait()
    copies[4].wait()
    dy_ref[...] = dot(w_out_ref[...], dout_ref[...], NT).astype(BF)
    copies[5].wait()
    logs = split3(jnp.log(decay_ref[...]))
    r = lax.broadcasted_iota(jnp.int32, (T, T), 0)
    c = lax.broadcasted_iota(jnp.int32, (T, T), 1)
    upper = (r <= c).astype(F32).astype(BF)
    lower = (c <= r).astype(F32).astype(BF)
    cum = sum(dot(p, upper) for p in logs)
    cum_ref[...] = cum
    cumt_ref[...] = sum(dot(lower, p, NT) for p in logs)
    start = jnp.exp(cum)
    c_nat = proj_ref[:, INNER + N :]
    scaled = jnp.concatenate(
        [
            (dy_ref[h * HP : (h + 1) * HP, :].astype(F32) * (SC * start[h : h + 1, :])).astype(BF)
            for h in range(H)
        ],
        axis=0,
    )
    sums = dot(scaled, c_nat).astype(BF)
    amount = jnp.exp(cum[:, T - 1 : T])
    parts = [jnp.broadcast_to(p.astype(F32), (H, N)) for p in split3(amount)]
    row = lax.broadcasted_iota(jnp.int32, (SROWS - HP, N), 0)
    for h in range(H):
        send_ref[h, 0:HP, :] = sums[h * HP : (h + 1) * HP, :]
        tail = jnp.where(
            row == 0,
            parts[0][h : h + 1, :],
            jnp.where(row == 1, parts[1][h : h + 1, :], jnp.where(row == 2, parts[2][h : h + 1, :], 0.0)),
        )
        send_ref[h, HP:SROWS, :] = tail.astype(BF)


def scan_kernel(got_ref, out_ref):
    carry = jnp.zeros((HP, N), F32)
    for j in range(CTX - 1, -1, -1):
        out_ref[j, :, :] = carry.astype(BF)
        if j:
            tail = got_ref[j, HP:SROWS, :].astype(F32)
            amount = tail[0:1, :] + tail[1:2, :] + tail[2:3, :]
            carry = got_ref[j, 0:HP, :].astype(F32) + amount * carry


def local_kernel(proj_ref, dy_ref, cum_ref, cumt_ref, h0_ref, dout_ref, index_ref, skip_ref, pos_ref,
                 keep_ref, give_ref, dx_ref, dbt_ref, dct_ref, misc_ref, hits_ref, y_ref, sdy_ref, h0t_ref, sum_ref):
    proj_t = jnp.transpose(proj_ref[...])
    bt = proj_t[INNER : INNER + N, :]
    ct = proj_t[INNER + N :, :]
    b_nat = proj_ref[:, INNER : INNER + N]
    c_nat = proj_ref[:, INNER + N :]
    pair = (SC * DT) * dot(b_nat, c_nat, NT)
    r = lax.broadcasted_iota(jnp.int32, (N, N), 0)
    c = lax.broadcasted_iota(jnp.int32, (N, N), 1)
    causal = r <= c
    cum = cum_ref[...]
    cumt = cumt_ref[...]
    start = jnp.exp(cum)
    h0t_ref[...] = h0_ref[...].astype(BF)
    y_ref[...] = dot(h0t_ref[...], ct)
    skip_sums = []
    a00 = jnp.zeros((N, N), F32)
    a01 = jnp.zeros((N, N), F32)
    a11 = jnp.zeros((N, N), F32)
    zero = jnp.zeros((N, N), BF)
    zrow = jnp.zeros((HP, T), BF)
    for h in range(H):
        lo, hi = h * HP, (h + 1) * HP
        row0, row1 = cum[h : h + 1, :N], cum[h : h + 1, N:]
        col0, col1 = cumt[:N, h : h + 1], cumt[N:, h : h + 1]
        m00 = jnp.exp(jnp.where(causal, row0 - col0, -1e30))
        m01 = jnp.exp(row1 - col0)
        m11 = jnp.exp(jnp.where(causal, row1 - col1, -1e30))
        weights = jnp.concatenate(
            [
                jnp.concatenate([(m00 * pair[:N, :N]).astype(BF), (m01 * pair[:N, N:]).astype(BF)], axis=1),
                jnp.concatenate([zero, (m11 * pair[N:, N:]).astype(BF)], axis=1),
            ],
            axis=0,
        )
        x_h = proj_t[lo:hi, :]
        dy_h = dy_ref[lo:hi, :]
        x_f, dy_f = x_h.astype(F32), dy_h.astype(F32)
        st = start[h : h + 1, :]
        skip = skip_ref[h]
        y_ref[lo:hi, :] = dot(x_h, weights) + SC * st * y_ref[lo:hi, :] + skip * x_f
        dx_ref[lo:hi, :] = dot(dy_h, weights, NT) + skip * dy_f
        sdy_ref[lo:hi, :] = (st * dy_f).astype(BF)
        x_pair = proj_ref[:, (h // 2) * N : (h // 2 + 1) * N]
        dy_z = jnp.concatenate([dy_h, zrow] if h % 2 == 0 else [zrow, dy_h], axis=0)
        q0 = dot(x_pair[:N, :], dy_z)
        q11 = dot(x_pair[N:, :], dy_z[:, N:])
        a00 += m00 * q0[:, :N]
        a01 += m01 * q0[:, N:]
        a11 += m11 * q11
        skip_sums.append(jnp.sum(x_f * dy_f, keepdims=True))
    core = pos_ref[1]
    half = INNER // 2
    mine = pl.ds(pl.multiple_of(core * half, half), half)
    other = pl.ds(pl.multiple_of((1 - core) * half, half), half)
    give_ref[...] = dot(y_ref[other, :].astype(BF), dout_ref[...]).astype(BF)
    keep_ref[...] = dot(y_ref[mine, :].astype(BF), dout_ref[...])
    sum_ref[:N, :N] = a00.astype(BF)
    sum_ref[:N, N:] = a01.astype(BF)
    sum_ref[N:, :N] = zero
    sum_ref[N:, N:] = a11.astype(BF)
    a = sum_ref[...]
    dct_ref[...] = (SC * (DT * dot(bt, a) + dot(h0t_ref[...], sdy_ref[...], TN))).astype(BF)
    dbt_ref[...] = (DT * SC) * dot(ct, a, NT)
    index = index_ref[...]
    owner_row = lax.shift_right_logical(index, 9)
    rr = lax.broadcasted_iota(jnp.int32, (T, T), 0)
    cc = lax.broadcasted_iota(jnp.int32, (T, T), 1)
    index_col = jnp.sum(jnp.where(rr == cc, index.astype(F32), 0.0), axis=1, keepdims=True)
    index_col = index_col.astype(jnp.int32)
    owner_col = lax.shift_right_logical(index_col, 9)
    same = owner_col == owner_row
    rank_row = jnp.sum(jnp.where(same & (rr < cc), 1.0, 0.0), axis=0, keepdims=True).astype(jnp.int32)
    rank_col = jnp.sum(jnp.where(same & (cc < rr), 1.0, 0.0), axis=1, keepdims=True).astype(jnp.int32)
    local_col = index_col - owner_col * ROWS_DEV
    id_hi = lax.shift_right_logical(local_col, 1)
    id_lo = local_col - 2 * id_hi
    v = jnp.where(cc == rank_col, id_hi, jnp.where(cc == rank_col + 64, id_lo, 0))
    row_id = lax.broadcasted_iota(jnp.int32, (8 * DEV, T), 0)
    hits_ref[...] = jnp.where(row_id == owner_row * 8 + 2 + rank_row, 1.0, 0.0).astype(BF)
    heads = jnp.where(row_id == owner_row * 8 + 6, 1.0, 0.0).astype(BF)
    lane = lax.broadcasted_iota(jnp.int32, (1, T), 1)
    extra = jnp.zeros((1, T), F32)
    for h in range(H):
        whole = skip_sums[h]
        top = whole.astype(BF).astype(F32)
        extra = extra + jnp.where(lane == 128 + h, top, 0.0) + jnp.where(lane == 160 + h, whole - top, 0.0)
    misc = dot(heads, v.astype(F32).astype(BF))
    misc_ref[...] = (misc + jnp.where((row_id & 7) == 6, extra, 0.0)).astype(BF)


def finish_kernel(carry_hbm, proj_hbm, cum_hbm, dx_hbm, dbt_hbm, dct_hbm, misc_hbm, hits_hbm, rows_hbm,
                  w_in_hbm, w_up_hbm, out_hbm,
                  carry_ref, proj_ref, cum_ref, dx_ref, dbt_ref, d_ref, misc_ref, hits_ref, rows_ref,
                  w_in_ref, w_up_ref, tx_ref, left_ref, right_ref, sems):
    copies = [
        pltpu.make_async_copy(a, b, sems.at[n])
        for n, (a, b) in enumerate((
            (carry_hbm, carry_ref), (proj_hbm, proj_ref), (cum_hbm, cum_ref), (dx_hbm, dx_ref),
            (dbt_hbm, dbt_ref), (dct_hbm, d_ref.at[INNER + N :, :]), (rows_hbm, rows_ref),
            (w_in_hbm, w_in_ref), (w_up_hbm, w_up_ref), (hits_hbm, hits_ref), (misc_hbm, misc_ref),
        ))
    ]
    for copy in copies:
        copy.start()
    for copy in copies[:3]:
        copy.wait()
    proj_t = jnp.transpose(proj_ref[...])
    bt = proj_t[INNER : INNER + N, :]
    cum = cum_ref[...]
    tail = DT * jnp.exp(cum[:, T - 1 : T] - cum)
    carry = carry_ref[...]
    entering = dot(carry, bt)
    copies[3].wait()
    for h in range(H):
        lo, hi = h * HP, (h + 1) * HP
        tl = tail[h : h + 1, :]
        d_ref[lo:hi, :] = (dx_ref[lo:hi, :] + tl * entering[lo:hi, :]).astype(BF)
        tx_ref[lo:hi, :] = (tl * proj_t[lo:hi, :].astype(F32)).astype(BF)
    for copy in copies[4:7]:
        copy.wait()
    d_ref[INNER : INNER + N, :] = (dbt_ref[...] + dot(carry, tx_ref[...], TN)).astype(BF)
    d = d_ref[...]
    g = dot(d, rows_ref[...]).astype(BF)
    left_ref[...] = g[:INNER, :]
    out_left = pltpu.make_async_copy(left_ref, out_hbm.at[:, :E], sems.at[11])
    out_left.start()
    copies[7].wait()
    du = dot(w_in_ref[...], d).astype(BF)
    copies[8].wait()
    de = dot(w_up_ref[...], du).astype(BF)
    r = lax.broadcasted_iota(jnp.int32, (8 * DEV, 2 * N), 0)
    j = lax.broadcasted_iota(jnp.int32, (1, 2 * N), 1)
    place = jnp.where(r == 8 * lax.shift_right_logical(j, 1) + (j & 1), 1.0, 0.0).astype(BF)
    copies[9].wait()
    copies[10].wait()
    misc = misc_ref[...].astype(F32) + dot(hits_ref[...], de, NT) + dot(place, g[INNER:, :])
    right_ref[...] = misc.astype(BF)
    out_right = pltpu.make_async_copy(right_ref, out_hbm.at[:, E:], sems.at[12])
    out_right.start()
    out_left.wait()
    out_right.wait()


def split_kernel(which, pos_ref, own_ref, *refs):
    got, (keep_ref, *give_refs, acc_ref) = refs[:-5], refs[-5:]
    total = own_ref[...]
    for ref in got:
        total = total + ref[...].astype(F32)
    acc_ref[...] = total
    at = pos_ref[which]
    part = keep_ref.shape[0]
    keep_ref[...] = acc_ref[pl.ds(pl.multiple_of(at * part, part), part), :]
    for k in range(1, 4):
        start = pl.multiple_of(((at + k) & 3) * part, part)
        give_refs[k - 1][...] = acc_ref[pl.ds(start, part), :].astype(BF)


def total_kernel(own_ref, a_ref, b_ref, c_ref, out_ref):
    total = own_ref[...] + a_ref[...].astype(F32) + b_ref[...].astype(F32) + c_ref[...].astype(F32)
    out_ref[...] = total.astype(BF)


def join_kernel(which, pos_ref, own_ref, a_ref, b_ref, c_ref, out_ref):
    at = pos_ref[which]
    out_ref[at] = own_ref[...]
    for k, ref in enumerate((a_ref, b_ref, c_ref)):
        out_ref[(at + 3 - k) & 3] = ref[...]


def write_kernel(pos_ref, own_ref, other_ref, out_ref):
    core = pos_ref[1]
    out_ref[core] = own_ref[...].astype(F32)
    out_ref[1 - core] = other_ref[...].astype(F32)


def sum_kernel(got_ref, chunk_ref, skip_ref):
    total = jnp.sum(got_ref[...].astype(F32), axis=0)
    side = jnp.concatenate([total[0:2, E : E + N], total[0:2, E + N :], jnp.zeros((4, N), F32)], axis=0)
    chunk = jnp.concatenate([total[:, :E], side], axis=1)
    chunk_ref[...] = jnp.broadcast_to(chunk[None], chunk_ref.shape).astype(BF)
    skip_ref[...] = total[6:7, E + 128 : E + 256]


def table_kernel(got_ref, table_ref):
    misc = got_ref[:, :, E : 2 * E]
    ids = misc[:, 6:7, 0:128].astype(F32)
    sub = lax.broadcasted_iota(jnp.int32, (DEV, 8, 128), 1) - 2
    lane = lax.broadcasted_iota(jnp.int32, (DEV, 8, 128), 2)
    want = jnp.where(lane == sub, 2.0, jnp.where(lane == sub + 64, 1.0, 0.0))
    row = jnp.sum(ids * want, axis=2, keepdims=True)
    row = jnp.where((sub[:, :, :1] >= 0) & (sub[:, :, :1] < CAP), row, -1.0)
    rid = lax.broadcasted_iota(jnp.int32, (DEV, 8, ROWS_DEV), 2).astype(F32)
    hits = jnp.where(rid == row, 1.0, 0.0).reshape(DEV * 8, ROWS_DEV).astype(BF)
    table_ref[...] = dot(hits, misc.reshape(DEV * 8, E), TN)


def last_kernel(got_ref, w_up_ref, w_in_ref, up_ref, in_ref, g_ref):
    @pl.when(pl.program_id(0) == 0)
    def _():
        g_ref[:INNER, :] = got_ref[:, :E]
        j = lax.broadcasted_iota(jnp.int32, (2 * N, 8 * DEV), 0)
        r = lax.broadcasted_iota(jnp.int32, (2 * N, 8 * DEV), 1)
        first = r - (8 * lax.shift_right_logical(j, 1) + (j & 1))
        for m in range(2):
            pick = jnp.where(first == 2 * m, 1.0, 0.0).astype(BF)
            g_ref[INNER:, m * N : (m + 1) * N] = dot(pick, got_ref[:, E:]).astype(BF)

    g = g_ref[...]
    in_ref[...] = lax.dot_general(w_up_ref[...], g, (((0,), (1,)), ((), ())), preferred_element_type=F32)
    up_ref[...] = jnp.transpose(dot(w_in_ref[...], g))


def hop(step, axis):
    if axis == "x":
        return [(i, (i + 2 * step) % 8) for i in range(8)]
    if axis == "core":
        return [(i, i ^ 1) for i in range(8)]
    if axis == "y":
        return [(i, (i + 4 * step) % 16) for i in range(16)]
    return [(i, i // 4 * 4 + (i + step) % 4) for i in range(16)]


def send(value, axis, step):
    return lax.ppermute(value, "batch" if axis in ("x", "core") else "ctx", hop(step, axis))


def spread(pos, own, got, which, axis, rows):
    keep, *give = call(
        partial(split_kernel, which),
        [((rows // 4, D), F32)] + [((rows // 4, D), BF)] * 3,
        4, rows * D * 4, rows * D * 8,
        in_specs=[SM] + [VM] * (1 + len(got)), out_specs=(VM,) * 4,
        scratch_shapes=[pltpu.VMEM((rows, D), F32)],
    )(pos, own, *got)
    return keep, [send(v, axis, k + 1) for k, v in enumerate(give)]


def gather(pos, own, which, axis, rows):
    got = [send(own, axis, k) for k in range(1, 4)]
    (out,) = call(
        partial(join_kernel, which), [((4, rows, D), BF)], 4, 0, rows * D * 16,
        in_specs=[SM] + [VM] * 4, out_specs=(VM,),
    )(pos, own, *got)
    return out.reshape(4 * rows, D)


def local(event_rows, event_index, decay, saved_state, dout, w_up, w_in, w_out, skip):
    every = ("batch", "ctx")
    rows, d_out = event_rows[0], dout[0]
    proj, dy, cum, cumt, sums = call(
        project_kernel,
        [((T, PROJ), BF), ((INNER, T), BF), ((H, T), F32), ((T, H), F32), ((H, SROWS, N), BF)],
        BIG, 750_000_000, 4_500_000,
        in_specs=[HBM] * 6, out_specs=(VM,) * 5,
        scratch_shapes=[
            pltpu.VMEM((T, E), BF), pltpu.VMEM((T, D), BF), pltpu.VMEM((H, T), F32),
            pltpu.VMEM((E, D), BF), pltpu.VMEM((D, PROJ), BF), pltpu.VMEM((INNER, D), BF),
            pltpu.SemaphoreType.DMA((6,)),
        ],
    )(rows, d_out, decay[0], w_up, w_in, w_out)
    got = lax.all_to_all(sums, "ctx", 0, 0, tiled=True)
    place, lane = lax.axis_index("batch"), lax.axis_index("ctx")
    pos = jnp.stack([place >> 1, place & 1, lane >> 2, lane & 3])
    keep, give, dx, dbt, dct, misc, hits = call(
        local_kernel,
        [((INNER // 2, D), F32), ((INNER // 2, D), BF), ((INNER, T), F32), ((N, T), F32), ((N, T), BF),
         ((8 * DEV, E), BF), ((8 * DEV, T), BF)],
        BIG, 2_500_000_000, 6_000_000,
        in_specs=[VM] * 7 + [SM] * 2, out_specs=(VM,) * 7,
        scratch_shapes=[
            pltpu.VMEM((INNER, T), F32), pltpu.VMEM((INNER, T), BF),
            pltpu.VMEM((INNER, N), BF), pltpu.VMEM((T, T), BF),
        ],
    )(proj, dy, cum, cumt, jnp.swapaxes(saved_state[0, 0], 1, 2).reshape(INNER, N), d_out, event_index, skip, pos)
    got, give = lax.optimization_barrier((got, give))
    (carries,) = call(
        scan_kernel, [((CTX, HP, N), BF)], 8, 4_000_000, 600_000, in_specs=[VM], out_specs=(VM,)
    )(got)
    carry = lax.all_to_all(carries, "ctx", 0, 0, tiled=True)
    own, got_go = spread(pos, keep, [send(give, "core", 1)], 0, "x", 512)
    carry, got_go = lax.optimization_barrier((carry, got_go))
    own, got_go = spread(pos, own, got_go, 2, "y", 128)
    own, got_go = spread(pos, own, got_go, 3, "z", 32)
    (part,) = call(
        total_kernel, [((8, D), BF)], 4, 20_000, 60_000, in_specs=[VM] * 4, out_specs=(VM,)
    )(own, *got_go)
    part = gather(pos, part, 3, "z", 8)
    part = gather(pos, part, 2, "y", 32)
    (pay,) = call(
        finish_kernel, [((8 * DEV, 2 * E), BF)], BIG, 1_400_000_000, 6_000_000,
        in_specs=[HBM] * 11, out_specs=(HBM,),
        scratch_shapes=[
            pltpu.VMEM((INNER, N), BF), pltpu.VMEM((T, PROJ), BF), pltpu.VMEM((H, T), F32),
            pltpu.VMEM((INNER, T), F32), pltpu.VMEM((N, T), F32), pltpu.VMEM((PROJ, T), BF),
            pltpu.VMEM((8 * DEV, E), BF), pltpu.VMEM((8 * DEV, T), BF), pltpu.VMEM((T, E), BF),
            pltpu.VMEM((D, PROJ), BF), pltpu.VMEM((E, D), BF), pltpu.VMEM((INNER, T), BF),
            pltpu.VMEM((INNER, E), BF), pltpu.VMEM((8 * DEV, E), BF), pltpu.SemaphoreType.DMA((13,)),
        ],
    )(carry.reshape(INNER, N), proj, cum, dx, dbt, dct, misc, hits, rows, w_in, w_up)
    pay_got = lax.all_to_all(pay.reshape(DEV, 8, 2 * E), every, 0, 0, tiled=True)
    pay_got, part = lax.optimization_barrier((pay_got, part))
    chunk, skip_sum = call(
        sum_kernel, [((DEV, 8, 3 * N), BF), ((1, 128), F32)], 12, 2_000_000, 2_000_000,
        in_specs=[VM], out_specs=(VM,) * 2,
    )(pay_got)
    whole = lax.all_to_all(chunk, every, 0, 0, tiled=True)
    part = gather(pos, part, 0, "x", 128)
    (grad_out,) = call(
        write_kernel, [((2, INNER // 2, D), F32)], 8, 500_000, 3_000_000,
        in_specs=[SM, VM, VM], out_specs=(VM,),
    )(pos, part, send(part, "core", 1))
    (table,) = call(
        table_kernel, [((ROWS_DEV, E), F32)], 12, 400_000_000, 2_000_000, in_specs=[VM], out_specs=(VM,)
    )(pay_got)
    grad_up, grad_in = pl.pallas_call(
        last_kernel,
        grid=(4,),
        out_shape=(jax.ShapeDtypeStruct((E, D), F32), jax.ShapeDtypeStruct((D, PROJ), F32)),
        in_specs=[
            pl.BlockSpec((8 * DEV, 3 * N), lambda i: (0, 0)),
            pl.BlockSpec((E, D // 4), lambda i: (0, i)),
            pl.BlockSpec((D // 4, PROJ), lambda i: (i, 0)),
        ],
        out_specs=(
            pl.BlockSpec((E, D // 4), lambda i: (0, i)),
            pl.BlockSpec((D // 4, PROJ), lambda i: (i, 0)),
        ),
        scratch_shapes=[pltpu.VMEM((PROJ, E), BF)],
        compiler_params=pltpu.CompilerParams(vmem_limit_bytes=24 * MB),
        cost_estimate=pl.CostEstimate(flops=700_000_000, bytes_accessed=5_000_000, transcendentals=0),
    )(whole.reshape(DEV * 8, 3 * N), w_up, w_in)
    grad_skip = skip_sum[0, :H] + skip_sum[0, 32 : 32 + H]
    return (grad_up, grad_in, grad_out.reshape(INNER, D), grad_skip, table)


def solution(mesh):
    in_specs = (
        P("batch", "ctx", None),
        P("batch", "ctx"),
        P("batch", None, "ctx"),
        P("batch", "ctx", None, None, None),
        P("batch", "ctx", None),
        P(),
        P(),
        P(),
        P(),
    )
    out_specs = (P(), P(), P(), P(), P(("batch", "ctx"), None))
    return jax.shard_map(local, mesh=mesh, in_specs=in_specs, out_specs=out_specs, check_vma=False)
```

```python
from functools import partial

import jax
import jax.numpy as jnp
from jax import lax
from jax.experimental import pallas as pl
from jax.experimental.pallas import tpu as pltpu
from jax.sharding import Mesh, PartitionSpec as P

T = 256
E = 256
D = 512
H = 16
HP = 64
N = 128
INNER = H * HP
PROJ = INNER + 2 * N
ROWS_DEV = 512
CAP = 4
DEV = 128
CTX = 16
SROWS = 80

DT = 0.0625
SC = 128.0**-0.5
F32 = jnp.float32
BF = jnp.bfloat16
NN = (((1,), (0,)), ((), ()))
NT = (((1,), (1,)), ((), ()))
TN = (((0,), (0,)), ((), ()))
MB = 1 << 20
BIG = 60


def dot(a, b, dims=NN):
    return lax.dot_general(a, b, dims, preferred_element_type=F32)


def split3(v):
    hi = v.astype(BF)
    rest = v - hi.astype(F32)
    mid = rest.astype(BF)
    return hi, mid, (rest - mid.astype(F32)).astype(BF)


def call(kernel, outs, vmem, flops, nbytes, **kw):
    return pl.pallas_call(
        kernel,
        out_shape=tuple(jax.ShapeDtypeStruct(s, d) for s, d in outs),
        compiler_params=pltpu.CompilerParams(vmem_limit_bytes=vmem * MB),
        cost_estimate=pl.CostEstimate(flops=flops, bytes_accessed=nbytes, transcendentals=0),
        **kw,
    )


VM = pl.BlockSpec(memory_space=pltpu.VMEM)
HBM = pl.BlockSpec(memory_space=pltpu.HBM)
SM = pl.BlockSpec(memory_space=pltpu.SMEM)


def project_kernel(rows_hbm, dout_hbm, decay_hbm, w_up_hbm, w_in_hbm, w_out_hbm,
                   proj_ref, dy_ref, cum_ref, cumt_ref, send_ref,
                   rows_ref, dout_ref, decay_ref, w_up_ref, w_in_ref, w_out_ref, sems):
    pairs = (
        (rows_hbm, rows_ref), (w_up_hbm, w_up_ref), (w_in_hbm, w_in_ref),
        (dout_hbm, dout_ref), (w_out_hbm, w_out_ref), (decay_hbm, decay_ref),
    )
    copies = [pltpu.make_async_copy(a, b, sems.at[i]) for i, (a, b) in enumerate(pairs)]
    for copy in copies:
        copy.start()
    copies[0].wait()
    copies[1].wait()
    u = dot(rows_ref[...], w_up_ref[...]).astype(BF)
    copies[2].wait()
    proj_ref[...] = dot(u, w_in_ref[...]).astype(BF)
    copies[3].wait()
    copies[4].wait()
    dy_ref[...] = dot(w_out_ref[...], dout_ref[...], NT).astype(BF)
    copies[5].wait()
    logs = split3(jnp.log(decay_ref[...]))
    r = lax.broadcasted_iota(jnp.int32, (T, T), 0)
    c = lax.broadcasted_iota(jnp.int32, (T, T), 1)
    upper = (r <= c).astype(F32).astype(BF)
    lower = (c <= r).astype(F32).astype(BF)
    cum = sum(dot(p, upper) for p in logs)
    cum_ref[...] = cum
    cumt_ref[...] = sum(dot(lower, p, NT) for p in logs)
    start = jnp.exp(cum)
    c_nat = proj_ref[:, INNER + N :]
    scaled = jnp.concatenate(
        [
            (dy_ref[h * HP : (h + 1) * HP, :].astype(F32) * (SC * start[h : h + 1, :])).astype(BF)
            for h in range(H)
        ],
        axis=0,
    )
    sums = dot(scaled, c_nat).astype(BF)
    amount = jnp.exp(cum[:, T - 1 : T])
    parts = [jnp.broadcast_to(p.astype(F32), (H, N)) for p in split3(amount)]
    row = lax.broadcasted_iota(jnp.int32, (SROWS - HP, N), 0)
    for h in range(H):
        send_ref[h, 0:HP, :] = sums[h * HP : (h + 1) * HP, :]
        tail = jnp.where(
            row == 0,
            parts[0][h : h + 1, :],
            jnp.where(row == 1, parts[1][h : h + 1, :], jnp.where(row == 2, parts[2][h : h + 1, :], 0.0)),
        )
        send_ref[h, HP:SROWS, :] = tail.astype(BF)


def scan_kernel(got_ref, out_ref):
    carry = jnp.zeros((HP, N), F32)
    for j in range(CTX - 1, -1, -1):
        out_ref[j, :, :] = carry.astype(BF)
        if j:
            tail = got_ref[j, HP:SROWS, :].astype(F32)
            amount = tail[0:1, :] + tail[1:2, :] + tail[2:3, :]
            carry = got_ref[j, 0:HP, :].astype(F32) + amount * carry


def local_kernel(proj_ref, dy_ref, cum_ref, cumt_ref, h0_ref, dout_ref, index_ref, skip_ref, core_ref,
                 keep_ref, give_ref, dx_ref, dbt_ref, dct_ref, misc_ref, hits_ref, y_ref, sdy_ref, h0t_ref, sum_ref):
    proj_t = jnp.transpose(proj_ref[...])
    bt = proj_t[INNER : INNER + N, :]
    ct = proj_t[INNER + N :, :]
    b_nat = proj_ref[:, INNER : INNER + N]
    c_nat = proj_ref[:, INNER + N :]
    pair = (SC * DT) * dot(b_nat, c_nat, NT)
    r = lax.broadcasted_iota(jnp.int32, (N, N), 0)
    c = lax.broadcasted_iota(jnp.int32, (N, N), 1)
    causal = r <= c
    cum = cum_ref[...]
    cumt = cumt_ref[...]
    start = jnp.exp(cum)
    h0t_ref[...] = h0_ref[...].astype(BF)
    y_ref[...] = dot(h0t_ref[...], ct)
    skip_sums = []
    a00 = jnp.zeros((N, N), F32)
    a01 = jnp.zeros((N, N), F32)
    a11 = jnp.zeros((N, N), F32)
    zero = jnp.zeros((N, N), BF)
    zrow = jnp.zeros((HP, T), BF)
    for h in range(H):
        lo, hi = h * HP, (h + 1) * HP
        row0, row1 = cum[h : h + 1, :N], cum[h : h + 1, N:]
        col0, col1 = cumt[:N, h : h + 1], cumt[N:, h : h + 1]
        m00 = jnp.exp(jnp.where(causal, row0 - col0, -1e30))
        m01 = jnp.exp(row1 - col0)
        m11 = jnp.exp(jnp.where(causal, row1 - col1, -1e30))
        weights = jnp.concatenate(
            [
                jnp.concatenate([(m00 * pair[:N, :N]).astype(BF), (m01 * pair[:N, N:]).astype(BF)], axis=1),
                jnp.concatenate([zero, (m11 * pair[N:, N:]).astype(BF)], axis=1),
            ],
            axis=0,
        )
        x_h = proj_t[lo:hi, :]
        dy_h = dy_ref[lo:hi, :]
        x_f, dy_f = x_h.astype(F32), dy_h.astype(F32)
        st = start[h : h + 1, :]
        skip = skip_ref[h]
        y_ref[lo:hi, :] = dot(x_h, weights) + SC * st * y_ref[lo:hi, :] + skip * x_f
        dx_ref[lo:hi, :] = dot(dy_h, weights, NT) + skip * dy_f
        sdy_ref[lo:hi, :] = (st * dy_f).astype(BF)
        x_pair = proj_ref[:, (h // 2) * N : (h // 2 + 1) * N]
        dy_z = jnp.concatenate([dy_h, zrow] if h % 2 == 0 else [zrow, dy_h], axis=0)
        q0 = dot(x_pair[:N, :], dy_z)
        q11 = dot(x_pair[N:, :], dy_z[:, N:])
        a00 += m00 * q0[:, :N]
        a01 += m01 * q0[:, N:]
        a11 += m11 * q11
        skip_sums.append(jnp.sum(x_f * dy_f, keepdims=True))
    core = core_ref[0]
    half = INNER // 2
    mine = pl.ds(pl.multiple_of(core * half, half), half)
    other = pl.ds(pl.multiple_of((1 - core) * half, half), half)
    give_ref[...] = dot(y_ref[other, :].astype(BF), dout_ref[...]).astype(BF)
    keep_ref[...] = dot(y_ref[mine, :].astype(BF), dout_ref[...])
    sum_ref[:N, :N] = a00.astype(BF)
    sum_ref[:N, N:] = a01.astype(BF)
    sum_ref[N:, :N] = zero
    sum_ref[N:, N:] = a11.astype(BF)
    a = sum_ref[...]
    dct_ref[...] = (SC * (DT * dot(bt, a) + dot(h0t_ref[...], sdy_ref[...], TN))).astype(BF)
    dbt_ref[...] = (DT * SC) * dot(ct, a, NT)
    index = index_ref[...]
    owner_row = lax.shift_right_logical(index, 9)
    rr = lax.broadcasted_iota(jnp.int32, (T, T), 0)
    cc = lax.broadcasted_iota(jnp.int32, (T, T), 1)
    index_col = jnp.sum(jnp.where(rr == cc, index.astype(F32), 0.0), axis=1, keepdims=True)
    index_col = index_col.astype(jnp.int32)
    owner_col = lax.shift_right_logical(index_col, 9)
    same = owner_col == owner_row
    rank_row = jnp.sum(jnp.where(same & (rr < cc), 1.0, 0.0), axis=0, keepdims=True).astype(jnp.int32)
    rank_col = jnp.sum(jnp.where(same & (cc < rr), 1.0, 0.0), axis=1, keepdims=True).astype(jnp.int32)
    local_col = index_col - owner_col * ROWS_DEV
    id_hi = lax.shift_right_logical(local_col, 1)
    id_lo = local_col - 2 * id_hi
    v = jnp.where(cc == rank_col, id_hi, jnp.where(cc == rank_col + 64, id_lo, 0))
    row_id = lax.broadcasted_iota(jnp.int32, (8 * DEV, T), 0)
    hits_ref[...] = jnp.where(row_id == owner_row * 8 + 2 + rank_row, 1.0, 0.0).astype(BF)
    heads = jnp.where(row_id == owner_row * 8 + 6, 1.0, 0.0).astype(BF)
    lane = lax.broadcasted_iota(jnp.int32, (1, T), 1)
    extra = jnp.zeros((1, T), F32)
    for h in range(H):
        whole = skip_sums[h]
        top = whole.astype(BF).astype(F32)
        extra = extra + jnp.where(lane == 128 + h, top, 0.0) + jnp.where(lane == 160 + h, whole - top, 0.0)
    misc = dot(heads, v.astype(F32).astype(BF))
    misc_ref[...] = (misc + jnp.where((row_id & 7) == 6, extra, 0.0)).astype(BF)


def finish_kernel(carry_hbm, proj_hbm, cum_hbm, dx_hbm, dbt_hbm, dct_hbm, misc_hbm, hits_hbm, rows_hbm,
                  w_in_hbm, w_up_hbm, outer_hbm, out_hbm,
                  carry_ref, proj_ref, cum_ref, dx_ref, dbt_ref, d_ref, misc_ref, hits_ref, rows_ref,
                  w_in_ref, w_up_ref, tx_ref, left_ref, right_ref, sems):
    copies = [
        pltpu.make_async_copy(a, b, sems.at[n])
        for n, (a, b) in enumerate((
            (carry_hbm, carry_ref), (proj_hbm, proj_ref), (cum_hbm, cum_ref), (dx_hbm, dx_ref),
            (dbt_hbm, dbt_ref), (dct_hbm, d_ref.at[INNER + N :, :]), (rows_hbm, rows_ref),
            (w_in_hbm, w_in_ref), (w_up_hbm, w_up_ref), (hits_hbm, hits_ref), (misc_hbm, misc_ref),
            (outer_hbm, out_hbm.at[:, 2 * E :]),
        ))
    ]
    for copy in copies:
        copy.start()
    for copy in copies[:3]:
        copy.wait()
    proj_t = jnp.transpose(proj_ref[...])
    bt = proj_t[INNER : INNER + N, :]
    cum = cum_ref[...]
    tail = DT * jnp.exp(cum[:, T - 1 : T] - cum)
    carry = carry_ref[...]
    entering = dot(carry, bt)
    copies[3].wait()
    for h in range(H):
        lo, hi = h * HP, (h + 1) * HP
        tl = tail[h : h + 1, :]
        d_ref[lo:hi, :] = (dx_ref[lo:hi, :] + tl * entering[lo:hi, :]).astype(BF)
        tx_ref[lo:hi, :] = (tl * proj_t[lo:hi, :].astype(F32)).astype(BF)
    for copy in copies[4:7]:
        copy.wait()
    d_ref[INNER : INNER + N, :] = (dbt_ref[...] + dot(carry, tx_ref[...], TN)).astype(BF)
    d = d_ref[...]
    g = dot(d, rows_ref[...]).astype(BF)
    left_ref[...] = g[:INNER, :]
    out_left = pltpu.make_async_copy(left_ref, out_hbm.at[:, :E], sems.at[12])
    out_left.start()
    copies[7].wait()
    du = dot(w_in_ref[...], d).astype(BF)
    copies[8].wait()
    de = dot(w_up_ref[...], du).astype(BF)
    r = lax.broadcasted_iota(jnp.int32, (8 * DEV, 2 * N), 0)
    j = lax.broadcasted_iota(jnp.int32, (1, 2 * N), 1)
    place = jnp.where(r == 8 * lax.shift_right_logical(j, 1) + (j & 1), 1.0, 0.0).astype(BF)
    copies[9].wait()
    copies[10].wait()
    misc = misc_ref[...].astype(F32) + dot(hits_ref[...], de, NT) + dot(place, g[INNER:, :])
    right_ref[...] = misc.astype(BF)
    out_right = pltpu.make_async_copy(right_ref, out_hbm.at[:, E : 2 * E], sems.at[13])
    out_right.start()
    copies[11].wait()
    out_left.wait()
    out_right.wait()


def pair_kernel(keep_ref, got_ref, out_ref):
    total = (keep_ref[...] + got_ref[...].astype(F32)).astype(BF)
    out_ref[: INNER // 2, :] = total[:, :E]
    out_ref[INNER // 2 :, :] = total[:, E:]


def sum_kernel(got_ref, chunk_ref, skip_ref):
    total = jnp.sum(got_ref[:, :, : 2 * E].astype(F32), axis=0)
    side = jnp.concatenate([total[0:2, E : E + N], total[0:2, E + N :], jnp.zeros((4, N), F32)], axis=0)
    outer = got_ref[:, :, 2 * E :].reshape(4, 2, CTX, 8, E)
    halves = [jnp.sum(outer[:, c].reshape(DEV // 2, 8, E).astype(F32), axis=0) for c in range(2)]
    chunk = jnp.concatenate([total[:, :E], side] + halves, axis=1)
    chunk_ref[...] = jnp.broadcast_to(chunk[None], chunk_ref.shape).astype(BF)
    skip_ref[...] = total[6:7, E + 128 : E + 256]


def table_kernel(got_ref, table_ref):
    misc = got_ref[:, :, E : 2 * E]
    ids = misc[:, 6:7, 0:128].astype(F32)
    sub = lax.broadcasted_iota(jnp.int32, (DEV, 8, 128), 1) - 2
    lane = lax.broadcasted_iota(jnp.int32, (DEV, 8, 128), 2)
    want = jnp.where(lane == sub, 2.0, jnp.where(lane == sub + 64, 1.0, 0.0))
    row = jnp.sum(ids * want, axis=2, keepdims=True)
    row = jnp.where((sub[:, :, :1] >= 0) & (sub[:, :, :1] < CAP), row, -1.0)
    rid = lax.broadcasted_iota(jnp.int32, (DEV, 8, ROWS_DEV), 2).astype(F32)
    hits = jnp.where(rid == row, 1.0, 0.0).reshape(DEV * 8, ROWS_DEV).astype(BF)
    table_ref[...] = dot(hits, misc.reshape(DEV * 8, E), TN)


def last_kernel(core_ref, own_ref, other_ref, w_up_ref, w_in_ref, up_ref, in_ref, go_ref, g_ref, side_ref):
    step = pl.program_id(0)
    core = core_ref[0]
    sources = ((core, own_ref), (1 - core, other_ref))

    @pl.when(step == 0)
    def _():
        for x in range(4):
            for at, ref in sources:
                rows = pl.ds(pl.multiple_of((2 * x + at) * N, N), N)
                g_ref[rows, :] = ref[x * N : (x + 1) * N, :E]
                side_ref[rows, :] = ref[x * N : (x + 1) * N, E : E + N]
        j = lax.broadcasted_iota(jnp.int32, (2 * N, 8 * DEV), 0)
        r = lax.broadcasted_iota(jnp.int32, (2 * N, 8 * DEV), 1)
        first = r - (8 * lax.shift_right_logical(j, 1) + (j & 1))
        for m in range(2):
            pick = jnp.where(first == 2 * m, 1.0, 0.0).astype(BF)
            g_ref[INNER:, m * N : (m + 1) * N] = dot(pick, side_ref[...]).astype(BF)

    g = g_ref[...]
    in_ref[...] = lax.dot_general(w_up_ref[...], g, (((0,), (1,)), ((), ())), preferred_element_type=F32)
    up_ref[...] = jnp.transpose(dot(w_in_ref[...], g))
    lanes = pl.ds(pl.multiple_of(E + N + E * lax.shift_right_logical(step, 1), N), E)
    for m in range(2):
        rows = pl.ds(pl.multiple_of((2 * m + (step & 1)) * N, N), N)
        for at, ref in sources:
            go_ref[pl.ds(pl.multiple_of(at * N, N), N), m * E : (m + 1) * E] = ref[rows, lanes].astype(F32)


def local(event_rows, event_index, decay, saved_state, dout, w_up, w_in, w_out, skip):
    every = ("x", "core", "y", "z")
    rows, d_out = event_rows[0], dout[0]
    proj, dy, cum, cumt, sums = call(
        project_kernel,
        [((T, PROJ), BF), ((INNER, T), BF), ((H, T), F32), ((T, H), F32), ((H, SROWS, N), BF)],
        BIG, 750_000_000, 4_500_000,
        in_specs=[HBM] * 6, out_specs=(VM,) * 5,
        scratch_shapes=[
            pltpu.VMEM((T, E), BF), pltpu.VMEM((T, D), BF), pltpu.VMEM((H, T), F32),
            pltpu.VMEM((E, D), BF), pltpu.VMEM((D, PROJ), BF), pltpu.VMEM((INNER, D), BF),
            pltpu.SemaphoreType.DMA((6,)),
        ],
    )(rows, d_out, decay[0], w_up, w_in, w_out)
    got = lax.all_to_all(sums, ("y", "z"), 0, 0, tiled=True)
    core = lax.axis_index("core").reshape(1)
    keep, give, dx, dbt, dct, misc, hits = call(
        local_kernel,
        [((INNER // 2, D), F32), ((INNER // 2, D), BF), ((INNER, T), F32), ((N, T), F32), ((N, T), BF),
         ((8 * DEV, E), BF), ((8 * DEV, T), BF)],
        BIG, 2_500_000_000, 6_000_000,
        in_specs=[VM] * 7 + [SM] * 2, out_specs=(VM,) * 7,
        scratch_shapes=[
            pltpu.VMEM((INNER, T), F32), pltpu.VMEM((INNER, T), BF),
            pltpu.VMEM((INNER, N), BF), pltpu.VMEM((T, T), BF),
        ],
    )(proj, dy, cum, cumt, jnp.swapaxes(saved_state[0, 0], 1, 2).reshape(INNER, N), d_out, event_index, skip, core)
    got, give = lax.optimization_barrier((got, give))
    (carries,) = call(
        scan_kernel, [((CTX, HP, N), BF)], 8, 4_000_000, 600_000, in_specs=[VM], out_specs=(VM,)
    )(got)
    carry = lax.all_to_all(carries, ("y", "z"), 0, 0, tiled=True)
    (outer,) = call(
        pair_kernel, [((8 * DEV, E), BF)], 8, 300_000, 2_000_000, in_specs=[VM] * 2, out_specs=(VM,)
    )(keep, lax.ppermute(give, "core", [(0, 1), (1, 0)]))
    carry, outer = lax.optimization_barrier((carry, outer))
    (pay,) = call(
        finish_kernel, [((8 * DEV, 3 * E), BF)], BIG, 1_400_000_000, 6_000_000,
        in_specs=[HBM] * 12, out_specs=(HBM,),
        scratch_shapes=[
            pltpu.VMEM((INNER, N), BF), pltpu.VMEM((T, PROJ), BF), pltpu.VMEM((H, T), F32),
            pltpu.VMEM((INNER, T), F32), pltpu.VMEM((N, T), F32), pltpu.VMEM((PROJ, T), BF),
            pltpu.VMEM((8 * DEV, E), BF), pltpu.VMEM((8 * DEV, T), BF), pltpu.VMEM((T, E), BF),
            pltpu.VMEM((D, PROJ), BF), pltpu.VMEM((E, D), BF), pltpu.VMEM((INNER, T), BF),
            pltpu.VMEM((INNER, E), BF), pltpu.VMEM((8 * DEV, E), BF), pltpu.SemaphoreType.DMA((14,)),
        ],
    )(carry.reshape(INNER, N), proj, cum, dx, dbt, dct, misc, hits, rows, w_in, w_up, outer)
    pay_got = lax.all_to_all(pay.reshape(DEV, 8, 3 * E), every, 0, 0, tiled=True)
    chunk, skip_sum = call(
        sum_kernel, [((DEV // 2, 8, 7 * N), BF), ((1, 128), F32)], 12, 2_000_000, 3_000_000,
        in_specs=[VM], out_specs=(VM,) * 2,
    )(pay_got)
    whole = lax.all_to_all(chunk, ("x", "y", "z"), 0, 0, tiled=True).reshape(DEV * 4, 7 * N)
    other = lax.ppermute(whole, "core", [(0, 1), (1, 0)])
    (table,) = call(
        table_kernel, [((ROWS_DEV, E), F32)], 12, 400_000_000, 2_000_000, in_specs=[VM], out_specs=(VM,)
    )(pay_got)
    full = pl.BlockSpec((DEV * 4, 7 * N), lambda i: (0, 0))
    column = pl.BlockSpec((E, D // 4), lambda i: (0, i))
    row = pl.BlockSpec((D // 4, PROJ), lambda i: (i, 0))
    grad_up, grad_in, grad_out = pl.pallas_call(
        last_kernel,
        grid=(4,),
        out_shape=tuple(jax.ShapeDtypeStruct(s, F32) for s in ((E, D), (D, PROJ), (INNER, D))),
        in_specs=[SM, full, full, column, row],
        out_specs=(column, row, pl.BlockSpec((INNER // 4, D), lambda i: (i, 0))),
        scratch_shapes=[pltpu.VMEM((PROJ, E), BF), pltpu.VMEM((8 * DEV, N), BF)],
        compiler_params=pltpu.CompilerParams(vmem_limit_bytes=24 * MB),
        cost_estimate=pl.CostEstimate(flops=700_000_000, bytes_accessed=8_000_000, transcendentals=0),
    )(core, whole, other, w_up, w_in)
    grad_skip = skip_sum[0, :H] + skip_sum[0, 32 : 32 + H]
    return (grad_up, grad_in, grad_out, grad_skip, table)


def solution(mesh):
    mesh = Mesh(mesh.devices.reshape(4, 2, 4, 4), ("x", "core", "y", "z"))
    batch, ctx = ("x", "core"), ("y", "z")
    in_specs = (
        P(batch, ctx, None),
        P(batch, ctx),
        P(batch, None, ctx),
        P(batch, ctx, None, None, None),
        P(batch, ctx, None),
        P(),
        P(),
        P(),
        P(),
    )
    out_specs = (P(), P(), P(), P(), P(batch + ctx, None))
    return jax.shard_map(local, mesh=mesh, in_specs=in_specs, out_specs=out_specs, check_vma=False)
```

```python
from functools import partial

import jax
import jax.numpy as jnp
from jax import lax
from jax.experimental import pallas as pl
from jax.experimental.pallas import tpu as pltpu
from jax.sharding import Mesh, PartitionSpec as P

T = 256
E = 256
D = 512
H = 16
HP = 64
N = 128
INNER = H * HP
PROJ = INNER + 2 * N
ROWS_DEV = 512
CAP = 4
DEV = 128
CTX = 16
SROWS = 80

DT = 0.0625
SC = 128.0**-0.5
F32 = jnp.float32
BF = jnp.bfloat16
NN = (((1,), (0,)), ((), ()))
NT = (((1,), (1,)), ((), ()))
TN = (((0,), (0,)), ((), ()))
MB = 1 << 20
BIG = 60


def dot(a, b, dims=NN):
    return lax.dot_general(a, b, dims, preferred_element_type=F32)


def split3(v):
    hi = v.astype(BF)
    rest = v - hi.astype(F32)
    mid = rest.astype(BF)
    return hi, mid, (rest - mid.astype(F32)).astype(BF)


def call(kernel, outs, vmem, flops, nbytes, **kw):
    return pl.pallas_call(
        kernel,
        out_shape=tuple(jax.ShapeDtypeStruct(s, d) for s, d in outs),
        compiler_params=pltpu.CompilerParams(vmem_limit_bytes=vmem * MB),
        cost_estimate=pl.CostEstimate(flops=flops, bytes_accessed=nbytes, transcendentals=0),
        **kw,
    )


VM = pl.BlockSpec(memory_space=pltpu.VMEM)
HBM = pl.BlockSpec(memory_space=pltpu.HBM)
SM = pl.BlockSpec(memory_space=pltpu.SMEM)


def project_kernel(rows_hbm, dout_hbm, decay_hbm, w_up_hbm, w_in_hbm, w_out_hbm,
                   proj_ref, dy_ref, cum_ref, cumt_ref, send_ref,
                   rows_ref, dout_ref, decay_ref, w_up_ref, w_in_ref, w_out_ref, sems):
    pairs = (
        (rows_hbm, rows_ref), (w_up_hbm, w_up_ref), (w_in_hbm, w_in_ref),
        (dout_hbm, dout_ref), (w_out_hbm, w_out_ref), (decay_hbm, decay_ref),
    )
    copies = [pltpu.make_async_copy(a, b, sems.at[i]) for i, (a, b) in enumerate(pairs)]
    for copy in copies:
        copy.start()
    copies[0].wait()
    copies[1].wait()
    u = dot(rows_ref[...], w_up_ref[...]).astype(BF)
    copies[2].wait()
    proj_ref[...] = dot(u, w_in_ref[...]).astype(BF)
    copies[3].wait()
    copies[4].wait()
    dy_ref[...] = dot(w_out_ref[...], dout_ref[...], NT).astype(BF)
    copies[5].wait()
    logs = split3(jnp.log(decay_ref[...]))
    r = lax.broadcasted_iota(jnp.int32, (T, T), 0)
    c = lax.broadcasted_iota(jnp.int32, (T, T), 1)
    upper = (r <= c).astype(F32).astype(BF)
    lower = (c <= r).astype(F32).astype(BF)
    cum = sum(dot(p, upper) for p in logs)
    cum_ref[...] = cum
    cumt_ref[...] = sum(dot(lower, p, NT) for p in logs)
    start = jnp.exp(cum)
    c_nat = proj_ref[:, INNER + N :]
    scaled = jnp.concatenate(
        [
            (dy_ref[h * HP : (h + 1) * HP, :].astype(F32) * (SC * start[h : h + 1, :])).astype(BF)
            for h in range(H)
        ],
        axis=0,
    )
    sums = dot(scaled, c_nat).astype(BF)
    amount = jnp.exp(cum[:, T - 1 : T])
    parts = [jnp.broadcast_to(p.astype(F32), (H, N)) for p in split3(amount)]
    row = lax.broadcasted_iota(jnp.int32, (SROWS - HP, N), 0)
    for h in range(H):
        send_ref[h, 0:HP, :] = sums[h * HP : (h + 1) * HP, :]
        tail = jnp.where(
            row == 0,
            parts[0][h : h + 1, :],
            jnp.where(row == 1, parts[1][h : h + 1, :], jnp.where(row == 2, parts[2][h : h + 1, :], 0.0)),
        )
        send_ref[h, HP:SROWS, :] = tail.astype(BF)


def scan_kernel(got_ref, out_ref):
    carry = jnp.zeros((HP, N), F32)
    for j in range(CTX - 1, -1, -1):
        out_ref[j, :, :] = carry.astype(BF)
        if j:
            tail = got_ref[j, HP:SROWS, :].astype(F32)
            amount = tail[0:1, :] + tail[1:2, :] + tail[2:3, :]
            carry = got_ref[j, 0:HP, :].astype(F32) + amount * carry


def local_kernel(proj_ref, dy_ref, cum_ref, cumt_ref, h0_ref, dout_ref, index_ref, skip_ref, core_ref,
                 keep_ref, give_ref, dx_ref, tx_ref, bt_ref, dbt_ref, dct_ref, misc_ref, hits_ref, y_ref, sdy_ref, h0t_ref, sum_ref):
    proj_t = jnp.transpose(proj_ref[...])
    bt = proj_t[INNER : INNER + N, :]
    ct = proj_t[INNER + N :, :]
    b_nat = proj_ref[:, INNER : INNER + N]
    c_nat = proj_ref[:, INNER + N :]
    pair = (SC * DT) * dot(b_nat, c_nat, NT)
    r = lax.broadcasted_iota(jnp.int32, (N, N), 0)
    c = lax.broadcasted_iota(jnp.int32, (N, N), 1)
    causal = r <= c
    cum = cum_ref[...]
    cumt = cumt_ref[...]
    start = jnp.exp(cum)
    tail = DT * jnp.exp(cum[:, T - 1 : T] - cum)
    bt_ref[...] = bt
    h0t_ref[...] = h0_ref[...].astype(BF)
    y_ref[...] = dot(h0t_ref[...], ct)
    skip_sums = []
    a00 = jnp.zeros((N, N), F32)
    a01 = jnp.zeros((N, N), F32)
    a11 = jnp.zeros((N, N), F32)
    zero = jnp.zeros((N, N), BF)
    zrow = jnp.zeros((HP, T), BF)
    for h in range(H):
        lo, hi = h * HP, (h + 1) * HP
        row0, row1 = cum[h : h + 1, :N], cum[h : h + 1, N:]
        col0, col1 = cumt[:N, h : h + 1], cumt[N:, h : h + 1]
        m00 = jnp.exp(jnp.where(causal, row0 - col0, -1e30))
        m01 = jnp.exp(row1 - col0)
        m11 = jnp.exp(jnp.where(causal, row1 - col1, -1e30))
        weights = jnp.concatenate(
            [
                jnp.concatenate([(m00 * pair[:N, :N]).astype(BF), (m01 * pair[:N, N:]).astype(BF)], axis=1),
                jnp.concatenate([zero, (m11 * pair[N:, N:]).astype(BF)], axis=1),
            ],
            axis=0,
        )
        x_h = proj_t[lo:hi, :]
        dy_h = dy_ref[lo:hi, :]
        x_f, dy_f = x_h.astype(F32), dy_h.astype(F32)
        st = start[h : h + 1, :]
        skip = skip_ref[h]
        y_ref[lo:hi, :] = dot(x_h, weights) + SC * st * y_ref[lo:hi, :] + skip * x_f
        dx_ref[lo:hi, :] = dot(dy_h, weights, NT) + skip * dy_f
        sdy_ref[lo:hi, :] = (st * dy_f).astype(BF)
        tx_ref[lo:hi, :] = (tail[h : h + 1, :] * x_f).astype(BF)
        x_pair = proj_ref[:, (h // 2) * N : (h // 2 + 1) * N]
        dy_z = jnp.concatenate([dy_h, zrow] if h % 2 == 0 else [zrow, dy_h], axis=0)
        q0 = dot(x_pair[:N, :], dy_z)
        q11 = dot(x_pair[N:, :], dy_z[:, N:])
        a00 += m00 * q0[:, :N]
        a01 += m01 * q0[:, N:]
        a11 += m11 * q11
        skip_sums.append(jnp.sum(x_f * dy_f, keepdims=True))
    core = core_ref[0]
    half = INNER // 2
    mine = pl.ds(pl.multiple_of(core * half, half), half)
    other = pl.ds(pl.multiple_of((1 - core) * half, half), half)
    give_ref[...] = dot(y_ref[other, :].astype(BF), dout_ref[...]).astype(BF)
    keep_ref[...] = dot(y_ref[mine, :].astype(BF), dout_ref[...])
    sum_ref[:N, :N] = a00.astype(BF)
    sum_ref[:N, N:] = a01.astype(BF)
    sum_ref[N:, :N] = zero
    sum_ref[N:, N:] = a11.astype(BF)
    a = sum_ref[...]
    dct_ref[...] = (SC * (DT * dot(bt, a) + dot(h0t_ref[...], sdy_ref[...], TN))).astype(BF)
    dbt_ref[...] = (DT * SC) * dot(ct, a, NT)
    index = index_ref[...]
    owner_row = lax.shift_right_logical(index, 9)
    rr = lax.broadcasted_iota(jnp.int32, (T, T), 0)
    cc = lax.broadcasted_iota(jnp.int32, (T, T), 1)
    index_col = jnp.sum(jnp.where(rr == cc, index.astype(F32), 0.0), axis=1, keepdims=True)
    index_col = index_col.astype(jnp.int32)
    owner_col = lax.shift_right_logical(index_col, 9)
    same = owner_col == owner_row
    rank_row = jnp.sum(jnp.where(same & (rr < cc), 1.0, 0.0), axis=0, keepdims=True).astype(jnp.int32)
    rank_col = jnp.sum(jnp.where(same & (cc < rr), 1.0, 0.0), axis=1, keepdims=True).astype(jnp.int32)
    local_col = index_col - owner_col * ROWS_DEV
    id_hi = lax.shift_right_logical(local_col, 1)
    id_lo = local_col - 2 * id_hi
    v = jnp.where(cc == rank_col, id_hi, jnp.where(cc == rank_col + 64, id_lo, 0))
    row_id = lax.broadcasted_iota(jnp.int32, (8 * DEV, T), 0)
    hits_ref[...] = jnp.where(row_id == owner_row * 8 + 2 + rank_row, 1.0, 0.0).astype(BF)
    heads = jnp.where(row_id == owner_row * 8 + 6, 1.0, 0.0).astype(BF)
    lane = lax.broadcasted_iota(jnp.int32, (1, T), 1)
    extra = jnp.zeros((1, T), F32)
    for h in range(H):
        whole = skip_sums[h]
        top = whole.astype(BF).astype(F32)
        extra = extra + jnp.where(lane == 128 + h, top, 0.0) + jnp.where(lane == 160 + h, whole - top, 0.0)
    misc = dot(heads, v.astype(F32).astype(BF))
    misc_ref[...] = (misc + jnp.where((row_id & 7) == 6, extra, 0.0)).astype(BF)


def finish_kernel(carry_hbm, bt_hbm, cum_hbm, dx_hbm, tx_hbm, dbt_hbm, dct_hbm, rows_hbm,
                  w_in_hbm, w_up_hbm, hits_hbm, misc_hbm, outer_hbm, out_hbm,
                  carry_ref, bt_ref, cum_ref, dx_ref, tx_ref, dbt_ref, d_ref, rows_ref,
                  w_in_ref, w_up_ref, hits_ref, misc_ref, outer_ref, left_ref, right_ref, sems):
    copies = [
        pltpu.make_async_copy(a, b, sems.at[n])
        for n, (a, b) in enumerate((
            (carry_hbm, carry_ref), (bt_hbm, bt_ref), (cum_hbm, cum_ref), (dx_hbm, dx_ref), (tx_hbm, tx_ref),
            (dbt_hbm, dbt_ref), (dct_hbm, d_ref.at[INNER + N :, :]), (rows_hbm, rows_ref),
            (w_in_hbm, w_in_ref), (w_up_hbm, w_up_ref), (hits_hbm, hits_ref), (misc_hbm, misc_ref),
            (outer_hbm, outer_ref),
        ))
    ]
    for copy in copies:
        copy.start()
    for copy in copies[:3]:
        copy.wait()
    cum = cum_ref[...]
    tail = DT * jnp.exp(cum[:, T - 1 : T] - cum)
    carry = carry_ref[...]
    entering = dot(carry, bt_ref[...])
    copies[3].wait()
    for h in range(H):
        lo, hi = h * HP, (h + 1) * HP
        d_ref[lo:hi, :] = (dx_ref[lo:hi, :] + tail[h : h + 1, :] * entering[lo:hi, :]).astype(BF)
    for copy in copies[4:8]:
        copy.wait()
    d_ref[INNER : INNER + N, :] = (dbt_ref[...] + dot(carry, tx_ref[...], TN)).astype(BF)
    d = d_ref[...]
    g = dot(d, rows_ref[...]).astype(BF)
    left_ref[...] = g[:INNER, :]
    outs = [pltpu.make_async_copy(left_ref, out_hbm.at[:, :E], sems.at[13])]
    outs[0].start()
    copies[8].wait()
    du = dot(w_in_ref[...], d).astype(BF)
    copies[9].wait()
    de = dot(w_up_ref[...], du).astype(BF)
    r = lax.broadcasted_iota(jnp.int32, (8 * DEV, 2 * N), 0)
    j = lax.broadcasted_iota(jnp.int32, (1, 2 * N), 1)
    place = jnp.where(r == 8 * lax.shift_right_logical(j, 1) + (j & 1), 1.0, 0.0).astype(BF)
    for copy in copies[10:]:
        copy.wait()
    outs.append(pltpu.make_async_copy(outer_ref, out_hbm.at[:, 2 * E :], sems.at[14]))
    outs[1].start()
    misc = misc_ref[...].astype(F32) + dot(hits_ref[...], de, NT) + dot(place, g[INNER:, :])
    right_ref[...] = misc.astype(BF)
    outs.append(pltpu.make_async_copy(right_ref, out_hbm.at[:, E : 2 * E], sems.at[15]))
    outs[2].start()
    for copy in outs:
        copy.wait()


def pair_kernel(keep_ref, got_ref, out_ref):
    total = (keep_ref[...] + got_ref[...].astype(F32)).astype(BF)
    out_ref[: INNER // 2, :] = total[:, :E]
    out_ref[INNER // 2 :, :] = total[:, E:]


def sum_kernel(got_ref, chunk_ref, skip_ref):
    total = jnp.sum(got_ref[:, :, : 2 * E].astype(F32), axis=0)
    side = jnp.concatenate([total[0:2, E : E + N], total[0:2, E + N :], jnp.zeros((4, N), F32)], axis=0)
    outer = got_ref[:, :, 2 * E :].reshape(4, 2, CTX, 8, E)
    halves = [jnp.sum(outer[:, c].reshape(DEV // 2, 8, E).astype(F32), axis=0) for c in range(2)]
    chunk = jnp.concatenate([total[:, :E], side] + halves, axis=1)
    chunk_ref[...] = jnp.broadcast_to(chunk[None], chunk_ref.shape).astype(BF)
    skip_ref[...] = total[6:7, E + 128 : E + 256]


def table_kernel(got_ref, table_ref):
    misc = got_ref[:, :, E : 2 * E]
    ids = misc[:, 6:7, 0:128].astype(F32)
    sub = lax.broadcasted_iota(jnp.int32, (DEV, 8, 128), 1) - 2
    lane = lax.broadcasted_iota(jnp.int32, (DEV, 8, 128), 2)
    want = jnp.where(lane == sub, 2.0, jnp.where(lane == sub + 64, 1.0, 0.0))
    row = jnp.sum(ids * want, axis=2, keepdims=True)
    row = jnp.where((sub[:, :, :1] >= 0) & (sub[:, :, :1] < CAP), row, -1.0)
    rid = lax.broadcasted_iota(jnp.int32, (DEV, 8, ROWS_DEV), 2).astype(F32)
    hits = jnp.where(rid == row, 1.0, 0.0).reshape(DEV * 8, ROWS_DEV).astype(BF)
    table_ref[...] = dot(hits, misc.reshape(DEV * 8, E), TN)


def last_kernel(core_ref, own_ref, other_ref, w_up_ref, w_in_ref, up_ref, in_ref, go_ref, g_ref, side_ref):
    step = pl.program_id(0)
    core = core_ref[0]
    sources = ((core, own_ref), (1 - core, other_ref))

    @pl.when(step == 0)
    def _():
        for x in range(4):
            for at, ref in sources:
                rows = pl.ds(pl.multiple_of((2 * x + at) * N, N), N)
                g_ref[rows, :] = ref[x * N : (x + 1) * N, :E]
                side_ref[rows, :] = ref[x * N : (x + 1) * N, E : E + N]
        j = lax.broadcasted_iota(jnp.int32, (2 * N, 8 * DEV), 0)
        r = lax.broadcasted_iota(jnp.int32, (2 * N, 8 * DEV), 1)
        first = r - (8 * lax.shift_right_logical(j, 1) + (j & 1))
        for m in range(2):
            pick = jnp.where(first == 2 * m, 1.0, 0.0).astype(BF)
            g_ref[INNER:, m * N : (m + 1) * N] = dot(pick, side_ref[...]).astype(BF)

    g = g_ref[...]
    in_ref[...] = lax.dot_general(w_up_ref[...], g, (((0,), (1,)), ((), ())), preferred_element_type=F32)
    up_ref[...] = jnp.transpose(dot(w_in_ref[...], g))
    lanes = pl.ds(pl.multiple_of(E + N + E * lax.shift_right_logical(step, 1), N), E)
    for m in range(2):
        rows = pl.ds(pl.multiple_of((2 * m + (step & 1)) * N, N), N)
        for at, ref in sources:
            go_ref[pl.ds(pl.multiple_of(at * N, N), N), m * E : (m + 1) * E] = ref[rows, lanes].astype(F32)


def local(event_rows, event_index, decay, saved_state, dout, w_up, w_in, w_out, skip):
    every = ("x", "core", "y", "z")
    rows, d_out = event_rows[0], dout[0]
    proj, dy, cum, cumt, sums = call(
        project_kernel,
        [((T, PROJ), BF), ((INNER, T), BF), ((H, T), F32), ((T, H), F32), ((H, SROWS, N), BF)],
        BIG, 750_000_000, 4_500_000,
        in_specs=[HBM] * 6, out_specs=(VM,) * 5,
        scratch_shapes=[
            pltpu.VMEM((T, E), BF), pltpu.VMEM((T, D), BF), pltpu.VMEM((H, T), F32),
            pltpu.VMEM((E, D), BF), pltpu.VMEM((D, PROJ), BF), pltpu.VMEM((INNER, D), BF),
            pltpu.SemaphoreType.DMA((6,)),
        ],
    )(rows, d_out, decay[0], w_up, w_in, w_out)
    got = lax.all_to_all(sums, ("y", "z"), 0, 0, tiled=True)
    core = lax.axis_index("core").reshape(1)
    keep, give, dx, tx, bt, dbt, dct, misc, hits = call(
        local_kernel,
        [((INNER // 2, D), F32), ((INNER // 2, D), BF), ((INNER, T), F32), ((INNER, T), BF), ((N, T), BF),
         ((N, T), F32), ((N, T), BF), ((8 * DEV, E), BF), ((8 * DEV, T), BF)],
        BIG, 2_500_000_000, 6_000_000,
        in_specs=[VM] * 7 + [SM] * 2, out_specs=(VM,) * 9,
        scratch_shapes=[
            pltpu.VMEM((INNER, T), F32), pltpu.VMEM((INNER, T), BF),
            pltpu.VMEM((INNER, N), BF), pltpu.VMEM((T, T), BF),
        ],
    )(proj, dy, cum, cumt, jnp.swapaxes(saved_state[0, 0], 1, 2).reshape(INNER, N), d_out, event_index, skip, core)
    got, give = lax.optimization_barrier((got, give))
    (carries,) = call(
        scan_kernel, [((CTX, HP, N), BF)], 8, 4_000_000, 600_000, in_specs=[VM], out_specs=(VM,)
    )(got)
    carry = lax.all_to_all(carries, ("y", "z"), 0, 0, tiled=True)
    (outer,) = call(
        pair_kernel, [((8 * DEV, E), BF)], 8, 300_000, 2_000_000, in_specs=[VM] * 2, out_specs=(VM,)
    )(keep, lax.ppermute(give, "core", [(0, 1), (1, 0)]))
    carry, outer = lax.optimization_barrier((carry, outer))
    (pay,) = call(
        finish_kernel, [((8 * DEV, 3 * E), BF)], BIG, 1_400_000_000, 6_000_000,
        in_specs=[HBM] * 13, out_specs=(HBM,),
        scratch_shapes=[
            pltpu.VMEM((INNER, N), BF), pltpu.VMEM((N, T), BF), pltpu.VMEM((H, T), F32),
            pltpu.VMEM((INNER, T), F32), pltpu.VMEM((INNER, T), BF), pltpu.VMEM((N, T), F32),
            pltpu.VMEM((PROJ, T), BF), pltpu.VMEM((T, E), BF), pltpu.VMEM((D, PROJ), BF), pltpu.VMEM((E, D), BF),
            pltpu.VMEM((8 * DEV, T), BF), pltpu.VMEM((8 * DEV, E), BF), pltpu.VMEM((8 * DEV, E), BF),
            pltpu.VMEM((INNER, E), BF), pltpu.VMEM((8 * DEV, E), BF), pltpu.SemaphoreType.DMA((16,)),
        ],
    )(carry.reshape(INNER, N), bt, cum, dx, tx, dbt, dct, rows, w_in, w_up, hits, misc, outer)
    pay_got = lax.all_to_all(pay.reshape(DEV, 8, 3 * E), every, 0, 0, tiled=True)
    chunk, skip_sum = call(
        sum_kernel, [((DEV // 2, 8, 7 * N), BF), ((1, 128), F32)], 12, 2_000_000, 3_000_000,
        in_specs=[VM], out_specs=(VM,) * 2,
    )(pay_got)
    whole = lax.all_to_all(chunk, ("x", "y", "z"), 0, 0, tiled=True).reshape(DEV * 4, 7 * N)
    other = lax.ppermute(whole, "core", [(0, 1), (1, 0)])
    (table,) = call(
        table_kernel, [((ROWS_DEV, E), F32)], 12, 400_000_000, 2_000_000, in_specs=[VM], out_specs=(VM,)
    )(pay_got)
    full = pl.BlockSpec((DEV * 4, 7 * N), lambda i: (0, 0))
    column = pl.BlockSpec((E, D // 4), lambda i: (0, i))
    row = pl.BlockSpec((D // 4, PROJ), lambda i: (i, 0))
    grad_up, grad_in, grad_out = pl.pallas_call(
        last_kernel,
        grid=(4,),
        out_shape=tuple(jax.ShapeDtypeStruct(s, F32) for s in ((E, D), (D, PROJ), (INNER, D))),
        in_specs=[SM, full, full, column, row],
        out_specs=(column, row, pl.BlockSpec((INNER // 4, D), lambda i: (i, 0))),
        scratch_shapes=[pltpu.VMEM((PROJ, E), BF), pltpu.VMEM((8 * DEV, N), BF)],
        compiler_params=pltpu.CompilerParams(vmem_limit_bytes=24 * MB),
        cost_estimate=pl.CostEstimate(flops=700_000_000, bytes_accessed=8_000_000, transcendentals=0),
    )(core, whole, other, w_up, w_in)
    grad_skip = skip_sum[0, :H] + skip_sum[0, 32 : 32 + H]
    return (grad_up, grad_in, grad_out, grad_skip, table)


def solution(mesh):
    mesh = Mesh(mesh.devices.reshape(4, 2, 4, 4), ("x", "core", "y", "z"))
    batch, ctx = ("x", "core"), ("y", "z")
    in_specs = (
        P(batch, ctx, None),
        P(batch, ctx),
        P(batch, None, ctx),
        P(batch, ctx, None, None, None),
        P(batch, ctx, None),
        P(),
        P(),
        P(),
        P(),
    )
    out_specs = (P(), P(), P(), P(), P(batch + ctx, None))
    return jax.shard_map(local, mesh=mesh, in_specs=in_specs, out_specs=out_specs, check_vma=False)
```

```python
from functools import partial

import jax
import jax.numpy as jnp
from jax import lax
from jax.experimental import pallas as pl
from jax.experimental.pallas import tpu as pltpu
from jax.sharding import Mesh, PartitionSpec as P

T = 256
E = 256
D = 512
H = 16
HP = 64
N = 128
INNER = H * HP
PROJ = INNER + 2 * N
ROWS_DEV = 512
CAP = 4
DEV = 128
CTX = 16
GH = 4
GR = GH * HP
MR = GR + 16

DT = 0.0625
SC = 128.0**-0.5
F32 = jnp.float32
BF = jnp.bfloat16
NN = (((1,), (0,)), ((), ()))
NT = (((1,), (1,)), ((), ()))
TN = (((0,), (0,)), ((), ()))
MB = 1 << 20
BIG = 60


def dot(a, b, dims=NN):
    return lax.dot_general(a, b, dims, preferred_element_type=F32)


def split3(v):
    hi = v.astype(BF)
    rest = v - hi.astype(F32)
    mid = rest.astype(BF)
    return hi, mid, (rest - mid.astype(F32)).astype(BF)


def call(kernel, outs, vmem, flops, nbytes, **kw):
    return pl.pallas_call(
        kernel,
        out_shape=tuple(jax.ShapeDtypeStruct(s, d) for s, d in outs),
        compiler_params=pltpu.CompilerParams(vmem_limit_bytes=vmem * MB),
        cost_estimate=pl.CostEstimate(flops=flops, bytes_accessed=nbytes, transcendentals=0),
        **kw,
    )


VM = pl.BlockSpec(memory_space=pltpu.VMEM)
HBM = pl.BlockSpec(memory_space=pltpu.HBM)
SM = pl.BlockSpec(memory_space=pltpu.SMEM)


def decay_rows(amounts):
    row = lax.broadcasted_iota(jnp.int32, (MR - GR, N), 0)
    out = jnp.zeros((MR - GR, N), F32)
    for i, amount in enumerate(amounts):
        for k, part in enumerate(split3(amount)):
            out = jnp.where(row == 3 * i + k, part.astype(F32), out)
    return out.astype(BF)


def decays(ref, at):
    rows = ref[at, GR:, :].astype(F32)
    return [rows[3 * i : 3 * i + 1] + rows[3 * i + 1 : 3 * i + 2] + rows[3 * i + 2 : 3 * i + 3] for i in range(GH)]


def sums_of(ref, at, i):
    return ref[at, i * HP : (i + 1) * HP, :].astype(F32)


def project_kernel(z_ref, rows_hbm, dout_hbm, decay_hbm, w_up_hbm, w_in_hbm, w_out_hbm,
                   proj_ref, dy_ref, cum_ref, cumt_ref, g0_ref, g1_ref, g2_ref, g3_ref,
                   rows_ref, dout_ref, decay_ref, w_up_ref, w_in_ref, w_out_ref, all_ref, sems):
    pairs = (
        (rows_hbm, rows_ref), (w_up_hbm, w_up_ref), (w_in_hbm, w_in_ref),
        (dout_hbm, dout_ref), (w_out_hbm, w_out_ref), (decay_hbm, decay_ref),
    )
    copies = [pltpu.make_async_copy(a, b, sems.at[i]) for i, (a, b) in enumerate(pairs)]
    for copy in copies:
        copy.start()
    copies[0].wait()
    copies[1].wait()
    u = dot(rows_ref[...], w_up_ref[...]).astype(BF)
    copies[2].wait()
    proj_ref[...] = dot(u, w_in_ref[...]).astype(BF)
    copies[3].wait()
    copies[4].wait()
    dy_ref[...] = dot(w_out_ref[...], dout_ref[...], NT).astype(BF)
    copies[5].wait()
    logs = split3(jnp.log(decay_ref[...]))
    r = lax.broadcasted_iota(jnp.int32, (T, T), 0)
    c = lax.broadcasted_iota(jnp.int32, (T, T), 1)
    upper = (r <= c).astype(F32).astype(BF)
    lower = (c <= r).astype(F32).astype(BF)
    cum = sum(dot(p, upper) for p in logs)
    cum_ref[...] = cum
    cumt_ref[...] = sum(dot(lower, p, NT) for p in logs)
    start = jnp.exp(cum)
    c_nat = proj_ref[:, INNER + N :]
    scaled = jnp.concatenate(
        [
            (dy_ref[h * HP : (h + 1) * HP, :].astype(F32) * (SC * start[h : h + 1, :])).astype(BF)
            for h in range(H)
        ],
        axis=0,
    )
    sums = dot(scaled, c_nat).astype(BF)
    amount = jnp.exp(cum[:, T - 1 : T])
    for q in range(H // GH):
        all_ref[q, :GR, :] = sums[q * GR : (q + 1) * GR, :]
        all_ref[q, GR:, :] = decay_rows([jnp.broadcast_to(amount[h : h + 1, :], (1, N)) for h in range(q * GH, (q + 1) * GH)])
    for k, ref in enumerate((g0_ref, g1_ref, g2_ref, g3_ref)):
        ref[...] = all_ref[(z_ref[0] + k) & 3]


def place(at, refs, out_ref):
    for k, ref in enumerate(refs):
        out_ref[(at + 4 - k) & 3] = ref[...]


def inner_kernel(z_ref, a_ref, b_ref, c_ref, d_ref, out_ref, st_ref):
    place(z_ref[0], (a_ref, b_ref, c_ref, d_ref), st_ref)
    amounts = [decays(st_ref, zz) for zz in range(4)]
    for i in range(GH):
        carry = sums_of(st_ref, 3, i)
        for zz in (2, 1, 0):
            carry = sums_of(st_ref, zz, i) + amounts[zz][i] * carry
        out_ref[i * HP : (i + 1) * HP, :] = carry.astype(BF)
    out_ref[GR:, :] = decay_rows([amounts[0][i] * amounts[1][i] * amounts[2][i] * amounts[3][i] for i in range(GH)])


def outer_kernel(y_ref, z_ref, a_ref, b_ref, c_ref, d_ref, ta_ref, tb_ref, tc_ref, td_ref,
                 g0_ref, g1_ref, g2_ref, g3_ref, st_ref, tt_ref, ct_ref):
    y, z = y_ref[0], z_ref[0]
    place(z, (a_ref, b_ref, c_ref, d_ref), st_ref)
    place(y, (ta_ref, tb_ref, tc_ref, td_ref), tt_ref)
    inner = [decays(st_ref, zz) for zz in range(4)]
    outer = [decays(tt_ref, yy) for yy in range(4)]
    for i in range(GH):
        carry = jnp.zeros((HP, N), F32)
        for yy in (3, 2, 1):
            carry = jnp.where(yy > y, sums_of(tt_ref, yy, i) + outer[yy][i] * carry, carry)
        for zz in (3, 2, 1, 0):
            ct_ref[zz, i * HP : (i + 1) * HP, :] = carry.astype(BF)
            if zz:
                carry = sums_of(st_ref, zz, i) + inner[zz][i] * carry
    for k, ref in enumerate((g0_ref, g1_ref, g2_ref, g3_ref)):
        ref[...] = ct_ref[(z + k) & 3]


def local_kernel(proj_ref, dy_ref, cum_ref, cumt_ref, h0_ref, dout_ref, skip_ref, core_ref,
                 keep_ref, give_ref, dx_ref, tx_ref, bt_ref, dbt_ref, dct_ref, extra_ref, y_ref, sdy_ref, h0t_ref, sum_ref):
    proj_t = jnp.transpose(proj_ref[...])
    bt = proj_t[INNER : INNER + N, :]
    ct = proj_t[INNER + N :, :]
    b_nat = proj_ref[:, INNER : INNER + N]
    c_nat = proj_ref[:, INNER + N :]
    pair = (SC * DT) * dot(b_nat, c_nat, NT)
    r = lax.broadcasted_iota(jnp.int32, (N, N), 0)
    c = lax.broadcasted_iota(jnp.int32, (N, N), 1)
    causal = r <= c
    cum = cum_ref[...]
    cumt = cumt_ref[...]
    start = jnp.exp(cum)
    tail = DT * jnp.exp(cum[:, T - 1 : T] - cum)
    bt_ref[...] = bt
    h0t_ref[...] = h0_ref[...].astype(BF)
    y_ref[...] = dot(h0t_ref[...], ct)
    skip_sums = []
    a00 = jnp.zeros((N, N), F32)
    a01 = jnp.zeros((N, N), F32)
    a11 = jnp.zeros((N, N), F32)
    zero = jnp.zeros((N, N), BF)
    zrow = jnp.zeros((HP, T), BF)
    for h in range(H):
        lo, hi = h * HP, (h + 1) * HP
        row0, row1 = cum[h : h + 1, :N], cum[h : h + 1, N:]
        col0, col1 = cumt[:N, h : h + 1], cumt[N:, h : h + 1]
        m00 = jnp.exp(jnp.where(causal, row0 - col0, -1e30))
        m01 = jnp.exp(row1 - col0)
        m11 = jnp.exp(jnp.where(causal, row1 - col1, -1e30))
        weights = jnp.concatenate(
            [
                jnp.concatenate([(m00 * pair[:N, :N]).astype(BF), (m01 * pair[:N, N:]).astype(BF)], axis=1),
                jnp.concatenate([zero, (m11 * pair[N:, N:]).astype(BF)], axis=1),
            ],
            axis=0,
        )
        x_h = proj_t[lo:hi, :]
        dy_h = dy_ref[lo:hi, :]
        x_f, dy_f = x_h.astype(F32), dy_h.astype(F32)
        st = start[h : h + 1, :]
        skip = skip_ref[h]
        y_ref[lo:hi, :] = dot(x_h, weights) + SC * st * y_ref[lo:hi, :] + skip * x_f
        dx_ref[lo:hi, :] = dot(dy_h, weights, NT) + skip * dy_f
        sdy_ref[lo:hi, :] = (st * dy_f).astype(BF)
        tx_ref[lo:hi, :] = (tail[h : h + 1, :] * x_f).astype(BF)
        x_pair = proj_ref[:, (h // 2) * N : (h // 2 + 1) * N]
        dy_z = jnp.concatenate([dy_h, zrow] if h % 2 == 0 else [zrow, dy_h], axis=0)
        q0 = dot(x_pair[:N, :], dy_z)
        q11 = dot(x_pair[N:, :], dy_z[:, N:])
        a00 += m00 * q0[:, :N]
        a01 += m01 * q0[:, N:]
        a11 += m11 * q11
        skip_sums.append(jnp.sum(x_f * dy_f, keepdims=True))
    core = core_ref[0]
    half = INNER // 2
    mine = pl.ds(pl.multiple_of(core * half, half), half)
    other = pl.ds(pl.multiple_of((1 - core) * half, half), half)
    give_ref[...] = dot(y_ref[other, :].astype(BF), dout_ref[...]).astype(BF)
    keep_ref[...] = dot(y_ref[mine, :].astype(BF), dout_ref[...])
    sum_ref[:N, :N] = a00.astype(BF)
    sum_ref[:N, N:] = a01.astype(BF)
    sum_ref[N:, :N] = zero
    sum_ref[N:, N:] = a11.astype(BF)
    a = sum_ref[...]
    dct_ref[...] = (SC * (DT * dot(bt, a) + dot(h0t_ref[...], sdy_ref[...], TN))).astype(BF)
    dbt_ref[...] = (DT * SC) * dot(ct, a, NT)
    lane = lax.broadcasted_iota(jnp.int32, (1, T), 1)
    extra = jnp.zeros((1, T), F32)
    for h in range(H):
        whole = skip_sums[h]
        top = whole.astype(BF).astype(F32)
        extra = extra + jnp.where(lane == 128 + h, top, 0.0) + jnp.where(lane == 160 + h, whole - top, 0.0)
    extra_ref[...] = extra


def slot_kernel(index_ref, extra_ref, misc_ref, hits_ref):
    index = index_ref[...]
    owner_row = lax.shift_right_logical(index, 9)
    rr = lax.broadcasted_iota(jnp.int32, (T, T), 0)
    cc = lax.broadcasted_iota(jnp.int32, (T, T), 1)
    index_col = jnp.sum(jnp.where(rr == cc, index.astype(F32), 0.0), axis=1, keepdims=True)
    index_col = index_col.astype(jnp.int32)
    owner_col = lax.shift_right_logical(index_col, 9)
    same = owner_col == owner_row
    rank_row = jnp.sum(jnp.where(same & (rr < cc), 1.0, 0.0), axis=0, keepdims=True).astype(jnp.int32)
    rank_col = jnp.sum(jnp.where(same & (cc < rr), 1.0, 0.0), axis=1, keepdims=True).astype(jnp.int32)
    local_col = index_col - owner_col * ROWS_DEV
    id_hi = lax.shift_right_logical(local_col, 1)
    id_lo = local_col - 2 * id_hi
    v = jnp.where(cc == rank_col, id_hi, jnp.where(cc == rank_col + 64, id_lo, 0))
    row_id = lax.broadcasted_iota(jnp.int32, (8 * DEV, T), 0)
    hits_ref[...] = jnp.where(row_id == owner_row * 8 + 2 + rank_row, 1.0, 0.0).astype(BF)
    heads = jnp.where(row_id == owner_row * 8 + 6, 1.0, 0.0).astype(BF)
    misc = dot(heads, v.astype(F32).astype(BF))
    misc_ref[...] = (misc + jnp.where((row_id & 7) == 6, extra_ref[...], 0.0)).astype(BF)


def finish_kernel(z_ref, c0_ref, c1_ref, c2_ref, c3_ref, outer_ref, bt_hbm, cum_hbm, dx_hbm, tx_hbm, dbt_hbm, dct_hbm, rows_hbm,
                  w_in_hbm, w_up_hbm, hits_hbm, misc_hbm, out_hbm,
                  carry_ref, bt_ref, cum_ref, dx_ref, tx_ref, dbt_ref, d_ref, rows_ref,
                  w_in_ref, w_up_ref, hits_ref, misc_ref, left_ref, right_ref, sems):
    copies = [
        pltpu.make_async_copy(a, b, sems.at[n])
        for n, (a, b) in enumerate((
            (bt_hbm, bt_ref), (cum_hbm, cum_ref), (dx_hbm, dx_ref), (tx_hbm, tx_ref),
            (dbt_hbm, dbt_ref), (dct_hbm, d_ref.at[INNER + N :, :]), (rows_hbm, rows_ref),
            (w_in_hbm, w_in_ref), (w_up_hbm, w_up_ref), (hits_hbm, hits_ref), (misc_hbm, misc_ref),
        ))
    ]
    for copy in copies:
        copy.start()
    outs = [pltpu.make_async_copy(outer_ref, out_hbm.at[:, 2 * E :], sems.at[11])]
    outs[0].start()
    for k, ref in enumerate((c0_ref, c1_ref, c2_ref, c3_ref)):
        carry_ref[pl.ds(pl.multiple_of(((z_ref[0] + 4 - k) & 3) * GR, GR), GR), :] = ref[...]
    for copy in copies[:2]:
        copy.wait()
    cum = cum_ref[...]
    tail = DT * jnp.exp(cum[:, T - 1 : T] - cum)
    carry = carry_ref[...]
    entering = dot(carry, bt_ref[...])
    copies[2].wait()
    for h in range(H):
        lo, hi = h * HP, (h + 1) * HP
        d_ref[lo:hi, :] = (dx_ref[lo:hi, :] + tail[h : h + 1, :] * entering[lo:hi, :]).astype(BF)
    for copy in copies[3:7]:
        copy.wait()
    d_ref[INNER : INNER + N, :] = (dbt_ref[...] + dot(carry, tx_ref[...], TN)).astype(BF)
    d = d_ref[...]
    g = dot(d, rows_ref[...]).astype(BF)
    left_ref[...] = g[:INNER, :]
    outs.append(pltpu.make_async_copy(left_ref, out_hbm.at[:, :E], sems.at[12]))
    outs[1].start()
    copies[7].wait()
    du = dot(w_in_ref[...], d).astype(BF)
    copies[8].wait()
    de = dot(w_up_ref[...], du).astype(BF)
    r = lax.broadcasted_iota(jnp.int32, (8 * DEV, 2 * N), 0)
    j = lax.broadcasted_iota(jnp.int32, (1, 2 * N), 1)
    place = jnp.where(r == 8 * lax.shift_right_logical(j, 1) + (j & 1), 1.0, 0.0).astype(BF)
    for copy in copies[9:]:
        copy.wait()
    misc = misc_ref[...].astype(F32) + dot(hits_ref[...], de, NT) + dot(place, g[INNER:, :])
    right_ref[...] = misc.astype(BF)
    outs.append(pltpu.make_async_copy(right_ref, out_hbm.at[:, E : 2 * E], sems.at[13]))
    outs[2].start()
    for copy in outs:
        copy.wait()


def pair_kernel(keep_ref, got_ref, out_ref):
    total = (keep_ref[...] + got_ref[...].astype(F32)).astype(BF)
    out_ref[: INNER // 2, :] = total[:, :E]
    out_ref[INNER // 2 :, :] = total[:, E:]


def sum_kernel(got_ref, chunk_ref, skip_ref):
    total = jnp.sum(got_ref[:, :, : 2 * E].astype(F32), axis=0)
    side = jnp.concatenate([total[0:2, E : E + N], total[0:2, E + N :], jnp.zeros((4, N), F32)], axis=0)
    outer = got_ref[:, :, 2 * E :].reshape(4, 2, CTX, 8, E)
    halves = [jnp.sum(outer[:, c].reshape(DEV // 2, 8, E).astype(F32), axis=0) for c in range(2)]
    chunk = jnp.concatenate([total[:, :E], side] + halves, axis=1)
    chunk_ref[...] = jnp.broadcast_to(chunk[None], chunk_ref.shape).astype(BF)
    skip_ref[...] = total[6:7, E + 128 : E + 256]


def table_kernel(got_ref, table_ref):
    misc = got_ref[:, :, E : 2 * E]
    ids = misc[:, 6:7, 0:128].astype(F32)
    sub = lax.broadcasted_iota(jnp.int32, (DEV, 8, 128), 1) - 2
    lane = lax.broadcasted_iota(jnp.int32, (DEV, 8, 128), 2)
    want = jnp.where(lane == sub, 2.0, jnp.where(lane == sub + 64, 1.0, 0.0))
    row = jnp.sum(ids * want, axis=2, keepdims=True)
    row = jnp.where((sub[:, :, :1] >= 0) & (sub[:, :, :1] < CAP), row, -1.0)
    rid = lax.broadcasted_iota(jnp.int32, (DEV, 8, ROWS_DEV), 2).astype(F32)
    hits = jnp.where(rid == row, 1.0, 0.0).reshape(DEV * 8, ROWS_DEV).astype(BF)
    table_ref[...] = dot(hits, misc.reshape(DEV * 8, E), TN)


def last_kernel(core_ref, own_ref, other_ref, w_up_ref, w_in_ref, up_ref, in_ref, go_ref, g_ref, side_ref):
    step = pl.program_id(0)
    core = core_ref[0]
    sources = ((core, own_ref), (1 - core, other_ref))

    @pl.when(step == 0)
    def _():
        for x in range(4):
            for at, ref in sources:
                rows = pl.ds(pl.multiple_of((2 * x + at) * N, N), N)
                g_ref[rows, :] = ref[x * N : (x + 1) * N, :E]
                side_ref[rows, :] = ref[x * N : (x + 1) * N, E : E + N]
        j = lax.broadcasted_iota(jnp.int32, (2 * N, 8 * DEV), 0)
        r = lax.broadcasted_iota(jnp.int32, (2 * N, 8 * DEV), 1)
        first = r - (8 * lax.shift_right_logical(j, 1) + (j & 1))
        for m in range(2):
            pick = jnp.where(first == 2 * m, 1.0, 0.0).astype(BF)
            g_ref[INNER:, m * N : (m + 1) * N] = dot(pick, side_ref[...]).astype(BF)

    g = g_ref[...]
    in_ref[...] = lax.dot_general(w_up_ref[...], g, (((0,), (1,)), ((), ())), preferred_element_type=F32)
    up_ref[...] = jnp.transpose(dot(w_in_ref[...], g))
    lanes = pl.ds(pl.multiple_of(E + N + E * lax.shift_right_logical(step, 1), N), E)
    for m in range(2):
        rows = pl.ds(pl.multiple_of((2 * m + (step & 1)) * N, N), N)
        for at, ref in sources:
            go_ref[pl.ds(pl.multiple_of(at * N, N), N), m * E : (m + 1) * E] = ref[rows, lanes].astype(F32)


def hop(value, axis, step):
    return lax.ppermute(value, axis, [(i, (i + step) % 4) for i in range(4)])


def local(event_rows, event_index, decay, saved_state, dout, w_up, w_in, w_out, skip):
    every = ("x", "core", "y", "z")
    rows, d_out = event_rows[0], dout[0]
    core, y, z = (lax.axis_index(a).reshape(1) for a in ("core", "y", "z"))
    proj, dy, cum, cumt, *sums = call(
        project_kernel,
        [((T, PROJ), BF), ((INNER, T), BF), ((H, T), F32), ((T, H), F32)] + [((MR, N), BF)] * 4,
        BIG, 750_000_000, 4_500_000,
        in_specs=[SM] + [HBM] * 6, out_specs=(VM,) * 8,
        scratch_shapes=[
            pltpu.VMEM((T, E), BF), pltpu.VMEM((T, D), BF), pltpu.VMEM((H, T), F32),
            pltpu.VMEM((E, D), BF), pltpu.VMEM((D, PROJ), BF), pltpu.VMEM((INNER, D), BF),
            pltpu.VMEM((4, MR, N), BF), pltpu.SemaphoreType.DMA((6,)),
        ],
    )(z, rows, d_out, decay[0], w_up, w_in, w_out)
    sums = sums[:1] + [hop(v, "z", k + 1) for k, v in enumerate(sums[1:])]
    keep, give, dx, tx, bt, dbt, dct, extra = call(
        local_kernel,
        [((INNER // 2, D), F32), ((INNER // 2, D), BF), ((INNER, T), F32), ((INNER, T), BF), ((N, T), BF),
         ((N, T), F32), ((N, T), BF), ((1, T), F32)],
        BIG, 2_500_000_000, 6_000_000,
        in_specs=[VM] * 6 + [SM] * 2, out_specs=(VM,) * 8,
        scratch_shapes=[
            pltpu.VMEM((INNER, T), F32), pltpu.VMEM((INNER, T), BF),
            pltpu.VMEM((INNER, N), BF), pltpu.VMEM((T, T), BF),
        ],
    )(proj, dy, cum, cumt, jnp.swapaxes(saved_state[0, 0], 1, 2).reshape(INNER, N), d_out, skip, core)
    sums, give = lax.optimization_barrier((sums, give))
    (total,) = call(
        inner_kernel, [((MR, N), BF)], 8, 2_000_000, 400_000,
        in_specs=[SM] + [VM] * 4, out_specs=(VM,), scratch_shapes=[pltpu.VMEM((4, MR, N), BF)],
    )(z, *sums)
    totals = [total] + [hop(total, "y", k) for k in range(1, 4)]
    misc, hits = call(
        slot_kernel, [((8 * DEV, E), BF), ((8 * DEV, T), BF)], BIG, 300_000_000, 1_500_000,
        in_specs=[VM] * 2, out_specs=(VM,) * 2,
    )(event_index, extra)
    totals, hits = lax.optimization_barrier((totals, hits))
    carries = call(
        outer_kernel, [((GR, N), BF)] * 4, 8, 4_000_000, 800_000,
        in_specs=[SM] * 2 + [VM] * 8, out_specs=(VM,) * 4,
        scratch_shapes=[pltpu.VMEM((4, MR, N), BF)] * 2 + [pltpu.VMEM((4, GR, N), BF)],
    )(y, z, *sums, *totals)
    carries = [carries[0]] + [hop(v, "z", k + 1) for k, v in enumerate(carries[1:])]
    (outer,) = call(
        pair_kernel, [((8 * DEV, E), BF)], 8, 300_000, 2_000_000, in_specs=[VM] * 2, out_specs=(VM,)
    )(keep, lax.ppermute(give, "core", [(0, 1), (1, 0)]))
    carries, outer = lax.optimization_barrier((carries, outer))
    (pay,) = call(
        finish_kernel, [((8 * DEV, 3 * E), BF)], 52, 1_400_000_000, 6_000_000,
        in_specs=[SM] + [VM] * 5 + [HBM] * 11, out_specs=(HBM,),
        scratch_shapes=[
            pltpu.VMEM((INNER, N), BF), pltpu.VMEM((N, T), BF), pltpu.VMEM((H, T), F32),
            pltpu.VMEM((INNER, T), F32), pltpu.VMEM((INNER, T), BF), pltpu.VMEM((N, T), F32),
            pltpu.VMEM((PROJ, T), BF), pltpu.VMEM((T, E), BF), pltpu.VMEM((D, PROJ), BF), pltpu.VMEM((E, D), BF),
            pltpu.VMEM((8 * DEV, T), BF), pltpu.VMEM((8 * DEV, E), BF),
            pltpu.VMEM((INNER, E), BF), pltpu.VMEM((8 * DEV, E), BF), pltpu.SemaphoreType.DMA((14,)),
        ],
    )(z, *carries, outer, bt, cum, dx, tx, dbt, dct, rows, w_in, w_up, hits, misc)
    pay_got = lax.all_to_all(pay.reshape(DEV, 8, 3 * E), every, 0, 0, tiled=True)
    chunk, skip_sum = call(
        sum_kernel, [((DEV // 2, 8, 7 * N), BF), ((1, 128), F32)], 12, 2_000_000, 3_000_000,
        in_specs=[VM], out_specs=(VM,) * 2,
    )(pay_got)
    whole = lax.all_to_all(chunk, ("x", "y", "z"), 0, 0, tiled=True).reshape(DEV * 4, 7 * N)
    other = lax.ppermute(whole, "core", [(0, 1), (1, 0)])
    (table,) = call(
        table_kernel, [((ROWS_DEV, E), F32)], 12, 400_000_000, 2_000_000, in_specs=[VM], out_specs=(VM,)
    )(pay_got)
    full = pl.BlockSpec((DEV * 4, 7 * N), lambda i: (0, 0))
    column = pl.BlockSpec((E, D // 4), lambda i: (0, i))
    row = pl.BlockSpec((D // 4, PROJ), lambda i: (i, 0))
    grad_up, grad_in, grad_out = pl.pallas_call(
        last_kernel,
        grid=(4,),
        out_shape=tuple(jax.ShapeDtypeStruct(s, F32) for s in ((E, D), (D, PROJ), (INNER, D))),
        in_specs=[SM, full, full, column, row],
        out_specs=(column, row, pl.BlockSpec((INNER // 4, D), lambda i: (i, 0))),
        scratch_shapes=[pltpu.VMEM((PROJ, E), BF), pltpu.VMEM((8 * DEV, N), BF)],
        compiler_params=pltpu.CompilerParams(vmem_limit_bytes=24 * MB),
        cost_estimate=pl.CostEstimate(flops=700_000_000, bytes_accessed=8_000_000, transcendentals=0),
    )(core, whole, other, w_up, w_in)
    grad_skip = skip_sum[0, :H] + skip_sum[0, 32 : 32 + H]
    return (grad_up, grad_in, grad_out, grad_skip, table)


def solution(mesh):
    mesh = Mesh(mesh.devices.reshape(4, 2, 4, 4), ("x", "core", "y", "z"))
    batch, ctx = ("x", "core"), ("y", "z")
    in_specs = (
        P(batch, ctx, None),
        P(batch, ctx),
        P(batch, None, ctx),
        P(batch, ctx, None, None, None),
        P(batch, ctx, None),
        P(),
        P(),
        P(),
        P(),
    )
    out_specs = (P(), P(), P(), P(), P(batch + ctx, None))
    return jax.shard_map(local, mesh=mesh, in_specs=in_specs, out_specs=out_specs, check_vma=False)
```

```python
from functools import partial

import jax
import jax.numpy as jnp
from jax import lax
from jax.experimental import pallas as pl
from jax.experimental.pallas import tpu as pltpu
from jax.sharding import Mesh, PartitionSpec as P

T = 256
E = 256
D = 512
H = 16
HP = 64
N = 128
INNER = H * HP
PROJ = INNER + 2 * N
ROWS_DEV = 512
CAP = 4
DEV = 128
CTX = 16
GH = 4
GR = GH * HP
MR = GR + 16

DT = 0.0625
SC = 128.0**-0.5
F32 = jnp.float32
BF = jnp.bfloat16
NN = (((1,), (0,)), ((), ()))
NT = (((1,), (1,)), ((), ()))
TN = (((0,), (0,)), ((), ()))
MB = 1 << 20
BIG = 60


def dot(a, b, dims=NN):
    return lax.dot_general(a, b, dims, preferred_element_type=F32)


def split3(v):
    hi = v.astype(BF)
    rest = v - hi.astype(F32)
    mid = rest.astype(BF)
    return hi, mid, (rest - mid.astype(F32)).astype(BF)


def call(kernel, outs, vmem, flops, nbytes, **kw):
    return pl.pallas_call(
        kernel,
        out_shape=tuple(jax.ShapeDtypeStruct(s, d) for s, d in outs),
        compiler_params=pltpu.CompilerParams(vmem_limit_bytes=vmem * MB),
        cost_estimate=pl.CostEstimate(flops=flops, bytes_accessed=nbytes, transcendentals=0),
        **kw,
    )


VM = pl.BlockSpec(memory_space=pltpu.VMEM)
HBM = pl.BlockSpec(memory_space=pltpu.HBM)
SM = pl.BlockSpec(memory_space=pltpu.SMEM)


def decay_rows(amounts):
    row = lax.broadcasted_iota(jnp.int32, (MR - GR, N), 0)
    out = jnp.zeros((MR - GR, N), F32)
    for i, amount in enumerate(amounts):
        for k, part in enumerate(split3(amount)):
            out = jnp.where(row == 3 * i + k, part.astype(F32), out)
    return out.astype(BF)


def decays(ref, at):
    rows = ref[at, GR:, :].astype(F32)
    return [rows[3 * i : 3 * i + 1] + rows[3 * i + 1 : 3 * i + 2] + rows[3 * i + 2 : 3 * i + 3] for i in range(GH)]


def sums_of(ref, at, i):
    return ref[at, i * HP : (i + 1) * HP, :].astype(F32)


def project_kernel(z_ref, rows_hbm, dout_hbm, decay_hbm, w_up_hbm, w_in_hbm, w_out_hbm,
                   proj_hbm, dy_hbm, cum_ref, cumt_ref, g0_ref, g1_ref, g2_ref, g3_ref,
                   rows_ref, dout_ref, decay_ref, w_up_ref, w_in_ref, w_out_ref, proj_ref, dy_ref, all_ref, sems):
    pairs = (
        (rows_hbm, rows_ref), (w_up_hbm, w_up_ref), (w_in_hbm, w_in_ref),
        (dout_hbm, dout_ref), (w_out_hbm, w_out_ref), (decay_hbm, decay_ref),
    )
    copies = [pltpu.make_async_copy(a, b, sems.at[i]) for i, (a, b) in enumerate(pairs)]
    for copy in copies:
        copy.start()
    copies[0].wait()
    copies[1].wait()
    u = dot(rows_ref[...], w_up_ref[...]).astype(BF)
    copies[2].wait()
    proj_ref[...] = dot(u, w_in_ref[...]).astype(BF)
    outs = [pltpu.make_async_copy(proj_ref, proj_hbm, sems.at[6])]
    outs[0].start()
    copies[3].wait()
    copies[4].wait()
    dy_ref[...] = dot(w_out_ref[...], dout_ref[...], NT).astype(BF)
    outs.append(pltpu.make_async_copy(dy_ref, dy_hbm, sems.at[7]))
    outs[1].start()
    copies[5].wait()
    logs = split3(jnp.log(decay_ref[...]))
    r = lax.broadcasted_iota(jnp.int32, (T, T), 0)
    c = lax.broadcasted_iota(jnp.int32, (T, T), 1)
    upper = (r <= c).astype(F32).astype(BF)
    lower = (c <= r).astype(F32).astype(BF)
    cum = sum(dot(p, upper) for p in logs)
    cum_ref[...] = cum
    cumt_ref[...] = sum(dot(lower, p, NT) for p in logs)
    start = jnp.exp(cum)
    c_nat = proj_ref[:, INNER + N :]
    scaled = jnp.concatenate(
        [
            (dy_ref[h * HP : (h + 1) * HP, :].astype(F32) * (SC * start[h : h + 1, :])).astype(BF)
            for h in range(H)
        ],
        axis=0,
    )
    sums = dot(scaled, c_nat).astype(BF)
    amount = jnp.exp(cum[:, T - 1 : T])
    for q in range(H // GH):
        all_ref[q, :GR, :] = sums[q * GR : (q + 1) * GR, :]
        all_ref[q, GR:, :] = decay_rows([jnp.broadcast_to(amount[h : h + 1, :], (1, N)) for h in range(q * GH, (q + 1) * GH)])
    for k, ref in enumerate((g0_ref, g1_ref, g2_ref, g3_ref)):
        ref[...] = all_ref[(z_ref[0] + k) & 3]
    for copy in outs:
        copy.wait()


def place(at, refs, out_ref):
    for k, ref in enumerate(refs):
        out_ref[(at + 4 - k) & 3] = ref[...]


def inner_kernel(z_ref, a_ref, b_ref, c_ref, d_ref, out_ref, st_ref):
    place(z_ref[0], (a_ref, b_ref, c_ref, d_ref), st_ref)
    amounts = [decays(st_ref, zz) for zz in range(4)]
    for i in range(GH):
        carry = sums_of(st_ref, 3, i)
        for zz in (2, 1, 0):
            carry = sums_of(st_ref, zz, i) + amounts[zz][i] * carry
        out_ref[i * HP : (i + 1) * HP, :] = carry.astype(BF)
    out_ref[GR:, :] = decay_rows([amounts[0][i] * amounts[1][i] * amounts[2][i] * amounts[3][i] for i in range(GH)])


def outer_kernel(y_ref, z_ref, a_ref, b_ref, c_ref, d_ref, ta_ref, tb_ref, tc_ref, td_ref,
                 g0_ref, g1_ref, g2_ref, g3_ref, st_ref, tt_ref, ct_ref):
    y, z = y_ref[0], z_ref[0]
    place(z, (a_ref, b_ref, c_ref, d_ref), st_ref)
    place(y, (ta_ref, tb_ref, tc_ref, td_ref), tt_ref)
    inner = [decays(st_ref, zz) for zz in range(4)]
    outer = [decays(tt_ref, yy) for yy in range(4)]
    for i in range(GH):
        carry = jnp.zeros((HP, N), F32)
        for yy in (3, 2, 1):
            carry = jnp.where(yy > y, sums_of(tt_ref, yy, i) + outer[yy][i] * carry, carry)
        for zz in (3, 2, 1, 0):
            ct_ref[zz, i * HP : (i + 1) * HP, :] = carry.astype(BF)
            if zz:
                carry = sums_of(st_ref, zz, i) + inner[zz][i] * carry
    for k, ref in enumerate((g0_ref, g1_ref, g2_ref, g3_ref)):
        ref[...] = ct_ref[(z + k) & 3]


def local_kernel(proj_hbm, dy_hbm, cum_ref, cumt_ref, h0_hbm, dout_hbm, skip_ref, core_ref,
                 keep_hbm, give_hbm, dx_hbm, tx_hbm, bt_ref, dbt_ref, dct_ref, extra_ref,
                 proj_ref, dy_ref, h0_ref, dout_ref, keep_ref, give_ref, dx_ref, tx_ref,
                 y_ref, sdy_ref, h0t_ref, sum_ref, sems):
    pairs = ((proj_hbm, proj_ref), (dy_hbm, dy_ref), (h0_hbm, h0_ref), (dout_hbm, dout_ref))
    copies = [pltpu.make_async_copy(a, b, sems.at[i]) for i, (a, b) in enumerate(pairs)]
    for copy in copies:
        copy.start()
    copies[0].wait()
    proj_t = jnp.transpose(proj_ref[...])
    bt = proj_t[INNER : INNER + N, :]
    ct = proj_t[INNER + N :, :]
    b_nat = proj_ref[:, INNER : INNER + N]
    c_nat = proj_ref[:, INNER + N :]
    pair = (SC * DT) * dot(b_nat, c_nat, NT)
    r = lax.broadcasted_iota(jnp.int32, (N, N), 0)
    c = lax.broadcasted_iota(jnp.int32, (N, N), 1)
    causal = r <= c
    cum = cum_ref[...]
    cumt = cumt_ref[...]
    start = jnp.exp(cum)
    tail = DT * jnp.exp(cum[:, T - 1 : T] - cum)
    bt_ref[...] = bt
    copies[1].wait()
    copies[2].wait()
    h0t_ref[...] = h0_ref[...].astype(BF)
    y_ref[...] = dot(h0t_ref[...], ct)
    skip_sums = []
    a00 = jnp.zeros((N, N), F32)
    a01 = jnp.zeros((N, N), F32)
    a11 = jnp.zeros((N, N), F32)
    zero = jnp.zeros((N, N), BF)
    zrow = jnp.zeros((HP, T), BF)
    for h in range(H):
        lo, hi = h * HP, (h + 1) * HP
        row0, row1 = cum[h : h + 1, :N], cum[h : h + 1, N:]
        col0, col1 = cumt[:N, h : h + 1], cumt[N:, h : h + 1]
        m00 = jnp.exp(jnp.where(causal, row0 - col0, -1e30))
        m01 = jnp.exp(row1 - col0)
        m11 = jnp.exp(jnp.where(causal, row1 - col1, -1e30))
        weights = jnp.concatenate(
            [
                jnp.concatenate([(m00 * pair[:N, :N]).astype(BF), (m01 * pair[:N, N:]).astype(BF)], axis=1),
                jnp.concatenate([zero, (m11 * pair[N:, N:]).astype(BF)], axis=1),
            ],
            axis=0,
        )
        x_h = proj_t[lo:hi, :]
        dy_h = dy_ref[lo:hi, :]
        x_f, dy_f = x_h.astype(F32), dy_h.astype(F32)
        st = start[h : h + 1, :]
        skip = skip_ref[h]
        y_ref[lo:hi, :] = dot(x_h, weights) + SC * st * y_ref[lo:hi, :] + skip * x_f
        dx_ref[lo:hi, :] = dot(dy_h, weights, NT) + skip * dy_f
        sdy_ref[lo:hi, :] = (st * dy_f).astype(BF)
        tx_ref[lo:hi, :] = (tail[h : h + 1, :] * x_f).astype(BF)
        x_pair = proj_ref[:, (h // 2) * N : (h // 2 + 1) * N]
        dy_z = jnp.concatenate([dy_h, zrow] if h % 2 == 0 else [zrow, dy_h], axis=0)
        q0 = dot(x_pair[:N, :], dy_z)
        q11 = dot(x_pair[N:, :], dy_z[:, N:])
        a00 += m00 * q0[:, :N]
        a01 += m01 * q0[:, N:]
        a11 += m11 * q11
        skip_sums.append(jnp.sum(x_f * dy_f, keepdims=True))
    pairs = ((dx_ref, dx_hbm), (tx_ref, tx_hbm), (give_ref, give_hbm), (keep_ref, keep_hbm))
    outs = [pltpu.make_async_copy(a, b, sems.at[4 + i]) for i, (a, b) in enumerate(pairs)]
    outs[0].start()
    outs[1].start()
    copies[3].wait()
    core = core_ref[0]
    half = INNER // 2
    mine = pl.ds(pl.multiple_of(core * half, half), half)
    other = pl.ds(pl.multiple_of((1 - core) * half, half), half)
    give_ref[...] = dot(y_ref[other, :].astype(BF), dout_ref[...]).astype(BF)
    outs[2].start()
    keep_ref[...] = dot(y_ref[mine, :].astype(BF), dout_ref[...])
    outs[3].start()
    sum_ref[:N, :N] = a00.astype(BF)
    sum_ref[:N, N:] = a01.astype(BF)
    sum_ref[N:, :N] = zero
    sum_ref[N:, N:] = a11.astype(BF)
    a = sum_ref[...]
    dct_ref[...] = (SC * (DT * dot(bt, a) + dot(h0t_ref[...], sdy_ref[...], TN))).astype(BF)
    dbt_ref[...] = (DT * SC) * dot(ct, a, NT)
    lane = lax.broadcasted_iota(jnp.int32, (1, T), 1)
    extra = jnp.zeros((1, T), F32)
    for h in range(H):
        whole = skip_sums[h]
        top = whole.astype(BF).astype(F32)
        extra = extra + jnp.where(lane == 128 + h, top, 0.0) + jnp.where(lane == 160 + h, whole - top, 0.0)
    extra_ref[...] = extra
    for copy in outs:
        copy.wait()


def slot_kernel(index_ref, extra_ref, misc_ref, hits_ref):
    index = index_ref[...]
    owner_row = lax.shift_right_logical(index, 9)
    rr = lax.broadcasted_iota(jnp.int32, (T, T), 0)
    cc = lax.broadcasted_iota(jnp.int32, (T, T), 1)
    index_col = jnp.sum(jnp.where(rr == cc, index.astype(F32), 0.0), axis=1, keepdims=True)
    index_col = index_col.astype(jnp.int32)
    owner_col = lax.shift_right_logical(index_col, 9)
    same = owner_col == owner_row
    rank_row = jnp.sum(jnp.where(same & (rr < cc), 1.0, 0.0), axis=0, keepdims=True).astype(jnp.int32)
    rank_col = jnp.sum(jnp.where(same & (cc < rr), 1.0, 0.0), axis=1, keepdims=True).astype(jnp.int32)
    local_col = index_col - owner_col * ROWS_DEV
    id_hi = lax.shift_right_logical(local_col, 1)
    id_lo = local_col - 2 * id_hi
    v = jnp.where(cc == rank_col, id_hi, jnp.where(cc == rank_col + 64, id_lo, 0))
    row_id = lax.broadcasted_iota(jnp.int32, (8 * DEV, T), 0)
    hits_ref[...] = jnp.where(row_id == owner_row * 8 + 2 + rank_row, 1.0, 0.0).astype(BF)
    heads = jnp.where(row_id == owner_row * 8 + 6, 1.0, 0.0).astype(BF)
    misc = dot(heads, v.astype(F32).astype(BF))
    misc_ref[...] = (misc + jnp.where((row_id & 7) == 6, extra_ref[...], 0.0)).astype(BF)


def finish_kernel(z_ref, c0_ref, c1_ref, c2_ref, c3_ref, outer_ref, bt_hbm, cum_hbm, dx_hbm, tx_hbm, dbt_hbm, dct_hbm, rows_hbm,
                  w_in_hbm, w_up_hbm, hits_hbm, misc_hbm, out_hbm,
                  carry_ref, bt_ref, cum_ref, dx_ref, tx_ref, dbt_ref, d_ref, rows_ref,
                  w_in_ref, w_up_ref, hits_ref, misc_ref, left_ref, right_ref, sems):
    copies = [
        pltpu.make_async_copy(a, b, sems.at[n])
        for n, (a, b) in enumerate((
            (bt_hbm, bt_ref), (cum_hbm, cum_ref), (dx_hbm, dx_ref), (tx_hbm, tx_ref),
            (dbt_hbm, dbt_ref), (dct_hbm, d_ref.at[INNER + N :, :]), (rows_hbm, rows_ref),
            (w_in_hbm, w_in_ref), (w_up_hbm, w_up_ref), (hits_hbm, hits_ref), (misc_hbm, misc_ref),
        ))
    ]
    for copy in copies:
        copy.start()
    outs = [pltpu.make_async_copy(outer_ref, out_hbm.at[:, 2 * E :], sems.at[11])]
    outs[0].start()
    for k, ref in enumerate((c0_ref, c1_ref, c2_ref, c3_ref)):
        carry_ref[pl.ds(pl.multiple_of(((z_ref[0] + 4 - k) & 3) * GR, GR), GR), :] = ref[...]
    for copy in copies[:2]:
        copy.wait()
    cum = cum_ref[...]
    tail = DT * jnp.exp(cum[:, T - 1 : T] - cum)
    carry = carry_ref[...]
    entering = dot(carry, bt_ref[...])
    copies[2].wait()
    for h in range(H):
        lo, hi = h * HP, (h + 1) * HP
        d_ref[lo:hi, :] = (dx_ref[lo:hi, :] + tail[h : h + 1, :] * entering[lo:hi, :]).astype(BF)
    for copy in copies[3:7]:
        copy.wait()
    d_ref[INNER : INNER + N, :] = (dbt_ref[...] + dot(carry, tx_ref[...], TN)).astype(BF)
    d = d_ref[...]
    g = dot(d, rows_ref[...]).astype(BF)
    left_ref[...] = g[:INNER, :]
    outs.append(pltpu.make_async_copy(left_ref, out_hbm.at[:, :E], sems.at[12]))
    outs[1].start()
    copies[7].wait()
    du = dot(w_in_ref[...], d).astype(BF)
    copies[8].wait()
    de = dot(w_up_ref[...], du).astype(BF)
    r = lax.broadcasted_iota(jnp.int32, (8 * DEV, 2 * N), 0)
    j = lax.broadcasted_iota(jnp.int32, (1, 2 * N), 1)
    place = jnp.where(r == 8 * lax.shift_right_logical(j, 1) + (j & 1), 1.0, 0.0).astype(BF)
    for copy in copies[9:]:
        copy.wait()
    misc = misc_ref[...].astype(F32) + dot(hits_ref[...], de, NT) + dot(place, g[INNER:, :])
    right_ref[...] = misc.astype(BF)
    outs.append(pltpu.make_async_copy(right_ref, out_hbm.at[:, E : 2 * E], sems.at[13]))
    outs[2].start()
    for copy in outs:
        copy.wait()


def pair_kernel(keep_ref, got_ref, out_ref):
    total = (keep_ref[...] + got_ref[...].astype(F32)).astype(BF)
    out_ref[: INNER // 2, :] = total[:, :E]
    out_ref[INNER // 2 :, :] = total[:, E:]


def sum_kernel(got_ref, chunk_ref, skip_ref):
    total = jnp.sum(got_ref[:, :, : 2 * E].astype(F32), axis=0)
    side = jnp.concatenate([total[0:2, E : E + N], total[0:2, E + N :], jnp.zeros((4, N), F32)], axis=0)
    outer = got_ref[:, :, 2 * E :].reshape(4, 2, CTX, 8, E)
    halves = [jnp.sum(outer[:, c].reshape(DEV // 2, 8, E).astype(F32), axis=0) for c in range(2)]
    chunk = jnp.concatenate([total[:, :E], side] + halves, axis=1)
    chunk_ref[...] = jnp.broadcast_to(chunk[None], chunk_ref.shape).astype(BF)
    skip_ref[...] = total[6:7, E + 128 : E + 256]


def table_kernel(got_ref, table_ref):
    misc = got_ref[:, :, E : 2 * E]
    ids = misc[:, 6:7, 0:128].astype(F32)
    sub = lax.broadcasted_iota(jnp.int32, (DEV, 8, 128), 1) - 2
    lane = lax.broadcasted_iota(jnp.int32, (DEV, 8, 128), 2)
    want = jnp.where(lane == sub, 2.0, jnp.where(lane == sub + 64, 1.0, 0.0))
    row = jnp.sum(ids * want, axis=2, keepdims=True)
    row = jnp.where((sub[:, :, :1] >= 0) & (sub[:, :, :1] < CAP), row, -1.0)
    rid = lax.broadcasted_iota(jnp.int32, (DEV, 8, ROWS_DEV), 2).astype(F32)
    hits = jnp.where(rid == row, 1.0, 0.0).reshape(DEV * 8, ROWS_DEV).astype(BF)
    table_ref[...] = dot(hits, misc.reshape(DEV * 8, E), TN)


def last_kernel(core_ref, own_ref, other_ref, w_up_ref, w_in_ref, up_ref, in_ref, go_ref, g_ref, side_ref):
    step = pl.program_id(0)
    core = core_ref[0]
    sources = ((core, own_ref), (1 - core, other_ref))

    @pl.when(step == 0)
    def _():
        for x in range(4):
            for at, ref in sources:
                rows = pl.ds(pl.multiple_of((2 * x + at) * N, N), N)
                g_ref[rows, :] = ref[x * N : (x + 1) * N, :E]
                side_ref[rows, :] = ref[x * N : (x + 1) * N, E : E + N]
        j = lax.broadcasted_iota(jnp.int32, (2 * N, 8 * DEV), 0)
        r = lax.broadcasted_iota(jnp.int32, (2 * N, 8 * DEV), 1)
        first = r - (8 * lax.shift_right_logical(j, 1) + (j & 1))
        for m in range(2):
            pick = jnp.where(first == 2 * m, 1.0, 0.0).astype(BF)
            g_ref[INNER:, m * N : (m + 1) * N] = dot(pick, side_ref[...]).astype(BF)

    g = g_ref[...]
    part = pl.ds(pl.multiple_of(step * N, N), N)
    in_ref[...] = lax.dot_general(w_up_ref[:, part], g, (((0,), (1,)), ((), ())), preferred_element_type=F32)
    up_ref[...] = jnp.transpose(dot(w_in_ref[part, :], g))
    lanes = pl.ds(pl.multiple_of(E + N + E * lax.shift_right_logical(step, 1), N), E)
    for m in range(2):
        rows = pl.ds(pl.multiple_of((2 * m + (step & 1)) * N, N), N)
        for at, ref in sources:
            go_ref[pl.ds(pl.multiple_of(at * N, N), N), m * E : (m + 1) * E] = ref[rows, lanes].astype(F32)


def hop(value, axis, step):
    return lax.ppermute(value, axis, [(i, (i + step) % 4) for i in range(4)])


def local(event_rows, event_index, decay, saved_state, dout, w_up, w_in, w_out, skip):
    every = ("x", "core", "y", "z")
    rows, d_out = event_rows[0], dout[0]
    core, y, z = (lax.axis_index(a).reshape(1) for a in ("core", "y", "z"))
    proj, dy, cum, cumt, *sums = call(
        project_kernel,
        [((T, PROJ), BF), ((INNER, T), BF), ((H, T), F32), ((T, H), F32)] + [((MR, N), BF)] * 4,
        BIG, 750_000_000, 4_500_000,
        in_specs=[SM] + [HBM] * 6, out_specs=(HBM,) * 2 + (VM,) * 6,
        scratch_shapes=[
            pltpu.VMEM((T, E), BF), pltpu.VMEM((T, D), BF), pltpu.VMEM((H, T), F32),
            pltpu.VMEM((E, D), BF), pltpu.VMEM((D, PROJ), BF), pltpu.VMEM((INNER, D), BF),
            pltpu.VMEM((T, PROJ), BF), pltpu.VMEM((INNER, T), BF),
            pltpu.VMEM((4, MR, N), BF), pltpu.SemaphoreType.DMA((8,)),
        ],
    )(z, rows, d_out, decay[0], w_up, w_in, w_out)
    sums = sums[:1] + [hop(v, "z", k + 1) for k, v in enumerate(sums[1:])]
    keep, give, dx, tx, bt, dbt, dct, extra = call(
        local_kernel,
        [((INNER // 2, D), F32), ((INNER // 2, D), BF), ((INNER, T), F32), ((INNER, T), BF), ((N, T), BF),
         ((N, T), F32), ((N, T), BF), ((1, T), F32)],
        BIG, 2_500_000_000, 6_000_000,
        in_specs=[HBM] * 2 + [VM] * 2 + [HBM] * 2 + [SM] * 2, out_specs=(HBM,) * 4 + (VM,) * 4,
        scratch_shapes=[
            pltpu.VMEM((T, PROJ), BF), pltpu.VMEM((INNER, T), BF), pltpu.VMEM((INNER, N), F32), pltpu.VMEM((T, D), BF),
            pltpu.VMEM((INNER // 2, D), F32), pltpu.VMEM((INNER // 2, D), BF),
            pltpu.VMEM((INNER, T), F32), pltpu.VMEM((INNER, T), BF),
            pltpu.VMEM((INNER, T), F32), pltpu.VMEM((INNER, T), BF),
            pltpu.VMEM((INNER, N), BF), pltpu.VMEM((T, T), BF), pltpu.SemaphoreType.DMA((8,)),
        ],
    )(proj, dy, cum, cumt, jnp.swapaxes(saved_state[0, 0], 1, 2).reshape(INNER, N), d_out, skip, core)
    sums, give = lax.optimization_barrier((sums, give))
    (total,) = call(
        inner_kernel, [((MR, N), BF)], 8, 2_000_000, 400_000,
        in_specs=[SM] + [VM] * 4, out_specs=(VM,), scratch_shapes=[pltpu.VMEM((4, MR, N), BF)],
    )(z, *sums)
    totals = [total] + [hop(total, "y", k) for k in range(1, 4)]
    misc, hits = call(
        slot_kernel, [((8 * DEV, E), BF), ((8 * DEV, T), BF)], BIG, 300_000_000, 1_500_000,
        in_specs=[VM] * 2, out_specs=(VM,) * 2,
    )(event_index, extra)
    totals, hits = lax.optimization_barrier((totals, hits))
    carries = call(
        outer_kernel, [((GR, N), BF)] * 4, 8, 4_000_000, 800_000,
        in_specs=[SM] * 2 + [VM] * 8, out_specs=(VM,) * 4,
        scratch_shapes=[pltpu.VMEM((4, MR, N), BF)] * 2 + [pltpu.VMEM((4, GR, N), BF)],
    )(y, z, *sums, *totals)
    carries = [carries[0]] + [hop(v, "z", k + 1) for k, v in enumerate(carries[1:])]
    (outer,) = call(
        pair_kernel, [((8 * DEV, E), BF)], 8, 300_000, 2_000_000, in_specs=[VM] * 2, out_specs=(VM,)
    )(keep, lax.ppermute(give, "core", [(0, 1), (1, 0)]))
    carries, outer = lax.optimization_barrier((carries, outer))
    (pay,) = call(
        finish_kernel, [((8 * DEV, 3 * E), BF)], 51, 1_400_000_000, 6_000_000,
        in_specs=[SM] + [VM] * 5 + [HBM] * 11, out_specs=(HBM,),
        scratch_shapes=[
            pltpu.VMEM((INNER, N), BF), pltpu.VMEM((N, T), BF), pltpu.VMEM((H, T), F32),
            pltpu.VMEM((INNER, T), F32), pltpu.VMEM((INNER, T), BF), pltpu.VMEM((N, T), F32),
            pltpu.VMEM((PROJ, T), BF), pltpu.VMEM((T, E), BF), pltpu.VMEM((D, PROJ), BF), pltpu.VMEM((E, D), BF),
            pltpu.VMEM((8 * DEV, T), BF), pltpu.VMEM((8 * DEV, E), BF),
            pltpu.VMEM((INNER, E), BF), pltpu.VMEM((8 * DEV, E), BF), pltpu.SemaphoreType.DMA((14,)),
        ],
    )(z, *carries, outer, bt, cum, dx, tx, dbt, dct, rows, w_in, w_up, hits, misc)
    pay_got = lax.all_to_all(pay.reshape(DEV, 8, 3 * E), every, 0, 0, tiled=True)
    chunk, skip_sum = call(
        sum_kernel, [((DEV // 2, 8, 7 * N), BF), ((1, 128), F32)], 12, 2_000_000, 3_000_000,
        in_specs=[VM], out_specs=(VM,) * 2,
    )(pay_got)
    whole = lax.all_to_all(chunk, ("x", "y", "z"), 0, 0, tiled=True).reshape(DEV * 4, 7 * N)
    other = lax.ppermute(whole, "core", [(0, 1), (1, 0)])
    (table,) = call(
        table_kernel, [((ROWS_DEV, E), F32)], 12, 400_000_000, 2_000_000, in_specs=[VM], out_specs=(VM,)
    )(pay_got)
    column = pl.BlockSpec((E, D // 4), lambda i: (0, i))
    row = pl.BlockSpec((D // 4, PROJ), lambda i: (i, 0))
    grad_up, grad_in, grad_out = pl.pallas_call(
        last_kernel,
        grid=(4,),
        out_shape=tuple(jax.ShapeDtypeStruct(s, F32) for s in ((E, D), (D, PROJ), (INNER, D))),
        in_specs=[SM] + [VM] * 4,
        out_specs=(column, row, pl.BlockSpec((INNER // 4, D), lambda i: (i, 0))),
        scratch_shapes=[pltpu.VMEM((PROJ, E), BF), pltpu.VMEM((8 * DEV, N), BF)],
        compiler_params=pltpu.CompilerParams(vmem_limit_bytes=24 * MB),
        cost_estimate=pl.CostEstimate(flops=700_000_000, bytes_accessed=8_000_000, transcendentals=0),
    )(core, whole, other, w_up, w_in)
    grad_skip = skip_sum[0, :H] + skip_sum[0, 32 : 32 + H]
    return (grad_up, grad_in, grad_out, grad_skip, table)


def solution(mesh):
    mesh = Mesh(mesh.devices.reshape(4, 2, 4, 4), ("x", "core", "y", "z"))
    batch, ctx = ("x", "core"), ("y", "z")
    in_specs = (
        P(batch, ctx, None),
        P(batch, ctx),
        P(batch, None, ctx),
        P(batch, ctx, None, None, None),
        P(batch, ctx, None),
        P(),
        P(),
        P(),
        P(),
    )
    out_specs = (P(), P(), P(), P(), P(batch + ctx, None))
    return jax.shard_map(local, mesh=mesh, in_specs=in_specs, out_specs=out_specs, check_vma=False)
```

```python
from functools import partial

import jax
import jax.numpy as jnp
from jax import lax
from jax.experimental import pallas as pl
from jax.experimental.pallas import tpu as pltpu
from jax.sharding import Mesh, PartitionSpec as P

T = 256
E = 256
D = 512
H = 16
HP = 64
N = 128
INNER = H * HP
PROJ = INNER + 2 * N
ROWS_DEV = 512
CAP = 4
DEV = 128
CTX = 16
GH = 4
GR = GH * HP
MR = GR + 16

DT = 0.0625
SC = 128.0**-0.5
F32 = jnp.float32
BF = jnp.bfloat16
NN = (((1,), (0,)), ((), ()))
NT = (((1,), (1,)), ((), ()))
TN = (((0,), (0,)), ((), ()))
MB = 1 << 20
BIG = 60


def dot(a, b, dims=NN):
    return lax.dot_general(a, b, dims, preferred_element_type=F32)


def split3(v):
    hi = v.astype(BF)
    rest = v - hi.astype(F32)
    mid = rest.astype(BF)
    return hi, mid, (rest - mid.astype(F32)).astype(BF)


def call(kernel, outs, vmem, flops, nbytes, **kw):
    return pl.pallas_call(
        kernel,
        out_shape=tuple(jax.ShapeDtypeStruct(s, d) for s, d in outs),
        compiler_params=pltpu.CompilerParams(vmem_limit_bytes=vmem * MB),
        cost_estimate=pl.CostEstimate(flops=flops, bytes_accessed=nbytes, transcendentals=0),
        **kw,
    )


VM = pl.BlockSpec(memory_space=pltpu.VMEM)
HBM = pl.BlockSpec(memory_space=pltpu.HBM)
SM = pl.BlockSpec(memory_space=pltpu.SMEM)


def decay_rows(amounts):
    row = lax.broadcasted_iota(jnp.int32, (MR - GR, N), 0)
    out = jnp.zeros((MR - GR, N), F32)
    for i, amount in enumerate(amounts):
        for k, part in enumerate(split3(amount)):
            out = jnp.where(row == 3 * i + k, part.astype(F32), out)
    return out.astype(BF)


def decays(ref, at):
    rows = ref[at, GR:, :].astype(F32)
    return [rows[3 * i : 3 * i + 1] + rows[3 * i + 1 : 3 * i + 2] + rows[3 * i + 2 : 3 * i + 3] for i in range(GH)]


def sums_of(ref, at, i):
    return ref[at, i * HP : (i + 1) * HP, :].astype(F32)


def project_kernel(z_ref, rows_hbm, dout_hbm, decay_hbm, w_up_hbm, w_in_hbm, w_out_hbm,
                   proj_ref, dy_ref, cum_ref, cumt_ref, g0_ref, g1_ref, g2_ref, g3_ref,
                   rows_ref, dout_ref, decay_ref, w_up_ref, w_in_ref, w_out_ref, all_ref, sems):
    pairs = (
        (rows_hbm, rows_ref), (w_up_hbm, w_up_ref), (w_in_hbm, w_in_ref),
        (dout_hbm, dout_ref), (w_out_hbm, w_out_ref), (decay_hbm, decay_ref),
    )
    copies = [pltpu.make_async_copy(a, b, sems.at[i]) for i, (a, b) in enumerate(pairs)]
    for copy in copies:
        copy.start()
    copies[0].wait()
    copies[1].wait()
    u = dot(rows_ref[...], w_up_ref[...]).astype(BF)
    copies[2].wait()
    proj_ref[...] = dot(u, w_in_ref[...]).astype(BF)
    copies[3].wait()
    copies[4].wait()
    dy_ref[...] = dot(w_out_ref[...], dout_ref[...], NT).astype(BF)
    copies[5].wait()
    logs = split3(jnp.log(decay_ref[...]))
    r = lax.broadcasted_iota(jnp.int32, (T, T), 0)
    c = lax.broadcasted_iota(jnp.int32, (T, T), 1)
    upper = (r <= c).astype(F32).astype(BF)
    lower = (c <= r).astype(F32).astype(BF)
    cum = sum(dot(p, upper) for p in logs)
    cum_ref[...] = cum
    cumt_ref[...] = sum(dot(lower, p, NT) for p in logs)
    start = jnp.exp(cum)
    c_nat = proj_ref[:, INNER + N :]
    scaled = jnp.concatenate(
        [
            (dy_ref[h * HP : (h + 1) * HP, :].astype(F32) * (SC * start[h : h + 1, :])).astype(BF)
            for h in range(H)
        ],
        axis=0,
    )
    sums = dot(scaled, c_nat).astype(BF)
    amount = jnp.exp(cum[:, T - 1 : T])
    for q in range(H // GH):
        all_ref[q, :GR, :] = sums[q * GR : (q + 1) * GR, :]
        all_ref[q, GR:, :] = decay_rows([jnp.broadcast_to(amount[h : h + 1, :], (1, N)) for h in range(q * GH, (q + 1) * GH)])
    for k, ref in enumerate((g0_ref, g1_ref, g2_ref, g3_ref)):
        ref[...] = all_ref[(z_ref[0] + k) & 3]


def place(at, refs, out_ref):
    for k, ref in enumerate(refs):
        out_ref[(at + 4 - k) & 3] = ref[...]


def inner_kernel(z_ref, a_ref, b_ref, c_ref, d_ref, out_ref, st_ref):
    place(z_ref[0], (a_ref, b_ref, c_ref, d_ref), st_ref)
    amounts = [decays(st_ref, zz) for zz in range(4)]
    for i in range(GH):
        carry = sums_of(st_ref, 3, i)
        for zz in (2, 1, 0):
            carry = sums_of(st_ref, zz, i) + amounts[zz][i] * carry
        out_ref[i * HP : (i + 1) * HP, :] = carry.astype(BF)
    out_ref[GR:, :] = decay_rows([amounts[0][i] * amounts[1][i] * amounts[2][i] * amounts[3][i] for i in range(GH)])


def outer_kernel(y_ref, z_ref, a_ref, b_ref, c_ref, d_ref, ta_ref, tb_ref, tc_ref, td_ref,
                 g0_ref, g1_ref, g2_ref, g3_ref, st_ref, tt_ref, ct_ref):
    y, z = y_ref[0], z_ref[0]
    place(z, (a_ref, b_ref, c_ref, d_ref), st_ref)
    place(y, (ta_ref, tb_ref, tc_ref, td_ref), tt_ref)
    inner = [decays(st_ref, zz) for zz in range(4)]
    outer = [decays(tt_ref, yy) for yy in range(4)]
    for i in range(GH):
        carry = jnp.zeros((HP, N), F32)
        for yy in (3, 2, 1):
            carry = jnp.where(yy > y, sums_of(tt_ref, yy, i) + outer[yy][i] * carry, carry)
        for zz in (3, 2, 1, 0):
            ct_ref[zz, i * HP : (i + 1) * HP, :] = carry.astype(BF)
            if zz:
                carry = sums_of(st_ref, zz, i) + inner[zz][i] * carry
    for k, ref in enumerate((g0_ref, g1_ref, g2_ref, g3_ref)):
        ref[...] = ct_ref[(z + k) & 3]


def local_kernel(proj_ref, dy_ref, cum_ref, cumt_ref, h0_ref, dout_ref, skip_ref, core_ref,
                 keep_ref, give_ref, dx_ref, tx_ref, bt_ref, dbt_ref, dct_ref, extra_ref, y_ref, sdy_ref, h0t_ref, sum_ref):
    proj_t = jnp.transpose(proj_ref[...])
    bt = proj_t[INNER : INNER + N, :]
    ct = proj_t[INNER + N :, :]
    b_nat = proj_ref[:, INNER : INNER + N]
    c_nat = proj_ref[:, INNER + N :]
    pair = (SC * DT) * dot(b_nat, c_nat, NT)
    r = lax.broadcasted_iota(jnp.int32, (N, N), 0)
    c = lax.broadcasted_iota(jnp.int32, (N, N), 1)
    causal = r <= c
    cum = cum_ref[...]
    cumt = cumt_ref[...]
    start = jnp.exp(cum)
    tail = DT * jnp.exp(cum[:, T - 1 : T] - cum)
    bt_ref[...] = bt
    h0t_ref[...] = h0_ref[...].astype(BF)
    y_ref[...] = dot(h0t_ref[...], ct)
    skip_sums = []
    a00 = jnp.zeros((N, N), F32)
    a01 = jnp.zeros((N, N), F32)
    a11 = jnp.zeros((N, N), F32)
    zero = jnp.zeros((N, N), BF)
    zrow = jnp.zeros((HP, T), BF)
    for h in range(H):
        lo, hi = h * HP, (h + 1) * HP
        row0, row1 = cum[h : h + 1, :N], cum[h : h + 1, N:]
        col0, col1 = cumt[:N, h : h + 1], cumt[N:, h : h + 1]
        m00 = jnp.exp(jnp.where(causal, row0 - col0, -1e30))
        m01 = jnp.exp(row1 - col0)
        m11 = jnp.exp(jnp.where(causal, row1 - col1, -1e30))
        weights = jnp.concatenate(
            [
                jnp.concatenate([(m00 * pair[:N, :N]).astype(BF), (m01 * pair[:N, N:]).astype(BF)], axis=1),
                jnp.concatenate([zero, (m11 * pair[N:, N:]).astype(BF)], axis=1),
            ],
            axis=0,
        )
        x_h = proj_t[lo:hi, :]
        dy_h = dy_ref[lo:hi, :]
        x_f, dy_f = x_h.astype(F32), dy_h.astype(F32)
        st = start[h : h + 1, :]
        skip = skip_ref[h]
        y_ref[lo:hi, :] = dot(x_h, weights) + SC * st * y_ref[lo:hi, :] + skip * x_f
        dx_ref[lo:hi, :] = dot(dy_h, weights, NT) + skip * dy_f
        sdy_ref[lo:hi, :] = (st * dy_f).astype(BF)
        tx_ref[lo:hi, :] = (tail[h : h + 1, :] * x_f).astype(BF)
        x_pair = proj_ref[:, (h // 2) * N : (h // 2 + 1) * N]
        dy_z = jnp.concatenate([dy_h, zrow] if h % 2 == 0 else [zrow, dy_h], axis=0)
        q0 = dot(x_pair[:N, :], dy_z)
        q11 = dot(x_pair[N:, :], dy_z[:, N:])
        a00 += m00 * q0[:, :N]
        a01 += m01 * q0[:, N:]
        a11 += m11 * q11
        skip_sums.append(jnp.sum(x_f * dy_f, keepdims=True))
    core = core_ref[0]
    half = INNER // 2
    mine = pl.ds(pl.multiple_of(core * half, half), half)
    other = pl.ds(pl.multiple_of((1 - core) * half, half), half)
    give_ref[...] = dot(y_ref[other, :].astype(BF), dout_ref[...]).astype(BF)
    keep_ref[...] = dot(y_ref[mine, :].astype(BF), dout_ref[...])
    sum_ref[:N, :N] = a00.astype(BF)
    sum_ref[:N, N:] = a01.astype(BF)
    sum_ref[N:, :N] = zero
    sum_ref[N:, N:] = a11.astype(BF)
    a = sum_ref[...]
    dct_ref[...] = (SC * (DT * dot(bt, a) + dot(h0t_ref[...], sdy_ref[...], TN))).astype(BF)
    dbt_ref[...] = (DT * SC) * dot(ct, a, NT)
    lane = lax.broadcasted_iota(jnp.int32, (1, T), 1)
    extra = jnp.zeros((1, T), F32)
    for h in range(H):
        whole = skip_sums[h]
        top = whole.astype(BF).astype(F32)
        extra = extra + jnp.where(lane == 128 + h, top, 0.0) + jnp.where(lane == 160 + h, whole - top, 0.0)
    extra_ref[...] = extra


def slot_kernel(index_ref, extra_ref, misc_ref, hits_ref):
    index = index_ref[...]
    owner_row = lax.shift_right_logical(index, 9)
    rr = lax.broadcasted_iota(jnp.int32, (T, T), 0)
    cc = lax.broadcasted_iota(jnp.int32, (T, T), 1)
    index_col = jnp.sum(jnp.where(rr == cc, index.astype(F32), 0.0), axis=1, keepdims=True)
    index_col = index_col.astype(jnp.int32)
    owner_col = lax.shift_right_logical(index_col, 9)
    same = owner_col == owner_row
    rank_row = jnp.sum(jnp.where(same & (rr < cc), 1.0, 0.0), axis=0, keepdims=True).astype(jnp.int32)
    rank_col = jnp.sum(jnp.where(same & (cc < rr), 1.0, 0.0), axis=1, keepdims=True).astype(jnp.int32)
    local_col = index_col - owner_col * ROWS_DEV
    id_hi = lax.shift_right_logical(local_col, 1)
    id_lo = local_col - 2 * id_hi
    v = jnp.where(cc == rank_col, id_hi, jnp.where(cc == rank_col + 64, id_lo, 0))
    row_id = lax.broadcasted_iota(jnp.int32, (8 * DEV, T), 0)
    hits_ref[...] = jnp.where(row_id == owner_row * 8 + 2 + rank_row, 1.0, 0.0).astype(BF)
    heads = jnp.where(row_id == owner_row * 8 + 6, 1.0, 0.0).astype(BF)
    misc = dot(heads, v.astype(F32).astype(BF))
    misc_ref[...] = (misc + jnp.where((row_id & 7) == 6, extra_ref[...], 0.0)).astype(BF)


def finish_kernel(z_ref, c0_ref, c1_ref, c2_ref, c3_ref, outer_ref, bt_ref, cum_ref, tx_ref, dbt_ref, dct_ref,
                  rows_ref, w_up_ref, hits_ref, misc_ref, dx_ref, w_in_ref, out_ref, carry_ref, d_ref):
    out_ref[:, 2 * E :] = outer_ref[...]
    for k, ref in enumerate((c0_ref, c1_ref, c2_ref, c3_ref)):
        carry_ref[pl.ds(pl.multiple_of(((z_ref[0] + 4 - k) & 3) * GR, GR), GR), :] = ref[...]
    cum = cum_ref[...]
    tail = DT * jnp.exp(cum[:, T - 1 : T] - cum)
    carry = carry_ref[...]
    entering = dot(carry, bt_ref[...])
    for h in range(H):
        lo, hi = h * HP, (h + 1) * HP
        d_ref[lo:hi, :] = (dx_ref[lo:hi, :] + tail[h : h + 1, :] * entering[lo:hi, :]).astype(BF)
    d_ref[INNER + N :, :] = dct_ref[...]
    d_ref[INNER : INNER + N, :] = (dbt_ref[...] + dot(carry, tx_ref[...], TN)).astype(BF)
    d = d_ref[...]
    g = dot(d, rows_ref[...]).astype(BF)
    out_ref[:, :E] = g[:INNER, :]
    du = dot(w_in_ref[...], d).astype(BF)
    de = dot(w_up_ref[...], du).astype(BF)
    r = lax.broadcasted_iota(jnp.int32, (8 * DEV, 2 * N), 0)
    j = lax.broadcasted_iota(jnp.int32, (1, 2 * N), 1)
    place = jnp.where(r == 8 * lax.shift_right_logical(j, 1) + (j & 1), 1.0, 0.0).astype(BF)
    misc = misc_ref[...].astype(F32) + dot(hits_ref[...], de, NT) + dot(place, g[INNER:, :])
    out_ref[:, E : 2 * E] = misc.astype(BF)


def pair_kernel(keep_ref, got_ref, out_ref):
    total = (keep_ref[...] + got_ref[...].astype(F32)).astype(BF)
    out_ref[: INNER // 2, :] = total[:, :E]
    out_ref[INNER // 2 :, :] = total[:, E:]


def sum_kernel(got_ref, chunk_ref, skip_ref):
    total = jnp.sum(got_ref[:, :, : 2 * E].astype(F32), axis=0)
    side = jnp.concatenate([total[0:2, E : E + N], total[0:2, E + N :], jnp.zeros((4, N), F32)], axis=0)
    outer = got_ref[:, :, 2 * E :].reshape(4, 2, CTX, 8, E)
    halves = [jnp.sum(outer[:, c].reshape(DEV // 2, 8, E).astype(F32), axis=0) for c in range(2)]
    chunk = jnp.concatenate([total[:, :E], side] + halves, axis=1)
    chunk_ref[...] = jnp.broadcast_to(chunk[None], chunk_ref.shape).astype(BF)
    skip_ref[...] = total[6:7, E + 128 : E + 256]


def table_kernel(got_ref, table_ref):
    misc = got_ref[:, :, E : 2 * E]
    ids = misc[:, 6:7, 0:128].astype(F32)
    sub = lax.broadcasted_iota(jnp.int32, (DEV, 8, 128), 1) - 2
    lane = lax.broadcasted_iota(jnp.int32, (DEV, 8, 128), 2)
    want = jnp.where(lane == sub, 2.0, jnp.where(lane == sub + 64, 1.0, 0.0))
    row = jnp.sum(ids * want, axis=2, keepdims=True)
    row = jnp.where((sub[:, :, :1] >= 0) & (sub[:, :, :1] < CAP), row, -1.0)
    rid = lax.broadcasted_iota(jnp.int32, (DEV, 8, ROWS_DEV), 2).astype(F32)
    hits = jnp.where(rid == row, 1.0, 0.0).reshape(DEV * 8, ROWS_DEV).astype(BF)
    table_ref[...] = dot(hits, misc.reshape(DEV * 8, E), TN)


def last_kernel(core_ref, own_ref, other_ref, w_up_ref, w_in_ref, up_ref, in_ref, go_ref, g_ref, side_ref):
    step = pl.program_id(0)
    core = core_ref[0]
    sources = ((core, own_ref), (1 - core, other_ref))

    @pl.when(step == 0)
    def _():
        for x in range(4):
            for at, ref in sources:
                rows = pl.ds(pl.multiple_of((2 * x + at) * N, N), N)
                g_ref[rows, :] = ref[x * N : (x + 1) * N, :E]
                side_ref[rows, :] = ref[x * N : (x + 1) * N, E : E + N]
        j = lax.broadcasted_iota(jnp.int32, (2 * N, 8 * DEV), 0)
        r = lax.broadcasted_iota(jnp.int32, (2 * N, 8 * DEV), 1)
        first = r - (8 * lax.shift_right_logical(j, 1) + (j & 1))
        for m in range(2):
            pick = jnp.where(first == 2 * m, 1.0, 0.0).astype(BF)
            g_ref[INNER:, m * N : (m + 1) * N] = dot(pick, side_ref[...]).astype(BF)

    g = g_ref[...]
    part = pl.ds(pl.multiple_of(step * N, N), N)
    in_ref[...] = lax.dot_general(w_up_ref[:, part], g, (((0,), (1,)), ((), ())), preferred_element_type=F32)
    up_ref[...] = jnp.transpose(dot(w_in_ref[part, :], g))
    lanes = pl.ds(pl.multiple_of(E + N + E * lax.shift_right_logical(step, 1), N), E)
    for m in range(2):
        rows = pl.ds(pl.multiple_of((2 * m + (step & 1)) * N, N), N)
        for at, ref in sources:
            go_ref[pl.ds(pl.multiple_of(at * N, N), N), m * E : (m + 1) * E] = ref[rows, lanes].astype(F32)


def hop(value, axis, step):
    return lax.ppermute(value, axis, [(i, (i + step) % 4) for i in range(4)])


def local(event_rows, event_index, decay, saved_state, dout, w_up, w_in, w_out, skip):
    every = ("x", "core", "y", "z")
    rows, d_out = event_rows[0], dout[0]
    core, y, z = (lax.axis_index(a).reshape(1) for a in ("core", "y", "z"))
    proj, dy, cum, cumt, *sums = call(
        project_kernel,
        [((T, PROJ), BF), ((INNER, T), BF), ((H, T), F32), ((T, H), F32)] + [((MR, N), BF)] * 4,
        BIG, 750_000_000, 4_500_000,
        in_specs=[SM] + [HBM] * 6, out_specs=(VM,) * 8,
        scratch_shapes=[
            pltpu.VMEM((T, E), BF), pltpu.VMEM((T, D), BF), pltpu.VMEM((H, T), F32),
            pltpu.VMEM((E, D), BF), pltpu.VMEM((D, PROJ), BF), pltpu.VMEM((INNER, D), BF),
            pltpu.VMEM((4, MR, N), BF), pltpu.SemaphoreType.DMA((6,)),
        ],
    )(z, rows, d_out, decay[0], w_up, w_in, w_out)
    sums = sums[:1] + [hop(v, "z", k + 1) for k, v in enumerate(sums[1:])]
    keep, give, dx, tx, bt, dbt, dct, extra = call(
        local_kernel,
        [((INNER // 2, D), F32), ((INNER // 2, D), BF), ((INNER, T), F32), ((INNER, T), BF), ((N, T), BF),
         ((N, T), F32), ((N, T), BF), ((1, T), F32)],
        BIG, 2_500_000_000, 6_000_000,
        in_specs=[VM] * 6 + [SM] * 2, out_specs=(VM,) * 8,
        scratch_shapes=[
            pltpu.VMEM((INNER, T), F32), pltpu.VMEM((INNER, T), BF),
            pltpu.VMEM((INNER, N), BF), pltpu.VMEM((T, T), BF),
        ],
    )(proj, dy, cum, cumt, jnp.swapaxes(saved_state[0, 0], 1, 2).reshape(INNER, N), d_out, skip, core)
    sums, give = lax.optimization_barrier((sums, give))
    (total,) = call(
        inner_kernel, [((MR, N), BF)], 8, 2_000_000, 400_000,
        in_specs=[SM] + [VM] * 4, out_specs=(VM,), scratch_shapes=[pltpu.VMEM((4, MR, N), BF)],
    )(z, *sums)
    totals = [total] + [hop(total, "y", k) for k in range(1, 4)]
    misc, hits = call(
        slot_kernel, [((8 * DEV, E), BF), ((8 * DEV, T), BF)], 16, 300_000_000, 1_500_000,
        in_specs=[VM] * 2, out_specs=(VM,) * 2,
    )(event_index, extra)
    totals, hits = lax.optimization_barrier((totals, hits))
    carries = call(
        outer_kernel, [((GR, N), BF)] * 4, 8, 4_000_000, 800_000,
        in_specs=[SM] * 2 + [VM] * 8, out_specs=(VM,) * 4,
        scratch_shapes=[pltpu.VMEM((4, MR, N), BF)] * 2 + [pltpu.VMEM((4, GR, N), BF)],
    )(y, z, *sums, *totals)
    carries = [carries[0]] + [hop(v, "z", k + 1) for k, v in enumerate(carries[1:])]
    (outer,) = call(
        pair_kernel, [((8 * DEV, E), BF)], 8, 300_000, 2_000_000, in_specs=[VM] * 2, out_specs=(VM,)
    )(keep, lax.ppermute(give, "core", [(0, 1), (1, 0)]))
    carries, outer = lax.optimization_barrier((carries, outer))
    (pay,) = call(
        finish_kernel, [((8 * DEV, 3 * E), BF)], 36, 1_400_000_000, 6_000_000,
        in_specs=[SM] + [VM] * 16, out_specs=(VM,),
        scratch_shapes=[pltpu.VMEM((INNER, N), BF), pltpu.VMEM((PROJ, T), BF)],
    )(z, *carries, outer, bt, cum, tx, dbt, dct, rows, w_up, hits, misc, dx, w_in)
    pay_got = lax.all_to_all(pay.reshape(DEV, 8, 3 * E), every, 0, 0, tiled=True)
    chunk, skip_sum = call(
        sum_kernel, [((DEV // 2, 8, 7 * N), BF), ((1, 128), F32)], 12, 2_000_000, 3_000_000,
        in_specs=[VM], out_specs=(VM,) * 2,
    )(pay_got)
    whole = lax.all_to_all(chunk, ("x", "y", "z"), 0, 0, tiled=True).reshape(DEV * 4, 7 * N)
    other = lax.ppermute(whole, "core", [(0, 1), (1, 0)])
    (table,) = call(
        table_kernel, [((ROWS_DEV, E), F32)], 12, 400_000_000, 2_000_000, in_specs=[VM], out_specs=(VM,)
    )(pay_got)
    column = pl.BlockSpec((E, D // 4), lambda i: (0, i))
    row = pl.BlockSpec((D // 4, PROJ), lambda i: (i, 0))
    grad_up, grad_in, grad_out = pl.pallas_call(
        last_kernel,
        grid=(4,),
        out_shape=tuple(jax.ShapeDtypeStruct(s, F32) for s in ((E, D), (D, PROJ), (INNER, D))),
        in_specs=[SM] + [VM] * 4,
        out_specs=(column, row, pl.BlockSpec((INNER // 4, D), lambda i: (i, 0))),
        scratch_shapes=[pltpu.VMEM((PROJ, E), BF), pltpu.VMEM((8 * DEV, N), BF)],
        compiler_params=pltpu.CompilerParams(vmem_limit_bytes=24 * MB),
        cost_estimate=pl.CostEstimate(flops=700_000_000, bytes_accessed=8_000_000, transcendentals=0),
    )(core, whole, other, w_up, w_in)
    grad_skip = skip_sum[0, :H] + skip_sum[0, 32 : 32 + H]
    return (grad_up, grad_in, grad_out, grad_skip, table)


def solution(mesh):
    mesh = Mesh(mesh.devices.reshape(4, 2, 4, 4), ("x", "core", "y", "z"))
    batch, ctx = ("x", "core"), ("y", "z")
    in_specs = (
        P(batch, ctx, None),
        P(batch, ctx),
        P(batch, None, ctx),
        P(batch, ctx, None, None, None),
        P(batch, ctx, None),
        P(),
        P(),
        P(),
        P(),
    )
    out_specs = (P(), P(), P(), P(), P(batch + ctx, None))
    return jax.shard_map(local, mesh=mesh, in_specs=in_specs, out_specs=out_specs, check_vma=False)
```

```python
from functools import partial

import jax
import jax.numpy as jnp
from jax import lax
from jax.experimental import pallas as pl
from jax.experimental.pallas import tpu as pltpu
from jax.sharding import Mesh, PartitionSpec as P

T = 256
E = 256
D = 512
H = 16
HP = 64
N = 128
INNER = H * HP
PROJ = INNER + 2 * N
ROWS_DEV = 512
CAP = 4
DEV = 128
CTX = 16
GH = 4
GR = GH * HP
MR = GR + 16

DT = 0.0625
SC = 128.0**-0.5
F32 = jnp.float32
BF = jnp.bfloat16
NN = (((1,), (0,)), ((), ()))
NT = (((1,), (1,)), ((), ()))
TN = (((0,), (0,)), ((), ()))
MB = 1 << 20
BIG = 60


def dot(a, b, dims=NN):
    return lax.dot_general(a, b, dims, preferred_element_type=F32)


def split3(v):
    hi = v.astype(BF)
    rest = v - hi.astype(F32)
    mid = rest.astype(BF)
    return hi, mid, (rest - mid.astype(F32)).astype(BF)


def call(kernel, outs, vmem, flops, nbytes, **kw):
    return pl.pallas_call(
        kernel,
        out_shape=tuple(jax.ShapeDtypeStruct(s, d) for s, d in outs),
        compiler_params=pltpu.CompilerParams(vmem_limit_bytes=vmem * MB),
        cost_estimate=pl.CostEstimate(flops=flops, bytes_accessed=nbytes, transcendentals=0),
        **kw,
    )


VM = pl.BlockSpec(memory_space=pltpu.VMEM)
HBM = pl.BlockSpec(memory_space=pltpu.HBM)
SM = pl.BlockSpec(memory_space=pltpu.SMEM)


def decay_rows(amounts):
    row = lax.broadcasted_iota(jnp.int32, (MR - GR, N), 0)
    out = jnp.zeros((MR - GR, N), F32)
    for i, amount in enumerate(amounts):
        for k, part in enumerate(split3(amount)):
            out = jnp.where(row == 3 * i + k, part.astype(F32), out)
    return out.astype(BF)


def decays(ref, at):
    rows = ref[at, GR:, :].astype(F32)
    return [rows[3 * i : 3 * i + 1] + rows[3 * i + 1 : 3 * i + 2] + rows[3 * i + 2 : 3 * i + 3] for i in range(GH)]


def sums_of(ref, at, i):
    return ref[at, i * HP : (i + 1) * HP, :].astype(F32)


def project_kernel(z_ref, rows_hbm, dout_hbm, decay_hbm, w_up_hbm, w_in_hbm, w_out_hbm,
                   u_ref, c_ref, dy_ref, cum_ref, cumt_ref, g0_ref, g1_ref, g2_ref, g3_ref,
                   rows_ref, dout_ref, decay_ref, w_up_ref, w_c_ref, w_out_ref, all_ref, sems):
    pairs = (
        (rows_hbm, rows_ref), (w_up_hbm, w_up_ref), (w_in_hbm.at[:, INNER + N :], w_c_ref),
        (dout_hbm, dout_ref), (w_out_hbm, w_out_ref), (decay_hbm, decay_ref),
    )
    copies = [pltpu.make_async_copy(a, b, sems.at[i]) for i, (a, b) in enumerate(pairs)]
    for copy in copies:
        copy.start()
    copies[0].wait()
    copies[1].wait()
    u_ref[...] = dot(rows_ref[...], w_up_ref[...]).astype(BF)
    copies[2].wait()
    c_ref[...] = dot(u_ref[...], w_c_ref[...]).astype(BF)
    copies[3].wait()
    copies[4].wait()
    dy_ref[...] = dot(w_out_ref[...], dout_ref[...], NT).astype(BF)
    copies[5].wait()
    logs = split3(jnp.log(decay_ref[...]))
    r = lax.broadcasted_iota(jnp.int32, (T, T), 0)
    c = lax.broadcasted_iota(jnp.int32, (T, T), 1)
    upper = (r <= c).astype(F32).astype(BF)
    lower = (c <= r).astype(F32).astype(BF)
    cum = sum(dot(p, upper) for p in logs)
    cum_ref[...] = cum
    cumt_ref[...] = sum(dot(lower, p, NT) for p in logs)
    start = jnp.exp(cum)
    scaled = jnp.concatenate(
        [
            (dy_ref[h * HP : (h + 1) * HP, :].astype(F32) * (SC * start[h : h + 1, :])).astype(BF)
            for h in range(H)
        ],
        axis=0,
    )
    sums = dot(scaled, c_ref[...]).astype(BF)
    amount = jnp.exp(cum[:, T - 1 : T])
    for q in range(H // GH):
        all_ref[q, :GR, :] = sums[q * GR : (q + 1) * GR, :]
        all_ref[q, GR:, :] = decay_rows([jnp.broadcast_to(amount[h : h + 1, :], (1, N)) for h in range(q * GH, (q + 1) * GH)])
    for k, ref in enumerate((g0_ref, g1_ref, g2_ref, g3_ref)):
        ref[...] = all_ref[(z_ref[0] + k) & 3]


def place(at, refs, out_ref):
    for k, ref in enumerate(refs):
        out_ref[(at + 4 - k) & 3] = ref[...]


def inner_kernel(z_ref, a_ref, b_ref, c_ref, d_ref, out_ref, st_ref):
    place(z_ref[0], (a_ref, b_ref, c_ref, d_ref), st_ref)
    amounts = [decays(st_ref, zz) for zz in range(4)]
    for i in range(GH):
        carry = sums_of(st_ref, 3, i)
        for zz in (2, 1, 0):
            carry = sums_of(st_ref, zz, i) + amounts[zz][i] * carry
        out_ref[i * HP : (i + 1) * HP, :] = carry.astype(BF)
    out_ref[GR:, :] = decay_rows([amounts[0][i] * amounts[1][i] * amounts[2][i] * amounts[3][i] for i in range(GH)])


def outer_kernel(y_ref, z_ref, a_ref, b_ref, c_ref, d_ref, ta_ref, tb_ref, tc_ref, td_ref,
                 g0_ref, g1_ref, g2_ref, g3_ref, st_ref, tt_ref, ct_ref):
    y, z = y_ref[0], z_ref[0]
    place(z, (a_ref, b_ref, c_ref, d_ref), st_ref)
    place(y, (ta_ref, tb_ref, tc_ref, td_ref), tt_ref)
    inner = [decays(st_ref, zz) for zz in range(4)]
    outer = [decays(tt_ref, yy) for yy in range(4)]
    for i in range(GH):
        carry = jnp.zeros((HP, N), F32)
        for yy in (3, 2, 1):
            carry = jnp.where(yy > y, sums_of(tt_ref, yy, i) + outer[yy][i] * carry, carry)
        for zz in (3, 2, 1, 0):
            ct_ref[zz, i * HP : (i + 1) * HP, :] = carry.astype(BF)
            if zz:
                carry = sums_of(st_ref, zz, i) + inner[zz][i] * carry
    for k, ref in enumerate((g0_ref, g1_ref, g2_ref, g3_ref)):
        ref[...] = ct_ref[(z + k) & 3]


def local_kernel(u_ref, c_ref, w_in_ref, dy_ref, cum_ref, cumt_ref, h0_ref, dout_ref, skip_ref, core_ref,
                 keep_ref, give_ref, dx_ref, tx_ref, bt_ref, dbt_ref, dct_ref, extra_ref, x_ref, y_ref, sdy_ref, h0t_ref, sum_ref):
    x_ref[...] = dot(u_ref[...], w_in_ref[:, : INNER + N]).astype(BF)
    proj_t = jnp.transpose(x_ref[...])
    bt = proj_t[INNER:, :]
    c_nat = c_ref[...]
    ct = jnp.transpose(c_nat)
    b_nat = x_ref[:, INNER:]
    pair = (SC * DT) * dot(b_nat, c_nat, NT)
    r = lax.broadcasted_iota(jnp.int32, (N, N), 0)
    c = lax.broadcasted_iota(jnp.int32, (N, N), 1)
    causal = r <= c
    cum = cum_ref[...]
    cumt = cumt_ref[...]
    start = jnp.exp(cum)
    tail = DT * jnp.exp(cum[:, T - 1 : T] - cum)
    bt_ref[...] = bt
    h0t_ref[...] = h0_ref[...].astype(BF)
    y_ref[...] = dot(h0t_ref[...], ct)
    skip_sums = []
    a00 = jnp.zeros((N, N), F32)
    a01 = jnp.zeros((N, N), F32)
    a11 = jnp.zeros((N, N), F32)
    zero = jnp.zeros((N, N), BF)
    zrow = jnp.zeros((HP, T), BF)
    for h in range(H):
        lo, hi = h * HP, (h + 1) * HP
        row0, row1 = cum[h : h + 1, :N], cum[h : h + 1, N:]
        col0, col1 = cumt[:N, h : h + 1], cumt[N:, h : h + 1]
        m00 = jnp.exp(jnp.where(causal, row0 - col0, -1e30))
        m01 = jnp.exp(row1 - col0)
        m11 = jnp.exp(jnp.where(causal, row1 - col1, -1e30))
        weights = jnp.concatenate(
            [
                jnp.concatenate([(m00 * pair[:N, :N]).astype(BF), (m01 * pair[:N, N:]).astype(BF)], axis=1),
                jnp.concatenate([zero, (m11 * pair[N:, N:]).astype(BF)], axis=1),
            ],
            axis=0,
        )
        x_h = proj_t[lo:hi, :]
        dy_h = dy_ref[lo:hi, :]
        x_f, dy_f = x_h.astype(F32), dy_h.astype(F32)
        st = start[h : h + 1, :]
        skip = skip_ref[h]
        y_ref[lo:hi, :] = dot(x_h, weights) + SC * st * y_ref[lo:hi, :] + skip * x_f
        dx_ref[lo:hi, :] = dot(dy_h, weights, NT) + skip * dy_f
        sdy_ref[lo:hi, :] = (st * dy_f).astype(BF)
        tx_ref[lo:hi, :] = (tail[h : h + 1, :] * x_f).astype(BF)
        x_pair = x_ref[:, (h // 2) * N : (h // 2 + 1) * N]
        dy_z = jnp.concatenate([dy_h, zrow] if h % 2 == 0 else [zrow, dy_h], axis=0)
        q0 = dot(x_pair[:N, :], dy_z)
        q11 = dot(x_pair[N:, :], dy_z[:, N:])
        a00 += m00 * q0[:, :N]
        a01 += m01 * q0[:, N:]
        a11 += m11 * q11
        skip_sums.append(jnp.sum(x_f * dy_f, keepdims=True))
    core = core_ref[0]
    half = INNER // 2
    mine = pl.ds(pl.multiple_of(core * half, half), half)
    other = pl.ds(pl.multiple_of((1 - core) * half, half), half)
    give_ref[...] = dot(y_ref[other, :].astype(BF), dout_ref[...]).astype(BF)
    keep_ref[...] = dot(y_ref[mine, :].astype(BF), dout_ref[...])
    sum_ref[:N, :N] = a00.astype(BF)
    sum_ref[:N, N:] = a01.astype(BF)
    sum_ref[N:, :N] = zero
    sum_ref[N:, N:] = a11.astype(BF)
    a = sum_ref[...]
    dct_ref[...] = (SC * (DT * dot(bt, a) + dot(h0t_ref[...], sdy_ref[...], TN))).astype(BF)
    dbt_ref[...] = (DT * SC) * dot(ct, a, NT)
    lane = lax.broadcasted_iota(jnp.int32, (1, T), 1)
    extra = jnp.zeros((1, T), F32)
    for h in range(H):
        whole = skip_sums[h]
        top = whole.astype(BF).astype(F32)
        extra = extra + jnp.where(lane == 128 + h, top, 0.0) + jnp.where(lane == 160 + h, whole - top, 0.0)
    extra_ref[...] = extra


def slot_kernel(index_ref, extra_ref, misc_ref, hits_ref):
    index = index_ref[...]
    owner_row = lax.shift_right_logical(index, 9)
    rr = lax.broadcasted_iota(jnp.int32, (T, T), 0)
    cc = lax.broadcasted_iota(jnp.int32, (T, T), 1)
    index_col = jnp.sum(jnp.where(rr == cc, index.astype(F32), 0.0), axis=1, keepdims=True)
    index_col = index_col.astype(jnp.int32)
    owner_col = lax.shift_right_logical(index_col, 9)
    same = owner_col == owner_row
    rank_row = jnp.sum(jnp.where(same & (rr < cc), 1.0, 0.0), axis=0, keepdims=True).astype(jnp.int32)
    rank_col = jnp.sum(jnp.where(same & (cc < rr), 1.0, 0.0), axis=1, keepdims=True).astype(jnp.int32)
    local_col = index_col - owner_col * ROWS_DEV
    id_hi = lax.shift_right_logical(local_col, 1)
    id_lo = local_col - 2 * id_hi
    v = jnp.where(cc == rank_col, id_hi, jnp.where(cc == rank_col + 64, id_lo, 0))
    row_id = lax.broadcasted_iota(jnp.int32, (8 * DEV, T), 0)
    hits_ref[...] = jnp.where(row_id == owner_row * 8 + 2 + rank_row, 1.0, 0.0).astype(BF)
    heads = jnp.where(row_id == owner_row * 8 + 6, 1.0, 0.0).astype(BF)
    misc = dot(heads, v.astype(F32).astype(BF))
    misc_ref[...] = (misc + jnp.where((row_id & 7) == 6, extra_ref[...], 0.0)).astype(BF)


def finish_kernel(z_ref, c0_ref, c1_ref, c2_ref, c3_ref, outer_ref, bt_ref, cum_ref, tx_ref, dbt_ref, dct_ref,
                  rows_ref, w_up_ref, hits_ref, misc_ref, dx_ref, w_in_ref, out_ref, carry_ref, d_ref):
    out_ref[:, 2 * E :] = outer_ref[...]
    for k, ref in enumerate((c0_ref, c1_ref, c2_ref, c3_ref)):
        carry_ref[pl.ds(pl.multiple_of(((z_ref[0] + 4 - k) & 3) * GR, GR), GR), :] = ref[...]
    cum = cum_ref[...]
    tail = DT * jnp.exp(cum[:, T - 1 : T] - cum)
    carry = carry_ref[...]
    entering = dot(carry, bt_ref[...])
    for h in range(H):
        lo, hi = h * HP, (h + 1) * HP
        d_ref[lo:hi, :] = (dx_ref[lo:hi, :] + tail[h : h + 1, :] * entering[lo:hi, :]).astype(BF)
    d_ref[INNER + N :, :] = dct_ref[...]
    d_ref[INNER : INNER + N, :] = (dbt_ref[...] + dot(carry, tx_ref[...], TN)).astype(BF)
    d = d_ref[...]
    g = dot(d, rows_ref[...]).astype(BF)
    out_ref[:, :E] = g[:INNER, :]
    du = dot(w_in_ref[...], d).astype(BF)
    de = dot(w_up_ref[...], du).astype(BF)
    r = lax.broadcasted_iota(jnp.int32, (8 * DEV, 2 * N), 0)
    j = lax.broadcasted_iota(jnp.int32, (1, 2 * N), 1)
    place = jnp.where(r == 8 * lax.shift_right_logical(j, 1) + (j & 1), 1.0, 0.0).astype(BF)
    misc = misc_ref[...].astype(F32) + dot(hits_ref[...], de, NT) + dot(place, g[INNER:, :])
    out_ref[:, E : 2 * E] = misc.astype(BF)


def pair_kernel(keep_ref, got_ref, tx_ref, out_ref, tx_out_ref):
    tx_out_ref[...] = tx_ref[...]
    total = (keep_ref[...] + got_ref[...].astype(F32)).astype(BF)
    out_ref[: INNER // 2, :] = total[:, :E]
    out_ref[INNER // 2 :, :] = total[:, E:]


def sum_kernel(got_ref, chunk_ref, skip_ref):
    total = jnp.sum(got_ref[:, :, : 2 * E].astype(F32), axis=0)
    side = jnp.concatenate([total[0:2, E : E + N], total[0:2, E + N :], jnp.zeros((4, N), F32)], axis=0)
    outer = got_ref[:, :, 2 * E :].reshape(4, 2, CTX, 8, E)
    halves = [jnp.sum(outer[:, c].reshape(DEV // 2, 8, E).astype(F32), axis=0) for c in range(2)]
    chunk = jnp.concatenate([total[:, :E], side] + halves, axis=1)
    chunk_ref[...] = jnp.broadcast_to(chunk[None], chunk_ref.shape).astype(BF)
    skip_ref[...] = total[6:7, E + 128 : E + 256]


def table_kernel(got_ref, table_ref):
    misc = got_ref[:, :, E : 2 * E]
    ids = misc[:, 6:7, 0:128].astype(F32)
    sub = lax.broadcasted_iota(jnp.int32, (DEV, 8, 128), 1) - 2
    lane = lax.broadcasted_iota(jnp.int32, (DEV, 8, 128), 2)
    want = jnp.where(lane == sub, 2.0, jnp.where(lane == sub + 64, 1.0, 0.0))
    row = jnp.sum(ids * want, axis=2, keepdims=True)
    row = jnp.where((sub[:, :, :1] >= 0) & (sub[:, :, :1] < CAP), row, -1.0)
    rid = lax.broadcasted_iota(jnp.int32, (DEV, 8, ROWS_DEV), 2).astype(F32)
    hits = jnp.where(rid == row, 1.0, 0.0).reshape(DEV * 8, ROWS_DEV).astype(BF)
    table_ref[...] = dot(hits, misc.reshape(DEV * 8, E), TN)


def last_kernel(core_ref, own_ref, other_ref, w_up_ref, w_in_ref, up_ref, in_ref, go_ref, g_ref, side_ref):
    step = pl.program_id(0)
    core = core_ref[0]
    sources = ((core, own_ref), (1 - core, other_ref))

    @pl.when(step == 0)
    def _():
        for x in range(4):
            for at, ref in sources:
                rows = pl.ds(pl.multiple_of((2 * x + at) * N, N), N)
                g_ref[rows, :] = ref[x * N : (x + 1) * N, :E]
                side_ref[rows, :] = ref[x * N : (x + 1) * N, E : E + N]
        j = lax.broadcasted_iota(jnp.int32, (2 * N, 8 * DEV), 0)
        r = lax.broadcasted_iota(jnp.int32, (2 * N, 8 * DEV), 1)
        first = r - (8 * lax.shift_right_logical(j, 1) + (j & 1))
        for m in range(2):
            pick = jnp.where(first == 2 * m, 1.0, 0.0).astype(BF)
            g_ref[INNER:, m * N : (m + 1) * N] = dot(pick, side_ref[...]).astype(BF)

    g = g_ref[...]
    part = pl.ds(pl.multiple_of(step * N, N), N)
    in_ref[...] = lax.dot_general(w_up_ref[:, part], g, (((0,), (1,)), ((), ())), preferred_element_type=F32)
    up_ref[...] = jnp.transpose(dot(w_in_ref[part, :], g))
    lanes = pl.ds(pl.multiple_of(E + N + E * lax.shift_right_logical(step, 1), N), E)
    for m in range(2):
        rows = pl.ds(pl.multiple_of((2 * m + (step & 1)) * N, N), N)
        for at, ref in sources:
            go_ref[pl.ds(pl.multiple_of(at * N, N), N), m * E : (m + 1) * E] = ref[rows, lanes].astype(F32)


def hop(value, axis, step):
    return lax.ppermute(value, axis, [(i, (i + step) % 4) for i in range(4)])


def local(event_rows, event_index, decay, saved_state, dout, w_up, w_in, w_out, skip):
    every = ("x", "core", "y", "z")
    rows, d_out = event_rows[0], dout[0]
    core, y, z = (lax.axis_index(a).reshape(1) for a in ("core", "y", "z"))
    u, c_nat, dy, cum, cumt, *sums = call(
        project_kernel,
        [((T, D), BF), ((T, N), BF), ((INNER, T), BF), ((H, T), F32), ((T, H), F32)] + [((MR, N), BF)] * 4,
        BIG, 750_000_000, 4_500_000,
        in_specs=[SM] + [HBM] * 6, out_specs=(VM,) * 9,
        scratch_shapes=[
            pltpu.VMEM((T, E), BF), pltpu.VMEM((T, D), BF), pltpu.VMEM((H, T), F32),
            pltpu.VMEM((E, D), BF), pltpu.VMEM((D, N), BF), pltpu.VMEM((INNER, D), BF),
            pltpu.VMEM((4, MR, N), BF), pltpu.SemaphoreType.DMA((6,)),
        ],
    )(z, rows, d_out, decay[0], w_up, w_in, w_out)
    sums = sums[:1] + [hop(v, "z", k + 1) for k, v in enumerate(sums[1:])]
    keep, give, dx, tx, bt, dbt, dct, extra = call(
        local_kernel,
        [((INNER // 2, D), F32), ((INNER // 2, D), BF), ((INNER, T), F32), ((INNER, T), BF), ((N, T), BF),
         ((N, T), F32), ((N, T), BF), ((1, T), F32)],
        BIG, 2_500_000_000, 6_000_000,
        in_specs=[VM] * 8 + [SM] * 2, out_specs=(VM,) * 8,
        scratch_shapes=[
            pltpu.VMEM((T, INNER + N), BF),
            pltpu.VMEM((INNER, T), F32), pltpu.VMEM((INNER, T), BF),
            pltpu.VMEM((INNER, N), BF), pltpu.VMEM((T, T), BF),
        ],
    )(u, c_nat, w_in, dy, cum, cumt, jnp.swapaxes(saved_state[0, 0], 1, 2).reshape(INNER, N), d_out, skip, core)
    sums, give = lax.optimization_barrier((sums, give))
    (total,) = call(
        inner_kernel, [((MR, N), BF)], 8, 2_000_000, 400_000,
        in_specs=[SM] + [VM] * 4, out_specs=(VM,), scratch_shapes=[pltpu.VMEM((4, MR, N), BF)],
    )(z, *sums)
    totals = [total] + [hop(total, "y", k) for k in range(1, 4)]
    misc, hits = call(
        slot_kernel, [((8 * DEV, E), BF), ((8 * DEV, T), BF)], 16, 300_000_000, 1_500_000,
        in_specs=[VM] * 2, out_specs=(VM,) * 2,
    )(event_index, extra)
    totals, hits = lax.optimization_barrier((totals, hits))
    carries = call(
        outer_kernel, [((GR, N), BF)] * 4, 8, 4_000_000, 800_000,
        in_specs=[SM] * 2 + [VM] * 8, out_specs=(VM,) * 4,
        scratch_shapes=[pltpu.VMEM((4, MR, N), BF)] * 2 + [pltpu.VMEM((4, GR, N), BF)],
    )(y, z, *sums, *totals)
    carries = [carries[0]] + [hop(v, "z", k + 1) for k, v in enumerate(carries[1:])]
    outer, tx = call(
        pair_kernel, [((8 * DEV, E), BF), ((INNER, T), BF)], 8, 300_000, 3_000_000, in_specs=[VM] * 3, out_specs=(VM,) * 2
    )(keep, lax.ppermute(give, "core", [(0, 1), (1, 0)]), tx)
    carries, outer = lax.optimization_barrier((carries, outer))
    (pay,) = call(
        finish_kernel, [((8 * DEV, 3 * E), BF)], 36, 1_400_000_000, 6_000_000,
        in_specs=[SM] + [VM] * 16, out_specs=(VM,),
        scratch_shapes=[pltpu.VMEM((INNER, N), BF), pltpu.VMEM((PROJ, T), BF)],
    )(z, *carries, outer, bt, cum, tx, dbt, dct, rows, w_up, hits, misc, dx, w_in)
    pay_got = lax.all_to_all(pay.reshape(DEV, 8, 3 * E), every, 0, 0, tiled=True)
    chunk, skip_sum = call(
        sum_kernel, [((DEV // 2, 8, 7 * N), BF), ((1, 128), F32)], 12, 2_000_000, 3_000_000,
        in_specs=[VM], out_specs=(VM,) * 2,
    )(pay_got)
    whole = lax.all_to_all(chunk, ("x", "y", "z"), 0, 0, tiled=True).reshape(DEV * 4, 7 * N)
    other = lax.ppermute(whole, "core", [(0, 1), (1, 0)])
    (table,) = call(
        table_kernel, [((ROWS_DEV, E), F32)], 12, 400_000_000, 2_000_000, in_specs=[VM], out_specs=(VM,)
    )(pay_got)
    column = pl.BlockSpec((E, D // 4), lambda i: (0, i))
    row = pl.BlockSpec((D // 4, PROJ), lambda i: (i, 0))
    grad_up, grad_in, grad_out = pl.pallas_call(
        last_kernel,
        grid=(4,),
        out_shape=tuple(jax.ShapeDtypeStruct(s, F32) for s in ((E, D), (D, PROJ), (INNER, D))),
        in_specs=[SM] + [VM] * 4,
        out_specs=(column, row, pl.BlockSpec((INNER // 4, D), lambda i: (i, 0))),
        scratch_shapes=[pltpu.VMEM((PROJ, E), BF), pltpu.VMEM((8 * DEV, N), BF)],
        compiler_params=pltpu.CompilerParams(vmem_limit_bytes=24 * MB),
        cost_estimate=pl.CostEstimate(flops=700_000_000, bytes_accessed=8_000_000, transcendentals=0),
    )(core, whole, other, w_up, w_in)
    grad_skip = skip_sum[0, :H] + skip_sum[0, 32 : 32 + H]
    return (grad_up, grad_in, grad_out, grad_skip, table)


def solution(mesh):
    mesh = Mesh(mesh.devices.reshape(4, 2, 4, 4), ("x", "core", "y", "z"))
    batch, ctx = ("x", "core"), ("y", "z")
    in_specs = (
        P(batch, ctx, None),
        P(batch, ctx),
        P(batch, None, ctx),
        P(batch, ctx, None, None, None),
        P(batch, ctx, None),
        P(),
        P(),
        P(),
        P(),
    )
    out_specs = (P(), P(), P(), P(), P(batch + ctx, None))
    return jax.shard_map(local, mesh=mesh, in_specs=in_specs, out_specs=out_specs, check_vma=False)
```

```python
from functools import partial

import jax
import jax.numpy as jnp
from jax import lax
from jax.experimental import pallas as pl
from jax.experimental.pallas import tpu as pltpu
from jax.sharding import Mesh, PartitionSpec as P

T = 256
E = 256
D = 512
H = 16
HP = 64
N = 128
INNER = H * HP
PROJ = INNER + 2 * N
ROWS_DEV = 512
CAP = 4
DEV = 128
CTX = 16
GH = 4
GR = GH * HP
MR = GR + 16

DT = 0.0625
SC = 128.0**-0.5
F32 = jnp.float32
BF = jnp.bfloat16
NN = (((1,), (0,)), ((), ()))
NT = (((1,), (1,)), ((), ()))
TN = (((0,), (0,)), ((), ()))
MB = 1 << 20
BIG = 60


def dot(a, b, dims=NN):
    return lax.dot_general(a, b, dims, preferred_element_type=F32)


def split3(v):
    hi = v.astype(BF)
    rest = v - hi.astype(F32)
    mid = rest.astype(BF)
    return hi, mid, (rest - mid.astype(F32)).astype(BF)


def call(kernel, outs, vmem, flops, nbytes, **kw):
    return pl.pallas_call(
        kernel,
        out_shape=tuple(jax.ShapeDtypeStruct(s, d) for s, d in outs),
        compiler_params=pltpu.CompilerParams(vmem_limit_bytes=vmem * MB),
        cost_estimate=pl.CostEstimate(flops=flops, bytes_accessed=nbytes, transcendentals=0),
        **kw,
    )


VM = pl.BlockSpec(memory_space=pltpu.VMEM)
HBM = pl.BlockSpec(memory_space=pltpu.HBM)
SM = pl.BlockSpec(memory_space=pltpu.SMEM)


def decay_rows(amounts):
    row = lax.broadcasted_iota(jnp.int32, (MR - GR, N), 0)
    out = jnp.zeros((MR - GR, N), F32)
    for i, amount in enumerate(amounts):
        for k, part in enumerate(split3(amount)):
            out = jnp.where(row == 3 * i + k, part.astype(F32), out)
    return out.astype(BF)


def decays(ref, at):
    rows = ref[at, GR:, :].astype(F32)
    return [rows[3 * i : 3 * i + 1] + rows[3 * i + 1 : 3 * i + 2] + rows[3 * i + 2 : 3 * i + 3] for i in range(GH)]


def sums_of(ref, at, i):
    return ref[at, i * HP : (i + 1) * HP, :].astype(F32)


def project_kernel(z_ref, rows_hbm, dout_hbm, decay_hbm, w_up_hbm, w_in_hbm, w_out_hbm,
                   u_ref, c_ref, dy_ref, cum_ref, cumt_ref, g0_ref, g1_ref, g2_ref, g3_ref,
                   rows_ref, dout_ref, decay_ref, w_up_ref, w_c_ref, w_out_ref, all_ref, sems):
    pairs = (
        (rows_hbm, rows_ref), (w_up_hbm, w_up_ref), (w_in_hbm.at[:, INNER + N :], w_c_ref),
        (dout_hbm, dout_ref), (w_out_hbm, w_out_ref), (decay_hbm, decay_ref),
    )
    copies = [pltpu.make_async_copy(a, b, sems.at[i]) for i, (a, b) in enumerate(pairs)]
    for copy in copies:
        copy.start()
    copies[0].wait()
    copies[1].wait()
    u_ref[...] = dot(rows_ref[...], w_up_ref[...]).astype(BF)
    copies[2].wait()
    c_ref[...] = dot(u_ref[...], w_c_ref[...]).astype(BF)
    copies[3].wait()
    copies[4].wait()
    dy_ref[...] = dot(w_out_ref[...], dout_ref[...], NT).astype(BF)
    copies[5].wait()
    logs = split3(jnp.log(decay_ref[...]))
    r = lax.broadcasted_iota(jnp.int32, (T, T), 0)
    c = lax.broadcasted_iota(jnp.int32, (T, T), 1)
    upper = (r <= c).astype(F32).astype(BF)
    lower = (c <= r).astype(F32).astype(BF)
    cum = sum(dot(p, upper) for p in logs)
    cum_ref[...] = cum
    cumt_ref[...] = sum(dot(lower, p, NT) for p in logs)
    start = jnp.exp(cum)
    scaled = jnp.concatenate(
        [
            (dy_ref[h * HP : (h + 1) * HP, :].astype(F32) * (SC * start[h : h + 1, :])).astype(BF)
            for h in range(H)
        ],
        axis=0,
    )
    sums = dot(scaled, c_ref[...]).astype(BF)
    amount = jnp.exp(cum[:, T - 1 : T])
    for q in range(H // GH):
        all_ref[q, :GR, :] = sums[q * GR : (q + 1) * GR, :]
        all_ref[q, GR:, :] = decay_rows([jnp.broadcast_to(amount[h : h + 1, :], (1, N)) for h in range(q * GH, (q + 1) * GH)])
    for k, ref in enumerate((g0_ref, g1_ref, g2_ref, g3_ref)):
        ref[...] = all_ref[(z_ref[0] + k) & 3]


def place(at, refs, out_ref):
    for k, ref in enumerate(refs):
        out_ref[(at + 4 - k) & 3] = ref[...]


def inner_kernel(z_ref, a_ref, b_ref, c_ref, d_ref, out_ref, st_ref):
    place(z_ref[0], (a_ref, b_ref, c_ref, d_ref), st_ref)
    amounts = [decays(st_ref, zz) for zz in range(4)]
    for i in range(GH):
        carry = sums_of(st_ref, 3, i)
        for zz in (2, 1, 0):
            carry = sums_of(st_ref, zz, i) + amounts[zz][i] * carry
        out_ref[i * HP : (i + 1) * HP, :] = carry.astype(BF)
    out_ref[GR:, :] = decay_rows([amounts[0][i] * amounts[1][i] * amounts[2][i] * amounts[3][i] for i in range(GH)])


def outer_kernel(y_ref, z_ref, a_ref, b_ref, c_ref, d_ref, ta_ref, tb_ref, tc_ref, td_ref,
                 g0_ref, g1_ref, g2_ref, g3_ref, st_ref, tt_ref, ct_ref):
    y, z = y_ref[0], z_ref[0]
    place(z, (a_ref, b_ref, c_ref, d_ref), st_ref)
    place(y, (ta_ref, tb_ref, tc_ref, td_ref), tt_ref)
    inner = [decays(st_ref, zz) for zz in range(4)]
    outer = [decays(tt_ref, yy) for yy in range(4)]
    for i in range(GH):
        carry = jnp.zeros((HP, N), F32)
        for yy in (3, 2, 1):
            carry = jnp.where(yy > y, sums_of(tt_ref, yy, i) + outer[yy][i] * carry, carry)
        for zz in (3, 2, 1, 0):
            ct_ref[zz, i * HP : (i + 1) * HP, :] = carry.astype(BF)
            if zz:
                carry = sums_of(st_ref, zz, i) + inner[zz][i] * carry
    for k, ref in enumerate((g0_ref, g1_ref, g2_ref, g3_ref)):
        ref[...] = ct_ref[(z + k) & 3]


def local_kernel(u_ref, c_ref, w_in_ref, dy_ref, cum_ref, cumt_ref, h0_ref, dout_ref, skip_ref, core_ref,
                 keep_ref, give_ref, dx_ref, tx_ref, bt_ref, dbt_ref, dct_ref, extra_ref, x_ref, y_ref, sdy_ref, h0t_ref, sum_ref):
    x_ref[...] = dot(u_ref[...], w_in_ref[:, : INNER + N]).astype(BF)
    proj_t = jnp.transpose(x_ref[...])
    bt = proj_t[INNER:, :]
    c_nat = c_ref[...]
    ct = jnp.transpose(c_nat)
    b_nat = x_ref[:, INNER:]
    pair = (SC * DT) * dot(b_nat, c_nat, NT)
    r = lax.broadcasted_iota(jnp.int32, (N, N), 0)
    c = lax.broadcasted_iota(jnp.int32, (N, N), 1)
    causal = r <= c
    cum = cum_ref[...]
    cumt = cumt_ref[...]
    start = jnp.exp(cum)
    tail = DT * jnp.exp(cum[:, T - 1 : T] - cum)
    bt_ref[...] = bt
    h0t_ref[...] = h0_ref[...].astype(BF)
    y_ref[...] = dot(h0t_ref[...], ct)
    skip_sums = []
    a00 = jnp.zeros((N, N), F32)
    a01 = jnp.zeros((N, N), F32)
    a11 = jnp.zeros((N, N), F32)
    zero = jnp.zeros((N, N), BF)
    zrow = jnp.zeros((HP, T), BF)
    for h in range(H):
        lo, hi = h * HP, (h + 1) * HP
        row0, row1 = cum[h : h + 1, :N], cum[h : h + 1, N:]
        col0, col1 = cumt[:N, h : h + 1], cumt[N:, h : h + 1]
        m00 = jnp.exp(jnp.where(causal, row0 - col0, -1e30))
        m01 = jnp.exp(row1 - col0)
        m11 = jnp.exp(jnp.where(causal, row1 - col1, -1e30))
        weights = jnp.concatenate(
            [
                jnp.concatenate([(m00 * pair[:N, :N]).astype(BF), (m01 * pair[:N, N:]).astype(BF)], axis=1),
                jnp.concatenate([zero, (m11 * pair[N:, N:]).astype(BF)], axis=1),
            ],
            axis=0,
        )
        x_h = proj_t[lo:hi, :]
        dy_h = dy_ref[lo:hi, :]
        x_f, dy_f = x_h.astype(F32), dy_h.astype(F32)
        st = start[h : h + 1, :]
        skip = skip_ref[h]
        y_ref[lo:hi, :] = dot(x_h, weights) + SC * st * y_ref[lo:hi, :] + skip * x_f
        dx_ref[lo:hi, :] = dot(dy_h, weights, NT) + skip * dy_f
        sdy_ref[lo:hi, :] = (st * dy_f).astype(BF)
        tx_ref[lo:hi, :] = (tail[h : h + 1, :] * x_f).astype(BF)
        x_pair = x_ref[:, (h // 2) * N : (h // 2 + 1) * N]
        dy_z = jnp.concatenate([dy_h, zrow] if h % 2 == 0 else [zrow, dy_h], axis=0)
        q0 = dot(x_pair[:N, :], dy_z)
        q11 = dot(x_pair[N:, :], dy_z[:, N:])
        a00 += m00 * q0[:, :N]
        a01 += m01 * q0[:, N:]
        a11 += m11 * q11
        skip_sums.append(jnp.sum(x_f * dy_f, keepdims=True))
    core = core_ref[0]
    half = INNER // 2
    mine = pl.ds(pl.multiple_of(core * half, half), half)
    other = pl.ds(pl.multiple_of((1 - core) * half, half), half)
    give_ref[...] = dot(y_ref[other, :].astype(BF), dout_ref[...]).astype(BF)
    keep_ref[...] = dot(y_ref[mine, :].astype(BF), dout_ref[...])
    sum_ref[:N, :N] = a00.astype(BF)
    sum_ref[:N, N:] = a01.astype(BF)
    sum_ref[N:, :N] = zero
    sum_ref[N:, N:] = a11.astype(BF)
    a = sum_ref[...]
    dct_ref[...] = (SC * (DT * dot(bt, a) + dot(h0t_ref[...], sdy_ref[...], TN))).astype(BF)
    dbt_ref[...] = (DT * SC) * dot(ct, a, NT)
    lane = lax.broadcasted_iota(jnp.int32, (1, T), 1)
    extra = jnp.zeros((1, T), F32)
    for h in range(H):
        whole = skip_sums[h]
        top = whole.astype(BF).astype(F32)
        extra = extra + jnp.where(lane == 128 + h, top, 0.0) + jnp.where(lane == 160 + h, whole - top, 0.0)
    extra_ref[...] = extra


def slot_kernel(index_ref, extra_ref, misc_ref, hits_ref):
    index = index_ref[...]
    owner_row = lax.shift_right_logical(index, 9)
    rr = lax.broadcasted_iota(jnp.int32, (T, T), 0)
    cc = lax.broadcasted_iota(jnp.int32, (T, T), 1)
    index_col = jnp.sum(jnp.where(rr == cc, index.astype(F32), 0.0), axis=1, keepdims=True)
    index_col = index_col.astype(jnp.int32)
    owner_col = lax.shift_right_logical(index_col, 9)
    same = owner_col == owner_row
    rank_row = jnp.sum(jnp.where(same & (rr < cc), 1.0, 0.0), axis=0, keepdims=True).astype(jnp.int32)
    rank_col = jnp.sum(jnp.where(same & (cc < rr), 1.0, 0.0), axis=1, keepdims=True).astype(jnp.int32)
    local_col = index_col - owner_col * ROWS_DEV
    id_hi = lax.shift_right_logical(local_col, 1)
    id_lo = local_col - 2 * id_hi
    v = jnp.where(cc == rank_col, id_hi, jnp.where(cc == rank_col + 64, id_lo, 0))
    row_id = lax.broadcasted_iota(jnp.int32, (8 * DEV, T), 0)
    hits_ref[...] = jnp.where(row_id == owner_row * 8 + 2 + rank_row, 1.0, 0.0).astype(BF)
    heads = jnp.where(row_id == owner_row * 8 + 6, 1.0, 0.0).astype(BF)
    misc = dot(heads, v.astype(F32).astype(BF))
    misc_ref[...] = (misc + jnp.where((row_id & 7) == 6, extra_ref[...], 0.0)).astype(BF)


def finish_kernel(z_ref, c0_ref, c1_ref, c2_ref, c3_ref, outer_ref, bt_ref, cum_ref, tx_ref, dbt_ref, dct_ref,
                  rows_ref, w_up_ref, hits_ref, misc_ref, dx_ref, w_in_ref, out_ref, carry_ref, d_ref):
    out_ref[:, 2 * E :] = outer_ref[...]
    for k, ref in enumerate((c0_ref, c1_ref, c2_ref, c3_ref)):
        carry_ref[pl.ds(pl.multiple_of(((z_ref[0] + 4 - k) & 3) * GR, GR), GR), :] = ref[...]
    cum = cum_ref[...]
    tail = DT * jnp.exp(cum[:, T - 1 : T] - cum)
    carry = carry_ref[...]
    entering = dot(carry, bt_ref[...])
    for h in range(H):
        lo, hi = h * HP, (h + 1) * HP
        d_ref[lo:hi, :] = (dx_ref[lo:hi, :] + tail[h : h + 1, :] * entering[lo:hi, :]).astype(BF)
    d_ref[INNER + N :, :] = dct_ref[...]
    d_ref[INNER : INNER + N, :] = (dbt_ref[...] + dot(carry, tx_ref[...], TN)).astype(BF)
    d = d_ref[...]
    g = dot(d, rows_ref[...]).astype(BF)
    out_ref[:, :E] = g[:INNER, :]
    du = dot(w_in_ref[...], d).astype(BF)
    de = dot(w_up_ref[...], du).astype(BF)
    r = lax.broadcasted_iota(jnp.int32, (8 * DEV, 2 * N), 0)
    j = lax.broadcasted_iota(jnp.int32, (1, 2 * N), 1)
    place = jnp.where(r == 8 * lax.shift_right_logical(j, 1) + (j & 1), 1.0, 0.0).astype(BF)
    misc = misc_ref[...].astype(F32) + dot(hits_ref[...], de, NT) + dot(place, g[INNER:, :])
    out_ref[:, E : 2 * E] = misc.astype(BF)


def pair_kernel(keep_ref, got_ref, tx_ref, out_ref, tx_out_ref):
    tx_out_ref[...] = tx_ref[...]
    total = (keep_ref[...] + got_ref[...].astype(F32)).astype(BF)
    out_ref[: INNER // 2, :] = total[:, :E]
    out_ref[INNER // 2 :, :] = total[:, E:]


def sum_kernel(got_ref, chunk_ref, skip_ref):
    total = jnp.sum(got_ref[:, :, : 2 * E].astype(F32), axis=0)
    side = jnp.concatenate([total[0:2, E : E + N], total[0:2, E + N :], jnp.zeros((4, N), F32)], axis=0)
    outer = got_ref[:, :, 2 * E :].reshape(4, 2, CTX, 8, E)
    halves = [jnp.sum(outer[:, c].reshape(DEV // 2, 8, E).astype(F32), axis=0) for c in range(2)]
    chunk = jnp.concatenate([total[:, :E], side] + halves, axis=1)
    chunk_ref[...] = jnp.broadcast_to(chunk[None], chunk_ref.shape).astype(BF)
    skip_ref[...] = total[6:7, E + 128 : E + 256]


def table_kernel(got_ref, table_ref):
    misc = got_ref[:, :, E : 2 * E]
    ids = misc[:, 6:7, 0:128].astype(F32)
    sub = lax.broadcasted_iota(jnp.int32, (DEV, 8, 128), 1) - 2
    lane = lax.broadcasted_iota(jnp.int32, (DEV, 8, 128), 2)
    want = jnp.where(lane == sub, 2.0, jnp.where(lane == sub + 64, 1.0, 0.0))
    row = jnp.sum(ids * want, axis=2, keepdims=True)
    row = jnp.where((sub[:, :, :1] >= 0) & (sub[:, :, :1] < CAP), row, -1.0)
    rid = lax.broadcasted_iota(jnp.int32, (DEV, 8, ROWS_DEV), 2).astype(F32)
    hits = jnp.where(rid == row, 1.0, 0.0).reshape(DEV * 8, ROWS_DEV).astype(BF)
    table_ref[...] = dot(hits, misc.reshape(DEV * 8, E), TN)


def last_kernel(core_ref, own_ref, other_ref, w_up_ref, w_in_ref, up_ref, in_ref, go_ref, g_ref, side_ref, acc_ref):
    step = pl.program_id(0)
    core = core_ref[0]
    sources = ((core, own_ref), (1 - core, other_ref))

    @pl.when(step < 4)
    def _():
        for at, ref in sources:
            g_ref[pl.ds(pl.multiple_of(at * N, N), N), :] = ref[pl.ds(pl.multiple_of(step * N, N), N), :E]
        lanes = pl.ds(pl.multiple_of(E + N + E * lax.shift_right_logical(step, 1), N), E)
        for m in range(2):
            rows = pl.ds(pl.multiple_of((2 * m + (step & 1)) * N, N), N)
            for at, ref in sources:
                go_ref[pl.ds(pl.multiple_of(at * N, N), N), m * E : (m + 1) * E] = ref[rows, lanes].astype(F32)

    @pl.when(step == 4)
    def _():
        for x in range(4):
            for at, ref in sources:
                rows = pl.ds(pl.multiple_of((2 * x + at) * N, N), N)
                side_ref[rows, :] = ref[x * N : (x + 1) * N, E : E + N]
        j = lax.broadcasted_iota(jnp.int32, (2 * N, 8 * DEV), 0)
        r = lax.broadcasted_iota(jnp.int32, (2 * N, 8 * DEV), 1)
        first = r - (8 * lax.shift_right_logical(j, 1) + (j & 1))
        for m in range(2):
            pick = jnp.where(first == 2 * m, 1.0, 0.0).astype(BF)
            g_ref[:, m * N : (m + 1) * N] = dot(pick, side_ref[...]).astype(BF)

    g = g_ref[...]
    in_ref[...] = lax.dot_general(w_up_ref[...], g, (((0,), (1,)), ((), ())), preferred_element_type=F32)
    part = dot(w_in_ref[:, pl.ds(pl.multiple_of(step * E, E), E)], g)

    @pl.when(step == 0)
    def _():
        acc_ref[...] = part

    @pl.when((step > 0) & (step < 4))
    def _():
        acc_ref[...] += part

    @pl.when(step == 4)
    def _():
        up_ref[...] = jnp.transpose(acc_ref[...] + part)


def hop(value, axis, step):
    return lax.ppermute(value, axis, [(i, (i + step) % 4) for i in range(4)])


def local(event_rows, event_index, decay, saved_state, dout, w_up, w_in, w_out, skip):
    every = ("x", "core", "y", "z")
    rows, d_out = event_rows[0], dout[0]
    core, y, z = (lax.axis_index(a).reshape(1) for a in ("core", "y", "z"))
    u, c_nat, dy, cum, cumt, *sums = call(
        project_kernel,
        [((T, D), BF), ((T, N), BF), ((INNER, T), BF), ((H, T), F32), ((T, H), F32)] + [((MR, N), BF)] * 4,
        BIG, 750_000_000, 4_500_000,
        in_specs=[SM] + [HBM] * 6, out_specs=(VM,) * 9,
        scratch_shapes=[
            pltpu.VMEM((T, E), BF), pltpu.VMEM((T, D), BF), pltpu.VMEM((H, T), F32),
            pltpu.VMEM((E, D), BF), pltpu.VMEM((D, N), BF), pltpu.VMEM((INNER, D), BF),
            pltpu.VMEM((4, MR, N), BF), pltpu.SemaphoreType.DMA((6,)),
        ],
    )(z, rows, d_out, decay[0], w_up, w_in, w_out)
    sums = sums[:1] + [hop(v, "z", k + 1) for k, v in enumerate(sums[1:])]
    keep, give, dx, tx, bt, dbt, dct, extra = call(
        local_kernel,
        [((INNER // 2, D), F32), ((INNER // 2, D), BF), ((INNER, T), F32), ((INNER, T), BF), ((N, T), BF),
         ((N, T), F32), ((N, T), BF), ((1, T), F32)],
        BIG, 2_500_000_000, 6_000_000,
        in_specs=[VM] * 8 + [SM] * 2, out_specs=(VM,) * 8,
        scratch_shapes=[
            pltpu.VMEM((T, INNER + N), BF),
            pltpu.VMEM((INNER, T), F32), pltpu.VMEM((INNER, T), BF),
            pltpu.VMEM((INNER, N), BF), pltpu.VMEM((T, T), BF),
        ],
    )(u, c_nat, w_in, dy, cum, cumt, jnp.swapaxes(saved_state[0, 0], 1, 2).reshape(INNER, N), d_out, skip, core)
    sums, give = lax.optimization_barrier((sums, give))
    (total,) = call(
        inner_kernel, [((MR, N), BF)], 8, 2_000_000, 400_000,
        in_specs=[SM] + [VM] * 4, out_specs=(VM,), scratch_shapes=[pltpu.VMEM((4, MR, N), BF)],
    )(z, *sums)
    totals = [total] + [hop(total, "y", k) for k in range(1, 4)]
    misc, hits = call(
        slot_kernel, [((8 * DEV, E), BF), ((8 * DEV, T), BF)], 16, 300_000_000, 1_500_000,
        in_specs=[VM] * 2, out_specs=(VM,) * 2,
    )(event_index, extra)
    totals, hits = lax.optimization_barrier((totals, hits))
    carries = call(
        outer_kernel, [((GR, N), BF)] * 4, 8, 4_000_000, 800_000,
        in_specs=[SM] * 2 + [VM] * 8, out_specs=(VM,) * 4,
        scratch_shapes=[pltpu.VMEM((4, MR, N), BF)] * 2 + [pltpu.VMEM((4, GR, N), BF)],
    )(y, z, *sums, *totals)
    carries = [carries[0]] + [hop(v, "z", k + 1) for k, v in enumerate(carries[1:])]
    outer, tx = call(
        pair_kernel, [((8 * DEV, E), BF), ((INNER, T), BF)], 8, 300_000, 3_000_000, in_specs=[VM] * 3, out_specs=(VM,) * 2
    )(keep, lax.ppermute(give, "core", [(0, 1), (1, 0)]), tx)
    carries, outer = lax.optimization_barrier((carries, outer))
    (pay,) = call(
        finish_kernel, [((8 * DEV, 3 * E), BF)], 36, 1_400_000_000, 6_000_000,
        in_specs=[SM] + [VM] * 16, out_specs=(VM,),
        scratch_shapes=[pltpu.VMEM((INNER, N), BF), pltpu.VMEM((PROJ, T), BF)],
    )(z, *carries, outer, bt, cum, tx, dbt, dct, rows, w_up, hits, misc, dx, w_in)
    pay_got = lax.all_to_all(pay.reshape(DEV, 8, 3 * E), every, 0, 0, tiled=True)
    chunk, skip_sum = call(
        sum_kernel, [((DEV // 2, 8, 7 * N), BF), ((1, 128), F32)], 12, 2_000_000, 3_000_000,
        in_specs=[VM], out_specs=(VM,) * 2,
    )(pay_got)
    whole = lax.all_to_all(chunk, ("x", "y", "z"), 0, 0, tiled=True).reshape(DEV * 4, 7 * N)
    other = lax.ppermute(whole, "core", [(0, 1), (1, 0)])
    (table,) = call(
        table_kernel, [((ROWS_DEV, E), F32)], 12, 400_000_000, 2_000_000, in_specs=[VM], out_specs=(VM,)
    )(pay_got)
    grad_up, grad_in, grad_out = pl.pallas_call(
        last_kernel,
        grid=(5,),
        out_shape=tuple(jax.ShapeDtypeStruct(s, F32) for s in ((E, D), (D, PROJ), (INNER, D))),
        in_specs=[SM] + [VM] * 4,
        out_specs=(
            pl.BlockSpec((E, D), lambda i: (0, 0)),
            pl.BlockSpec((D, E), lambda i: (0, i)),
            pl.BlockSpec((INNER // 4, D), lambda i: (jnp.minimum(i, 3), 0)),
        ),
        scratch_shapes=[pltpu.VMEM((E, E), BF), pltpu.VMEM((8 * DEV, N), BF), pltpu.VMEM((D, E), F32)],
        compiler_params=pltpu.CompilerParams(vmem_limit_bytes=24 * MB),
        cost_estimate=pl.CostEstimate(flops=700_000_000, bytes_accessed=8_000_000, transcendentals=0),
    )(core, whole, other, w_up, w_in)
    grad_skip = skip_sum[0, :H] + skip_sum[0, 32 : 32 + H]
    return (grad_up, grad_in, grad_out, grad_skip, table)


def solution(mesh):
    mesh = Mesh(mesh.devices.reshape(4, 2, 4, 4), ("x", "core", "y", "z"))
    batch, ctx = ("x", "core"), ("y", "z")
    in_specs = (
        P(batch, ctx, None),
        P(batch, ctx),
        P(batch, None, ctx),
        P(batch, ctx, None, None, None),
        P(batch, ctx, None),
        P(),
        P(),
        P(),
        P(),
    )
    out_specs = (P(), P(), P(), P(), P(batch + ctx, None))
    return jax.shard_map(local, mesh=mesh, in_specs=in_specs, out_specs=out_specs, check_vma=False)
```

```python
from functools import partial

import jax
import jax.numpy as jnp
from jax import lax
from jax.experimental import pallas as pl
from jax.experimental.pallas import tpu as pltpu
from jax.sharding import Mesh, PartitionSpec as P

T = 256
E = 256
D = 512
H = 16
HP = 64
N = 128
INNER = H * HP
PROJ = INNER + 2 * N
ROWS_DEV = 512
CAP = 4
DEV = 128
CTX = 16
GH = 4
GR = GH * HP
MR = GR + 16

DT = 0.0625
SC = 128.0**-0.5
F32 = jnp.float32
BF = jnp.bfloat16
NN = (((1,), (0,)), ((), ()))
NT = (((1,), (1,)), ((), ()))
TN = (((0,), (0,)), ((), ()))
MB = 1 << 20
BIG = 60


def dot(a, b, dims=NN):
    return lax.dot_general(a, b, dims, preferred_element_type=F32)


def split3(v):
    hi = v.astype(BF)
    rest = v - hi.astype(F32)
    mid = rest.astype(BF)
    return hi, mid, (rest - mid.astype(F32)).astype(BF)


def call(kernel, outs, vmem, flops, nbytes, **kw):
    return pl.pallas_call(
        kernel,
        out_shape=tuple(jax.ShapeDtypeStruct(s, d) for s, d in outs),
        compiler_params=pltpu.CompilerParams(vmem_limit_bytes=vmem * MB),
        cost_estimate=pl.CostEstimate(flops=flops, bytes_accessed=nbytes, transcendentals=0),
        **kw,
    )


VM = pl.BlockSpec(memory_space=pltpu.VMEM)
HBM = pl.BlockSpec(memory_space=pltpu.HBM)
SM = pl.BlockSpec(memory_space=pltpu.SMEM)


def decay_rows(amounts):
    row = lax.broadcasted_iota(jnp.int32, (MR - GR, N), 0)
    out = jnp.zeros((MR - GR, N), F32)
    for i, amount in enumerate(amounts):
        for k, part in enumerate(split3(amount)):
            out = jnp.where(row == 3 * i + k, part.astype(F32), out)
    return out.astype(BF)


def decays(ref, at):
    rows = ref[at, GR:, :].astype(F32)
    return [rows[3 * i : 3 * i + 1] + rows[3 * i + 1 : 3 * i + 2] + rows[3 * i + 2 : 3 * i + 3] for i in range(GH)]


def sums_of(ref, at, i):
    return ref[at, i * HP : (i + 1) * HP, :].astype(F32)


def project_kernel(z_ref, rows_hbm, dout_hbm, decay_hbm, w_up_hbm, w_in_hbm, w_out_hbm,
                   u_ref, c_ref, dy_ref, cum_ref, cumt_ref, g0_ref, g1_ref, g2_ref, g3_ref,
                   rows_ref, dout_ref, decay_ref, w_up_ref, w_c_ref, w_out_ref, all_ref, sems):
    pairs = (
        (rows_hbm, rows_ref), (w_up_hbm, w_up_ref), (w_in_hbm.at[:, INNER + N :], w_c_ref),
        (dout_hbm, dout_ref), (w_out_hbm, w_out_ref), (decay_hbm, decay_ref),
    )
    copies = [pltpu.make_async_copy(a, b, sems.at[i]) for i, (a, b) in enumerate(pairs)]
    for copy in copies:
        copy.start()
    copies[0].wait()
    copies[1].wait()
    u_ref[...] = dot(rows_ref[...], w_up_ref[...]).astype(BF)
    copies[2].wait()
    c_ref[...] = dot(u_ref[...], w_c_ref[...]).astype(BF)
    copies[3].wait()
    copies[4].wait()
    dy_ref[...] = dot(w_out_ref[...], dout_ref[...], NT).astype(BF)
    copies[5].wait()
    logs = split3(jnp.log(decay_ref[...]))
    r = lax.broadcasted_iota(jnp.int32, (T, T), 0)
    c = lax.broadcasted_iota(jnp.int32, (T, T), 1)
    upper = (r <= c).astype(F32).astype(BF)
    lower = (c <= r).astype(F32).astype(BF)
    cum = sum(dot(p, upper) for p in logs)
    cum_ref[...] = cum
    cumt_ref[...] = sum(dot(lower, p, NT) for p in logs)
    start = jnp.exp(cum)
    scaled = jnp.concatenate(
        [
            (dy_ref[h * HP : (h + 1) * HP, :].astype(F32) * (SC * start[h : h + 1, :])).astype(BF)
            for h in range(H)
        ],
        axis=0,
    )
    sums = dot(scaled, c_ref[...]).astype(BF)
    amount = jnp.exp(cum[:, T - 1 : T])
    for q in range(H // GH):
        all_ref[q, :GR, :] = sums[q * GR : (q + 1) * GR, :]
        all_ref[q, GR:, :] = decay_rows([jnp.broadcast_to(amount[h : h + 1, :], (1, N)) for h in range(q * GH, (q + 1) * GH)])
    for k, ref in enumerate((g0_ref, g1_ref, g2_ref, g3_ref)):
        ref[...] = all_ref[(z_ref[0] + k) & 3]


def place(at, refs, out_ref):
    for k, ref in enumerate(refs):
        out_ref[(at + 4 - k) & 3] = ref[...]


def inner_kernel(z_ref, a_ref, b_ref, c_ref, d_ref, out_ref, st_ref):
    place(z_ref[0], (a_ref, b_ref, c_ref, d_ref), st_ref)
    amounts = [decays(st_ref, zz) for zz in range(4)]
    for i in range(GH):
        carry = sums_of(st_ref, 3, i)
        for zz in (2, 1, 0):
            carry = sums_of(st_ref, zz, i) + amounts[zz][i] * carry
        out_ref[i * HP : (i + 1) * HP, :] = carry.astype(BF)
    out_ref[GR:, :] = decay_rows([amounts[0][i] * amounts[1][i] * amounts[2][i] * amounts[3][i] for i in range(GH)])


def outer_kernel(y_ref, z_ref, a_ref, b_ref, c_ref, d_ref, ta_ref, tb_ref, tc_ref, td_ref,
                 g0_ref, g1_ref, g2_ref, g3_ref, st_ref, tt_ref, ct_ref):
    y, z = y_ref[0], z_ref[0]
    place(z, (a_ref, b_ref, c_ref, d_ref), st_ref)
    place(y, (ta_ref, tb_ref, tc_ref, td_ref), tt_ref)
    inner = [decays(st_ref, zz) for zz in range(4)]
    outer = [decays(tt_ref, yy) for yy in range(4)]
    for i in range(GH):
        carry = jnp.zeros((HP, N), F32)
        for yy in (3, 2, 1):
            carry = jnp.where(yy > y, sums_of(tt_ref, yy, i) + outer[yy][i] * carry, carry)
        for zz in (3, 2, 1, 0):
            ct_ref[zz, i * HP : (i + 1) * HP, :] = carry.astype(BF)
            if zz:
                carry = sums_of(st_ref, zz, i) + inner[zz][i] * carry
    for k, ref in enumerate((g0_ref, g1_ref, g2_ref, g3_ref)):
        ref[...] = ct_ref[(z + k) & 3]


def local_kernel(u_ref, c_ref, w_in_ref, dy_ref, cum_ref, cumt_ref, h0_ref, dout_ref, skip_ref, core_ref,
                 keep_ref, give_ref, dx_ref, tx_ref, bt_ref, dbt_ref, dct_ref, extra_ref, x_ref, y_ref, sdy_ref, h0t_ref, sum_ref):
    x_ref[...] = dot(u_ref[...], w_in_ref[:, : INNER + N]).astype(BF)
    proj_t = jnp.transpose(x_ref[...])
    bt = proj_t[INNER:, :]
    c_nat = c_ref[...]
    ct = jnp.transpose(c_nat)
    b_nat = x_ref[:, INNER:]
    pair = (SC * DT) * dot(b_nat, c_nat, NT)
    r = lax.broadcasted_iota(jnp.int32, (N, N), 0)
    c = lax.broadcasted_iota(jnp.int32, (N, N), 1)
    causal = r <= c
    cum = cum_ref[...]
    cumt = cumt_ref[...]
    start = jnp.exp(cum)
    tail = DT * jnp.exp(cum[:, T - 1 : T] - cum)
    bt_ref[...] = bt
    h0t_ref[...] = h0_ref[...].astype(BF)
    y_ref[...] = dot(h0t_ref[...], ct)
    skip_sums = []
    a00 = jnp.zeros((N, N), F32)
    a01 = jnp.zeros((N, N), F32)
    a11 = jnp.zeros((N, N), F32)
    zero = jnp.zeros((N, N), BF)
    zrow = jnp.zeros((HP, T), BF)
    for h in range(H):
        lo, hi = h * HP, (h + 1) * HP
        row0, row1 = cum[h : h + 1, :N], cum[h : h + 1, N:]
        col0, col1 = cumt[:N, h : h + 1], cumt[N:, h : h + 1]
        m00 = jnp.exp(jnp.where(causal, row0 - col0, -1e30))
        m01 = jnp.exp(row1 - col0)
        m11 = jnp.exp(jnp.where(causal, row1 - col1, -1e30))
        weights = jnp.concatenate(
            [
                jnp.concatenate([(m00 * pair[:N, :N]).astype(BF), (m01 * pair[:N, N:]).astype(BF)], axis=1),
                jnp.concatenate([zero, (m11 * pair[N:, N:]).astype(BF)], axis=1),
            ],
            axis=0,
        )
        x_h = proj_t[lo:hi, :]
        dy_h = dy_ref[lo:hi, :]
        x_f, dy_f = x_h.astype(F32), dy_h.astype(F32)
        st = start[h : h + 1, :]
        skip = skip_ref[h]
        y_ref[lo:hi, :] = dot(x_h, weights) + SC * st * y_ref[lo:hi, :] + skip * x_f
        dx_ref[lo:hi, :] = dot(dy_h, weights, NT) + skip * dy_f
        sdy_ref[lo:hi, :] = (st * dy_f).astype(BF)
        tx_ref[lo:hi, :] = (tail[h : h + 1, :] * x_f).astype(BF)
        x_pair = x_ref[:, (h // 2) * N : (h // 2 + 1) * N]
        dy_z = jnp.concatenate([dy_h, zrow] if h % 2 == 0 else [zrow, dy_h], axis=0)
        q0 = dot(x_pair[:N, :], dy_z)
        q11 = dot(x_pair[N:, :], dy_z[:, N:])
        a00 += m00 * q0[:, :N]
        a01 += m01 * q0[:, N:]
        a11 += m11 * q11
        skip_sums.append(jnp.sum(x_f * dy_f, keepdims=True))
    core = core_ref[0]
    half = INNER // 2
    mine = pl.ds(pl.multiple_of(core * half, half), half)
    other = pl.ds(pl.multiple_of((1 - core) * half, half), half)
    give_ref[...] = dot(y_ref[other, :].astype(BF), dout_ref[...]).astype(BF)
    keep_ref[...] = dot(y_ref[mine, :].astype(BF), dout_ref[...]).astype(BF)
    sum_ref[:N, :N] = a00.astype(BF)
    sum_ref[:N, N:] = a01.astype(BF)
    sum_ref[N:, :N] = zero
    sum_ref[N:, N:] = a11.astype(BF)
    a = sum_ref[...]
    dct_ref[...] = (SC * (DT * dot(bt, a) + dot(h0t_ref[...], sdy_ref[...], TN))).astype(BF)
    dbt_ref[...] = (DT * SC) * dot(ct, a, NT)
    lane = lax.broadcasted_iota(jnp.int32, (1, T), 1)
    extra = jnp.zeros((1, T), F32)
    for h in range(H):
        whole = skip_sums[h]
        top = whole.astype(BF).astype(F32)
        extra = extra + jnp.where(lane == 128 + h, top, 0.0) + jnp.where(lane == 160 + h, whole - top, 0.0)
    extra_ref[...] = extra


def slot_kernel(index_ref, extra_ref, misc_ref, hits_ref):
    index = index_ref[...]
    owner_row = lax.shift_right_logical(index, 9)
    rr = lax.broadcasted_iota(jnp.int32, (T, T), 0)
    cc = lax.broadcasted_iota(jnp.int32, (T, T), 1)
    index_col = jnp.sum(jnp.where(rr == cc, index.astype(F32), 0.0), axis=1, keepdims=True)
    index_col = index_col.astype(jnp.int32)
    owner_col = lax.shift_right_logical(index_col, 9)
    same = owner_col == owner_row
    rank_row = jnp.sum(jnp.where(same & (rr < cc), 1.0, 0.0), axis=0, keepdims=True).astype(jnp.int32)
    rank_col = jnp.sum(jnp.where(same & (cc < rr), 1.0, 0.0), axis=1, keepdims=True).astype(jnp.int32)
    local_col = index_col - owner_col * ROWS_DEV
    id_hi = lax.shift_right_logical(local_col, 1)
    id_lo = local_col - 2 * id_hi
    v = jnp.where(cc == rank_col, id_hi, jnp.where(cc == rank_col + 64, id_lo, 0))
    row_id = lax.broadcasted_iota(jnp.int32, (8 * DEV, T), 0)
    hits_ref[...] = jnp.where(row_id == owner_row * 8 + 2 + rank_row, 1.0, 0.0).astype(BF)
    heads = jnp.where(row_id == owner_row * 8 + 6, 1.0, 0.0).astype(BF)
    misc = dot(heads, v.astype(F32).astype(BF))
    misc_ref[...] = (misc + jnp.where((row_id & 7) == 6, extra_ref[...], 0.0)).astype(BF)


def finish_kernel(z_ref, c0_ref, c1_ref, c2_ref, c3_ref, outer_ref, bt_ref, cum_ref, tx_ref, dbt_ref, dct_ref,
                  rows_ref, w_up_ref, hits_ref, misc_ref, dx_ref, w_in_ref, out_ref, carry_ref, d_ref):
    out_ref[:, 2 * E :] = outer_ref[...]
    for k, ref in enumerate((c0_ref, c1_ref, c2_ref, c3_ref)):
        carry_ref[pl.ds(pl.multiple_of(((z_ref[0] + 4 - k) & 3) * GR, GR), GR), :] = ref[...]
    cum = cum_ref[...]
    tail = DT * jnp.exp(cum[:, T - 1 : T] - cum)
    carry = carry_ref[...]
    entering = dot(carry, bt_ref[...])
    for h in range(H):
        lo, hi = h * HP, (h + 1) * HP
        d_ref[lo:hi, :] = (dx_ref[lo:hi, :] + tail[h : h + 1, :] * entering[lo:hi, :]).astype(BF)
    d_ref[INNER + N :, :] = dct_ref[...]
    d_ref[INNER : INNER + N, :] = (dbt_ref[...] + dot(carry, tx_ref[...], TN)).astype(BF)
    d = d_ref[...]
    g = dot(d, rows_ref[...]).astype(BF)
    out_ref[:, :E] = g[:INNER, :]
    du = dot(w_in_ref[...], d).astype(BF)
    de = dot(w_up_ref[...], du).astype(BF)
    r = lax.broadcasted_iota(jnp.int32, (8 * DEV, 2 * N), 0)
    j = lax.broadcasted_iota(jnp.int32, (1, 2 * N), 1)
    place = jnp.where(r == 8 * lax.shift_right_logical(j, 1) + (j & 1), 1.0, 0.0).astype(BF)
    misc = misc_ref[...].astype(F32) + dot(hits_ref[...], de, NT) + dot(place, g[INNER:, :])
    out_ref[:, E : 2 * E] = misc.astype(BF)


def pair_kernel(keep_ref, got_ref, tx_ref, out_ref, tx_out_ref):
    tx_out_ref[...] = tx_ref[...]
    total = (keep_ref[...].astype(F32) + got_ref[...].astype(F32)).astype(BF)
    out_ref[: INNER // 2, :] = total[:, :E]
    out_ref[INNER // 2 :, :] = total[:, E:]


def sum_kernel(got_ref, chunk_ref, skip_ref):
    total = jnp.sum(got_ref[:, :, : 2 * E].astype(F32), axis=0)
    side = jnp.concatenate([total[0:2, E : E + N], total[0:2, E + N :], jnp.zeros((4, N), F32)], axis=0)
    outer = got_ref[:, :, 2 * E :].reshape(4, 2, CTX, 8, E)
    halves = [jnp.sum(outer[:, c].reshape(DEV // 2, 8, E).astype(F32), axis=0) for c in range(2)]
    chunk = jnp.concatenate([total[:, :E], side] + halves, axis=1)
    chunk_ref[...] = jnp.broadcast_to(chunk[None], chunk_ref.shape).astype(BF)
    skip_ref[...] = total[6:7, E + 128 : E + 256]


def table_kernel(got_ref, table_ref):
    misc = got_ref[:, :, E : 2 * E]
    ids = misc[:, 6:7, 0:128].astype(F32)
    sub = lax.broadcasted_iota(jnp.int32, (DEV, 8, 128), 1) - 2
    lane = lax.broadcasted_iota(jnp.int32, (DEV, 8, 128), 2)
    want = jnp.where(lane == sub, 2.0, jnp.where(lane == sub + 64, 1.0, 0.0))
    row = jnp.sum(ids * want, axis=2, keepdims=True)
    row = jnp.where((sub[:, :, :1] >= 0) & (sub[:, :, :1] < CAP), row, -1.0)
    rid = lax.broadcasted_iota(jnp.int32, (DEV, 8, ROWS_DEV), 2).astype(F32)
    hits = jnp.where(rid == row, 1.0, 0.0).reshape(DEV * 8, ROWS_DEV).astype(BF)
    table_ref[...] = dot(hits, misc.reshape(DEV * 8, E), TN)


def last_kernel(core_ref, own_ref, other_ref, w_up_ref, w_in_ref, up_ref, in_ref, go_ref, g_ref, side_ref):
    step = pl.program_id(0)
    core = core_ref[0]
    sources = ((core, own_ref), (1 - core, other_ref))

    @pl.when(step == 0)
    def _():
        for x in range(4):
            for at, ref in sources:
                rows = pl.ds(pl.multiple_of((2 * x + at) * N, N), N)
                g_ref[rows, :] = ref[x * N : (x + 1) * N, :E]
                side_ref[rows, :] = ref[x * N : (x + 1) * N, E : E + N]
        j = lax.broadcasted_iota(jnp.int32, (2 * N, 8 * DEV), 0)
        r = lax.broadcasted_iota(jnp.int32, (2 * N, 8 * DEV), 1)
        first = r - (8 * lax.shift_right_logical(j, 1) + (j & 1))
        for m in range(2):
            pick = jnp.where(first == 2 * m, 1.0, 0.0).astype(BF)
            g_ref[INNER:, m * N : (m + 1) * N] = dot(pick, side_ref[...]).astype(BF)

    g = g_ref[...]
    part = pl.ds(pl.multiple_of(step * E, E), E)
    in_ref[...] = lax.dot_general(w_up_ref[:, part], g, (((0,), (1,)), ((), ())), preferred_element_type=F32)
    up_ref[...] = jnp.transpose(dot(w_in_ref[part, :], g))
    lanes = pl.ds(pl.multiple_of(E + N + E * step, N), E)
    for x in range(4):
        for at, ref in sources:
            rows = pl.ds(pl.multiple_of((x & 1) * E + at * N, N), N)
            go_ref[rows, (x >> 1) * E : (x >> 1) * E + E] = ref[x * N : (x + 1) * N, lanes].astype(F32)


def hop(value, axis, step):
    return lax.ppermute(value, axis, [(i, (i + step) % 4) for i in range(4)])


def local(event_rows, event_index, decay, saved_state, dout, w_up, w_in, w_out, skip):
    every = ("x", "core", "y", "z")
    rows, d_out = event_rows[0], dout[0]
    core, y, z = (lax.axis_index(a).reshape(1) for a in ("core", "y", "z"))
    u, c_nat, dy, cum, cumt, *sums = call(
        project_kernel,
        [((T, D), BF), ((T, N), BF), ((INNER, T), BF), ((H, T), F32), ((T, H), F32)] + [((MR, N), BF)] * 4,
        BIG, 750_000_000, 4_500_000,
        in_specs=[SM] + [HBM] * 6, out_specs=(VM,) * 9,
        scratch_shapes=[
            pltpu.VMEM((T, E), BF), pltpu.VMEM((T, D), BF), pltpu.VMEM((H, T), F32),
            pltpu.VMEM((E, D), BF), pltpu.VMEM((D, N), BF), pltpu.VMEM((INNER, D), BF),
            pltpu.VMEM((4, MR, N), BF), pltpu.SemaphoreType.DMA((6,)),
        ],
    )(z, rows, d_out, decay[0], w_up, w_in, w_out)
    sums = sums[:1] + [hop(v, "z", k + 1) for k, v in enumerate(sums[1:])]
    keep, give, dx, tx, bt, dbt, dct, extra = call(
        local_kernel,
        [((INNER // 2, D), BF), ((INNER // 2, D), BF), ((INNER, T), F32), ((INNER, T), BF), ((N, T), BF),
         ((N, T), F32), ((N, T), BF), ((1, T), F32)],
        BIG, 2_500_000_000, 6_000_000,
        in_specs=[VM] * 8 + [SM] * 2, out_specs=(VM,) * 8,
        scratch_shapes=[
            pltpu.VMEM((T, INNER + N), BF),
            pltpu.VMEM((INNER, T), F32), pltpu.VMEM((INNER, T), BF),
            pltpu.VMEM((INNER, N), BF), pltpu.VMEM((T, T), BF),
        ],
    )(u, c_nat, w_in, dy, cum, cumt, jnp.swapaxes(saved_state[0, 0], 1, 2).reshape(INNER, N), d_out, skip, core)
    sums, give = lax.optimization_barrier((sums, give))
    (total,) = call(
        inner_kernel, [((MR, N), BF)], 8, 2_000_000, 400_000,
        in_specs=[SM] + [VM] * 4, out_specs=(VM,), scratch_shapes=[pltpu.VMEM((4, MR, N), BF)],
    )(z, *sums)
    totals = [total] + [hop(total, "y", k) for k in range(1, 4)]
    misc, hits = call(
        slot_kernel, [((8 * DEV, E), BF), ((8 * DEV, T), BF)], 16, 300_000_000, 1_500_000,
        in_specs=[VM] * 2, out_specs=(VM,) * 2,
    )(event_index, extra)
    totals, hits = lax.optimization_barrier((totals, hits))
    carries = call(
        outer_kernel, [((GR, N), BF)] * 4, 8, 4_000_000, 800_000,
        in_specs=[SM] * 2 + [VM] * 8, out_specs=(VM,) * 4,
        scratch_shapes=[pltpu.VMEM((4, MR, N), BF)] * 2 + [pltpu.VMEM((4, GR, N), BF)],
    )(y, z, *sums, *totals)
    carries = [carries[0]] + [hop(v, "z", k + 1) for k, v in enumerate(carries[1:])]
    outer, tx = call(
        pair_kernel, [((8 * DEV, E), BF), ((INNER, T), BF)], 8, 300_000, 3_000_000, in_specs=[VM] * 3, out_specs=(VM,) * 2
    )(keep, lax.ppermute(give, "core", [(0, 1), (1, 0)]), tx)
    carries, outer = lax.optimization_barrier((carries, outer))
    (pay,) = call(
        finish_kernel, [((8 * DEV, 3 * E), BF)], 36, 1_400_000_000, 6_000_000,
        in_specs=[SM] + [VM] * 16, out_specs=(VM,),
        scratch_shapes=[pltpu.VMEM((INNER, N), BF), pltpu.VMEM((PROJ, T), BF)],
    )(z, *carries, outer, bt, cum, tx, dbt, dct, rows, w_up, hits, misc, dx, w_in)
    pay_got = lax.all_to_all(pay.reshape(DEV, 8, 3 * E), every, 0, 0, tiled=True)
    chunk, skip_sum = call(
        sum_kernel, [((DEV // 2, 8, 7 * N), BF), ((1, 128), F32)], 12, 2_000_000, 3_000_000,
        in_specs=[VM], out_specs=(VM,) * 2,
    )(pay_got)
    whole = lax.all_to_all(chunk, ("x", "y", "z"), 0, 0, tiled=True).reshape(DEV * 4, 7 * N)
    other = lax.ppermute(whole, "core", [(0, 1), (1, 0)])
    (table,) = call(
        table_kernel, [((ROWS_DEV, E), F32)], 12, 400_000_000, 2_000_000, in_specs=[VM], out_specs=(VM,)
    )(pay_got)
    column = pl.BlockSpec((E, D // 2), lambda i: (0, i))
    row = pl.BlockSpec((D // 2, PROJ), lambda i: (i, 0))
    grad_up, grad_in, grad_out = pl.pallas_call(
        last_kernel,
        grid=(2,),
        out_shape=tuple(jax.ShapeDtypeStruct(s, F32) for s in ((E, D), (D, PROJ), (INNER, D))),
        in_specs=[SM] + [VM] * 4,
        out_specs=(column, row, pl.BlockSpec((INNER // 2, D), lambda i: (i, 0))),
        scratch_shapes=[pltpu.VMEM((PROJ, E), BF), pltpu.VMEM((8 * DEV, N), BF)],
        compiler_params=pltpu.CompilerParams(vmem_limit_bytes=28 * MB),
        cost_estimate=pl.CostEstimate(flops=700_000_000, bytes_accessed=8_000_000, transcendentals=0),
    )(core, whole, other, w_up, w_in)
    grad_skip = skip_sum[0, :H] + skip_sum[0, 32 : 32 + H]
    return (grad_up, grad_in, grad_out, grad_skip, table)


def solution(mesh):
    mesh = Mesh(mesh.devices.reshape(4, 2, 4, 4), ("x", "core", "y", "z"))
    batch, ctx = ("x", "core"), ("y", "z")
    in_specs = (
        P(batch, ctx, None),
        P(batch, ctx),
        P(batch, None, ctx),
        P(batch, ctx, None, None, None),
        P(batch, ctx, None),
        P(),
        P(),
        P(),
        P(),
    )
    out_specs = (P(), P(), P(), P(), P(batch + ctx, None))
    return jax.shard_map(local, mesh=mesh, in_specs=in_specs, out_specs=out_specs, check_vma=False)
```

```python
from functools import partial

import jax
import jax.numpy as jnp
from jax import lax
from jax.experimental import pallas as pl
from jax.experimental.pallas import tpu as pltpu
from jax.sharding import Mesh, PartitionSpec as P

T = 256
E = 256
D = 512
H = 16
HP = 64
N = 128
INNER = H * HP
PROJ = INNER + 2 * N
ROWS_DEV = 512
CAP = 4
DEV = 128
CTX = 16
GH = 4
GR = GH * HP
MR = GR + 16

DT = 0.0625
SC = 128.0**-0.5
F32 = jnp.float32
BF = jnp.bfloat16
NN = (((1,), (0,)), ((), ()))
NT = (((1,), (1,)), ((), ()))
TN = (((0,), (0,)), ((), ()))
MB = 1 << 20
BIG = 60


def dot(a, b, dims=NN):
    return lax.dot_general(a, b, dims, preferred_element_type=F32)


def split3(v):
    hi = v.astype(BF)
    rest = v - hi.astype(F32)
    mid = rest.astype(BF)
    return hi, mid, (rest - mid.astype(F32)).astype(BF)


def call(kernel, outs, vmem, flops, nbytes, **kw):
    return pl.pallas_call(
        kernel,
        out_shape=tuple(jax.ShapeDtypeStruct(s, d) for s, d in outs),
        compiler_params=pltpu.CompilerParams(vmem_limit_bytes=vmem * MB),
        cost_estimate=pl.CostEstimate(flops=flops, bytes_accessed=nbytes, transcendentals=0),
        **kw,
    )


VM = pl.BlockSpec(memory_space=pltpu.VMEM)
HBM = pl.BlockSpec(memory_space=pltpu.HBM)
SM = pl.BlockSpec(memory_space=pltpu.SMEM)


def decay_rows(amounts):
    row = lax.broadcasted_iota(jnp.int32, (MR - GR, N), 0)
    out = jnp.zeros((MR - GR, N), F32)
    for i, amount in enumerate(amounts):
        for k, part in enumerate(split3(amount)):
            out = jnp.where(row == 3 * i + k, part.astype(F32), out)
    return out.astype(BF)


def decays(ref, at):
    rows = ref[at, GR:, :].astype(F32)
    return [rows[3 * i : 3 * i + 1] + rows[3 * i + 1 : 3 * i + 2] + rows[3 * i + 2 : 3 * i + 3] for i in range(GH)]


def sums_of(ref, at, i):
    return ref[at, i * HP : (i + 1) * HP, :].astype(F32)


def project_kernel(z_ref, rows_hbm, dout_hbm, decay_hbm, w_up_hbm, w_in_hbm, w_out_hbm,
                   u_ref, c_ref, dy_ref, cum_ref, cumt_ref, g0_ref, g1_ref, g2_ref, g3_ref,
                   rows_ref, dout_ref, decay_ref, w_up_ref, w_c_ref, w_out_ref, all_ref, sems):
    pairs = (
        (rows_hbm, rows_ref), (w_up_hbm, w_up_ref), (w_in_hbm.at[:, INNER + N :], w_c_ref),
        (dout_hbm, dout_ref), (w_out_hbm, w_out_ref), (decay_hbm, decay_ref),
    )
    copies = [pltpu.make_async_copy(a, b, sems.at[i]) for i, (a, b) in enumerate(pairs)]
    for copy in copies:
        copy.start()
    copies[0].wait()
    copies[1].wait()
    u_ref[...] = dot(rows_ref[...], w_up_ref[...]).astype(BF)
    copies[2].wait()
    c_ref[...] = dot(u_ref[...], w_c_ref[...]).astype(BF)
    copies[3].wait()
    copies[4].wait()
    dy_ref[...] = dot(w_out_ref[...], dout_ref[...], NT).astype(BF)
    copies[5].wait()
    logs = split3(jnp.log(decay_ref[...]))
    r = lax.broadcasted_iota(jnp.int32, (T, T), 0)
    c = lax.broadcasted_iota(jnp.int32, (T, T), 1)
    upper = (r <= c).astype(F32).astype(BF)
    lower = (c <= r).astype(F32).astype(BF)
    cum = sum(dot(p, upper) for p in logs)
    cum_ref[...] = cum
    cumt_ref[...] = sum(dot(lower, p, NT) for p in logs)
    start = jnp.exp(cum)
    scaled = jnp.concatenate(
        [
            (dy_ref[h * HP : (h + 1) * HP, :].astype(F32) * (SC * start[h : h + 1, :])).astype(BF)
            for h in range(H)
        ],
        axis=0,
    )
    sums = dot(scaled, c_ref[...]).astype(BF)
    amount = jnp.exp(cum[:, T - 1 : T])
    for q in range(H // GH):
        all_ref[q, :GR, :] = sums[q * GR : (q + 1) * GR, :]
        all_ref[q, GR:, :] = decay_rows([jnp.broadcast_to(amount[h : h + 1, :], (1, N)) for h in range(q * GH, (q + 1) * GH)])
    for k, ref in enumerate((g0_ref, g1_ref, g2_ref, g3_ref)):
        ref[...] = all_ref[(z_ref[0] + k) & 3]


def place(at, refs, out_ref):
    for k, ref in enumerate(refs):
        out_ref[(at + 4 - k) & 3] = ref[...]


def inner_kernel(z_ref, a_ref, b_ref, c_ref, d_ref, out_ref, st_ref):
    place(z_ref[0], (a_ref, b_ref, c_ref, d_ref), st_ref)
    amounts = [decays(st_ref, zz) for zz in range(4)]
    for i in range(GH):
        carry = sums_of(st_ref, 3, i)
        for zz in (2, 1, 0):
            carry = sums_of(st_ref, zz, i) + amounts[zz][i] * carry
        out_ref[i * HP : (i + 1) * HP, :] = carry.astype(BF)
    out_ref[GR:, :] = decay_rows([amounts[0][i] * amounts[1][i] * amounts[2][i] * amounts[3][i] for i in range(GH)])


def outer_kernel(y_ref, z_ref, a_ref, b_ref, c_ref, d_ref, ta_ref, tb_ref, tc_ref, td_ref,
                 g0_ref, g1_ref, g2_ref, g3_ref, st_ref, tt_ref, ct_ref):
    y, z = y_ref[0], z_ref[0]
    place(z, (a_ref, b_ref, c_ref, d_ref), st_ref)
    place(y, (ta_ref, tb_ref, tc_ref, td_ref), tt_ref)
    inner = [decays(st_ref, zz) for zz in range(4)]
    outer = [decays(tt_ref, yy) for yy in range(4)]
    for i in range(GH):
        carry = jnp.zeros((HP, N), F32)
        for yy in (3, 2, 1):
            carry = jnp.where(yy > y, sums_of(tt_ref, yy, i) + outer[yy][i] * carry, carry)
        for zz in (3, 2, 1, 0):
            ct_ref[zz, i * HP : (i + 1) * HP, :] = carry.astype(BF)
            if zz:
                carry = sums_of(st_ref, zz, i) + inner[zz][i] * carry
    for k, ref in enumerate((g0_ref, g1_ref, g2_ref, g3_ref)):
        ref[...] = ct_ref[(z + k) & 3]


def local_kernel(u_ref, c_ref, w_in_ref, dy_ref, cum_ref, cumt_ref, h0_ref, dout_ref, skip_ref, core_ref,
                 keep_ref, give_ref, dx_ref, tx_ref, bt_ref, dbt_ref, dct_ref, extra_ref, x_ref, y_ref, sdy_ref, h0t_ref, sum_ref):
    x_ref[...] = dot(u_ref[...], w_in_ref[:, : INNER + N]).astype(BF)
    proj_t = jnp.transpose(x_ref[...])
    bt = proj_t[INNER:, :]
    c_nat = c_ref[...]
    ct = jnp.transpose(c_nat)
    b_nat = x_ref[:, INNER:]
    pair = (SC * DT) * dot(b_nat, c_nat, NT)
    r = lax.broadcasted_iota(jnp.int32, (N, N), 0)
    c = lax.broadcasted_iota(jnp.int32, (N, N), 1)
    causal = r <= c
    cum = cum_ref[...]
    cumt = cumt_ref[...]
    start = jnp.exp(cum)
    tail = DT * jnp.exp(cum[:, T - 1 : T] - cum)
    bt_ref[...] = bt
    h0t_ref[...] = h0_ref[...].astype(BF)
    y_ref[...] = dot(h0t_ref[...], ct)
    skip_sums = []
    a00 = jnp.zeros((N, N), F32)
    a01 = jnp.zeros((N, N), F32)
    a11 = jnp.zeros((N, N), F32)
    zero = jnp.zeros((N, N), BF)
    zrow = jnp.zeros((HP, T), BF)
    for h in range(H):
        lo, hi = h * HP, (h + 1) * HP
        row0, row1 = cum[h : h + 1, :N], cum[h : h + 1, N:]
        col0, col1 = cumt[:N, h : h + 1], cumt[N:, h : h + 1]
        m00 = jnp.exp(jnp.where(causal, row0 - col0, -1e30))
        m01 = jnp.exp(row1 - col0)
        m11 = jnp.exp(jnp.where(causal, row1 - col1, -1e30))
        weights = jnp.concatenate(
            [
                jnp.concatenate([(m00 * pair[:N, :N]).astype(BF), (m01 * pair[:N, N:]).astype(BF)], axis=1),
                jnp.concatenate([zero, (m11 * pair[N:, N:]).astype(BF)], axis=1),
            ],
            axis=0,
        )
        x_h = proj_t[lo:hi, :]
        dy_h = dy_ref[lo:hi, :]
        x_f, dy_f = x_h.astype(F32), dy_h.astype(F32)
        st = start[h : h + 1, :]
        skip = skip_ref[h]
        y_ref[lo:hi, :] = dot(x_h, weights) + SC * st * y_ref[lo:hi, :] + skip * x_f
        dx_ref[lo:hi, :] = (dot(dy_h, weights, NT) + skip * dy_f).astype(BF)
        sdy_ref[lo:hi, :] = (st * dy_f).astype(BF)
        tx_ref[lo:hi, :] = (tail[h : h + 1, :] * x_f).astype(BF)
        x_pair = x_ref[:, (h // 2) * N : (h // 2 + 1) * N]
        dy_z = jnp.concatenate([dy_h, zrow] if h % 2 == 0 else [zrow, dy_h], axis=0)
        q0 = dot(x_pair[:N, :], dy_z)
        q11 = dot(x_pair[N:, :], dy_z[:, N:])
        a00 += m00 * q0[:, :N]
        a01 += m01 * q0[:, N:]
        a11 += m11 * q11
        skip_sums.append(jnp.sum(x_f * dy_f, keepdims=True))
    core = core_ref[0]
    half = INNER // 2
    mine = pl.ds(pl.multiple_of(core * half, half), half)
    other = pl.ds(pl.multiple_of((1 - core) * half, half), half)
    give_ref[...] = dot(y_ref[other, :].astype(BF), dout_ref[...]).astype(BF)
    keep_ref[...] = dot(y_ref[mine, :].astype(BF), dout_ref[...]).astype(BF)
    sum_ref[:N, :N] = a00.astype(BF)
    sum_ref[:N, N:] = a01.astype(BF)
    sum_ref[N:, :N] = zero
    sum_ref[N:, N:] = a11.astype(BF)
    a = sum_ref[...]
    dct_ref[...] = (SC * (DT * dot(bt, a) + dot(h0t_ref[...], sdy_ref[...], TN))).astype(BF)
    dbt_ref[...] = (DT * SC) * dot(ct, a, NT)
    lane = lax.broadcasted_iota(jnp.int32, (1, T), 1)
    extra = jnp.zeros((1, T), F32)
    for h in range(H):
        whole = skip_sums[h]
        top = whole.astype(BF).astype(F32)
        extra = extra + jnp.where(lane == 128 + h, top, 0.0) + jnp.where(lane == 160 + h, whole - top, 0.0)
    extra_ref[...] = extra


def slot_kernel(index_ref, extra_ref, misc_ref, hits_ref):
    index = index_ref[...]
    owner_row = lax.shift_right_logical(index, 9)
    rr = lax.broadcasted_iota(jnp.int32, (T, T), 0)
    cc = lax.broadcasted_iota(jnp.int32, (T, T), 1)
    index_col = jnp.sum(jnp.where(rr == cc, index.astype(F32), 0.0), axis=1, keepdims=True)
    index_col = index_col.astype(jnp.int32)
    owner_col = lax.shift_right_logical(index_col, 9)
    same = owner_col == owner_row
    rank_row = jnp.sum(jnp.where(same & (rr < cc), 1.0, 0.0), axis=0, keepdims=True).astype(jnp.int32)
    rank_col = jnp.sum(jnp.where(same & (cc < rr), 1.0, 0.0), axis=1, keepdims=True).astype(jnp.int32)
    local_col = index_col - owner_col * ROWS_DEV
    id_hi = lax.shift_right_logical(local_col, 1)
    id_lo = local_col - 2 * id_hi
    v = jnp.where(cc == rank_col, id_hi, jnp.where(cc == rank_col + 64, id_lo, 0))
    row_id = lax.broadcasted_iota(jnp.int32, (8 * DEV, T), 0)
    hits_ref[...] = jnp.where(row_id == owner_row * 8 + 2 + rank_row, 1.0, 0.0).astype(BF)
    heads = jnp.where(row_id == owner_row * 8 + 6, 1.0, 0.0).astype(BF)
    misc = dot(heads, v.astype(F32).astype(BF))
    misc_ref[...] = (misc + jnp.where((row_id & 7) == 6, extra_ref[...], 0.0)).astype(BF)


def finish_kernel(z_ref, c0_ref, c1_ref, c2_ref, c3_ref, outer_ref, bt_ref, cum_ref, tx_ref, dbt_ref, dct_ref,
                  rows_ref, w_up_ref, hits_ref, misc_ref, dx_ref, w_in_ref, out_ref, carry_ref, d_ref):
    out_ref[:, 2 * E :] = outer_ref[...]
    for k, ref in enumerate((c0_ref, c1_ref, c2_ref, c3_ref)):
        carry_ref[pl.ds(pl.multiple_of(((z_ref[0] + 4 - k) & 3) * GR, GR), GR), :] = ref[...]
    cum = cum_ref[...]
    tail = DT * jnp.exp(cum[:, T - 1 : T] - cum)
    carry = carry_ref[...]
    entering = dot(carry, bt_ref[...])
    for h in range(H):
        lo, hi = h * HP, (h + 1) * HP
        d_ref[lo:hi, :] = (dx_ref[lo:hi, :].astype(F32) + tail[h : h + 1, :] * entering[lo:hi, :]).astype(BF)
    d_ref[INNER + N :, :] = dct_ref[...]
    d_ref[INNER : INNER + N, :] = (dbt_ref[...] + dot(carry, tx_ref[...], TN)).astype(BF)
    d = d_ref[...]
    g = dot(d, rows_ref[...]).astype(BF)
    out_ref[:, :E] = g[:INNER, :]
    du = dot(w_in_ref[...], d).astype(BF)
    de = dot(w_up_ref[...], du).astype(BF)
    r = lax.broadcasted_iota(jnp.int32, (8 * DEV, 2 * N), 0)
    j = lax.broadcasted_iota(jnp.int32, (1, 2 * N), 1)
    place = jnp.where(r == 8 * lax.shift_right_logical(j, 1) + (j & 1), 1.0, 0.0).astype(BF)
    misc = misc_ref[...].astype(F32) + dot(hits_ref[...], de, NT) + dot(place, g[INNER:, :])
    out_ref[:, E : 2 * E] = misc.astype(BF)


def pair_kernel(keep_ref, got_ref, tx_ref, out_ref, tx_out_ref):
    tx_out_ref[...] = tx_ref[...]
    total = (keep_ref[...].astype(F32) + got_ref[...].astype(F32)).astype(BF)
    out_ref[: INNER // 2, :] = total[:, :E]
    out_ref[INNER // 2 :, :] = total[:, E:]


def sum_kernel(got_ref, chunk_ref, skip_ref):
    total = jnp.sum(got_ref[:, :, : 2 * E].astype(F32), axis=0)
    side = jnp.concatenate([total[0:2, E : E + N], total[0:2, E + N :], jnp.zeros((4, N), F32)], axis=0)
    outer = got_ref[:, :, 2 * E :].reshape(4, 2, CTX, 8, E)
    halves = [jnp.sum(outer[:, c].reshape(DEV // 2, 8, E).astype(F32), axis=0) for c in range(2)]
    chunk = jnp.concatenate([total[:, :E], side] + halves, axis=1)
    chunk_ref[...] = jnp.broadcast_to(chunk[None], chunk_ref.shape).astype(BF)
    skip_row = total[6:7, E + 128 : E + 256]
    skip_ref[...] = skip_row[:, :H] + skip_row[:, 32 : 32 + H]


def table_kernel(got_ref, table_ref):
    misc = got_ref[:, :, E : 2 * E]
    ids = misc[:, 6:7, 0:128].astype(F32)
    sub = lax.broadcasted_iota(jnp.int32, (DEV, 8, 128), 1) - 2
    lane = lax.broadcasted_iota(jnp.int32, (DEV, 8, 128), 2)
    want = jnp.where(lane == sub, 2.0, jnp.where(lane == sub + 64, 1.0, 0.0))
    row = jnp.sum(ids * want, axis=2, keepdims=True)
    row = jnp.where((sub[:, :, :1] >= 0) & (sub[:, :, :1] < CAP), row, -1.0)
    rid = lax.broadcasted_iota(jnp.int32, (DEV, 8, ROWS_DEV), 2).astype(F32)
    hits = jnp.where(rid == row, 1.0, 0.0).reshape(DEV * 8, ROWS_DEV).astype(BF)
    table_ref[...] = dot(hits, misc.reshape(DEV * 8, E), TN)


def last_kernel(core_ref, own_ref, other_ref, w_up_ref, w_in_ref, up_ref, in_ref, go_ref, g_ref, side_ref):
    step = pl.program_id(0)
    core = core_ref[0]
    sources = ((core, own_ref), (1 - core, other_ref))

    @pl.when(step == 0)
    def _():
        for x in range(4):
            for at, ref in sources:
                rows = pl.ds(pl.multiple_of((2 * x + at) * N, N), N)
                g_ref[rows, :] = ref[x * N : (x + 1) * N, :E]
                side_ref[rows, :] = ref[x * N : (x + 1) * N, E : E + N]
        j = lax.broadcasted_iota(jnp.int32, (2 * N, 8 * DEV), 0)
        r = lax.broadcasted_iota(jnp.int32, (2 * N, 8 * DEV), 1)
        first = r - (8 * lax.shift_right_logical(j, 1) + (j & 1))
        for m in range(2):
            pick = jnp.where(first == 2 * m, 1.0, 0.0).astype(BF)
            g_ref[INNER:, m * N : (m + 1) * N] = dot(pick, side_ref[...]).astype(BF)

    g = g_ref[...]
    part = pl.ds(pl.multiple_of(step * E, E), E)
    in_ref[...] = lax.dot_general(w_up_ref[:, part], g, (((0,), (1,)), ((), ())), preferred_element_type=F32)
    up_ref[...] = jnp.transpose(dot(w_in_ref[part, :], g))
    lanes = pl.ds(pl.multiple_of(E + N + E * step, N), E)
    for x in range(4):
        for at, ref in sources:
            rows = pl.ds(pl.multiple_of((x & 1) * E + at * N, N), N)
            go_ref[rows, (x >> 1) * E : (x >> 1) * E + E] = ref[x * N : (x + 1) * N, lanes].astype(F32)


def hop(value, axis, step):
    return lax.ppermute(value, axis, [(i, (i + step) % 4) for i in range(4)])


def local(event_rows, event_index, decay, saved_state, dout, w_up, w_in, w_out, skip):
    every = ("x", "core", "y", "z")
    rows, d_out = event_rows[0], dout[0]
    core, y, z = (lax.axis_index(a).reshape(1) for a in ("core", "y", "z"))
    u, c_nat, dy, cum, cumt, *sums = call(
        project_kernel,
        [((T, D), BF), ((T, N), BF), ((INNER, T), BF), ((H, T), F32), ((T, H), F32)] + [((MR, N), BF)] * 4,
        BIG, 750_000_000, 4_500_000,
        in_specs=[SM] + [HBM] * 6, out_specs=(VM,) * 9,
        scratch_shapes=[
            pltpu.VMEM((T, E), BF), pltpu.VMEM((T, D), BF), pltpu.VMEM((H, T), F32),
            pltpu.VMEM((E, D), BF), pltpu.VMEM((D, N), BF), pltpu.VMEM((INNER, D), BF),
            pltpu.VMEM((4, MR, N), BF), pltpu.SemaphoreType.DMA((6,)),
        ],
    )(z, rows, d_out, decay[0], w_up, w_in, w_out)
    sums = sums[:1] + [hop(v, "z", k + 1) for k, v in enumerate(sums[1:])]
    keep, give, dx, tx, bt, dbt, dct, extra = call(
        local_kernel,
        [((INNER // 2, D), BF), ((INNER // 2, D), BF), ((INNER, T), BF), ((INNER, T), BF), ((N, T), BF),
         ((N, T), F32), ((N, T), BF), ((1, T), F32)],
        BIG, 2_500_000_000, 6_000_000,
        in_specs=[VM] * 8 + [SM] * 2, out_specs=(VM,) * 8,
        scratch_shapes=[
            pltpu.VMEM((T, INNER + N), BF),
            pltpu.VMEM((INNER, T), F32), pltpu.VMEM((INNER, T), BF),
            pltpu.VMEM((INNER, N), BF), pltpu.VMEM((T, T), BF),
        ],
    )(u, c_nat, w_in, dy, cum, cumt, jnp.swapaxes(saved_state[0, 0], 1, 2).reshape(INNER, N), d_out, skip, core)
    sums, give = lax.optimization_barrier((sums, give))
    (total,) = call(
        inner_kernel, [((MR, N), BF)], 8, 2_000_000, 400_000,
        in_specs=[SM] + [VM] * 4, out_specs=(VM,), scratch_shapes=[pltpu.VMEM((4, MR, N), BF)],
    )(z, *sums)
    totals = [total] + [hop(total, "y", k) for k in range(1, 4)]
    misc, hits = call(
        slot_kernel, [((8 * DEV, E), BF), ((8 * DEV, T), BF)], 16, 300_000_000, 1_500_000,
        in_specs=[VM] * 2, out_specs=(VM,) * 2,
    )(event_index, extra)
    totals, hits = lax.optimization_barrier((totals, hits))
    carries = call(
        outer_kernel, [((GR, N), BF)] * 4, 8, 4_000_000, 800_000,
        in_specs=[SM] * 2 + [VM] * 8, out_specs=(VM,) * 4,
        scratch_shapes=[pltpu.VMEM((4, MR, N), BF)] * 2 + [pltpu.VMEM((4, GR, N), BF)],
    )(y, z, *sums, *totals)
    carries = [carries[0]] + [hop(v, "z", k + 1) for k, v in enumerate(carries[1:])]
    outer, tx = call(
        pair_kernel, [((8 * DEV, E), BF), ((INNER, T), BF)], 8, 300_000, 3_000_000, in_specs=[VM] * 3, out_specs=(VM,) * 2
    )(keep, lax.ppermute(give, "core", [(0, 1), (1, 0)]), tx)
    carries, outer = lax.optimization_barrier((carries, outer))
    (pay,) = call(
        finish_kernel, [((8 * DEV, 3 * E), BF)], 36, 1_400_000_000, 6_000_000,
        in_specs=[SM] + [VM] * 16, out_specs=(VM,),
        scratch_shapes=[pltpu.VMEM((INNER, N), BF), pltpu.VMEM((PROJ, T), BF)],
    )(z, *carries, outer, bt, cum, tx, dbt, dct, rows, w_up, hits, misc, dx, w_in)
    pay_got = lax.all_to_all(pay.reshape(DEV, 8, 3 * E), every, 0, 0, tiled=True)
    chunk, skip_sum = call(
        sum_kernel, [((DEV // 2, 8, 7 * N), BF), ((1, H), F32)], 12, 2_000_000, 3_000_000,
        in_specs=[VM], out_specs=(VM,) * 2,
    )(pay_got)
    whole = lax.all_to_all(chunk, ("x", "y", "z"), 0, 0, tiled=True).reshape(DEV * 4, 7 * N)
    other = lax.ppermute(whole, "core", [(0, 1), (1, 0)])
    (table,) = call(
        table_kernel, [((ROWS_DEV, E), F32)], 12, 400_000_000, 2_000_000, in_specs=[VM], out_specs=(VM,)
    )(pay_got)
    column = pl.BlockSpec((E, D // 2), lambda i: (0, i))
    row = pl.BlockSpec((D // 2, PROJ), lambda i: (i, 0))
    grad_up, grad_in, grad_out = pl.pallas_call(
        last_kernel,
        grid=(2,),
        out_shape=tuple(jax.ShapeDtypeStruct(s, F32) for s in ((E, D), (D, PROJ), (INNER, D))),
        in_specs=[SM] + [VM] * 4,
        out_specs=(column, row, pl.BlockSpec((INNER // 2, D), lambda i: (i, 0))),
        scratch_shapes=[pltpu.VMEM((PROJ, E), BF), pltpu.VMEM((8 * DEV, N), BF)],
        compiler_params=pltpu.CompilerParams(vmem_limit_bytes=28 * MB),
        cost_estimate=pl.CostEstimate(flops=700_000_000, bytes_accessed=8_000_000, transcendentals=0),
    )(core, whole, other, w_up, w_in)
    grad_skip = skip_sum.reshape(H)
    return (grad_up, grad_in, grad_out, grad_skip, table)


def solution(mesh):
    mesh = Mesh(mesh.devices.reshape(4, 2, 4, 4), ("x", "core", "y", "z"))
    batch, ctx = ("x", "core"), ("y", "z")
    in_specs = (
        P(batch, ctx, None),
        P(batch, ctx),
        P(batch, None, ctx),
        P(batch, ctx, None, None, None),
        P(batch, ctx, None),
        P(),
        P(),
        P(),
        P(),
    )
    out_specs = (P(), P(), P(), P(), P(batch + ctx, None))
    return jax.shard_map(local, mesh=mesh, in_specs=in_specs, out_specs=out_specs, check_vma=False)
```

```python
from functools import partial

import jax
import jax.numpy as jnp
from jax import lax
from jax.experimental import pallas as pl
from jax.experimental.pallas import tpu as pltpu
from jax.sharding import Mesh, PartitionSpec as P

T = 256
E = 256
D = 512
H = 16
HP = 64
N = 128
INNER = H * HP
PROJ = INNER + 2 * N
ROWS_DEV = 512
CAP = 4
DEV = 128
CTX = 16
GH = 4
GR = GH * HP
MR = GR + 16

DT = 0.0625
SC = 128.0**-0.5
F32 = jnp.float32
BF = jnp.bfloat16
NN = (((1,), (0,)), ((), ()))
NT = (((1,), (1,)), ((), ()))
TN = (((0,), (0,)), ((), ()))
MB = 1 << 20
BIG = 60


def dot(a, b, dims=NN):
    return lax.dot_general(a, b, dims, preferred_element_type=F32)


def split3(v):
    hi = v.astype(BF)
    rest = v - hi.astype(F32)
    mid = rest.astype(BF)
    return hi, mid, (rest - mid.astype(F32)).astype(BF)


def call(kernel, outs, vmem, flops, nbytes, **kw):
    return pl.pallas_call(
        kernel,
        out_shape=tuple(jax.ShapeDtypeStruct(s, d) for s, d in outs),
        compiler_params=pltpu.CompilerParams(vmem_limit_bytes=vmem * MB),
        cost_estimate=pl.CostEstimate(flops=flops, bytes_accessed=nbytes, transcendentals=0),
        **kw,
    )


VM = pl.BlockSpec(memory_space=pltpu.VMEM)
HBM = pl.BlockSpec(memory_space=pltpu.HBM)
SM = pl.BlockSpec(memory_space=pltpu.SMEM)


def decay_rows(amounts):
    row = lax.broadcasted_iota(jnp.int32, (MR - GR, N), 0)
    out = jnp.zeros((MR - GR, N), F32)
    for i, amount in enumerate(amounts):
        for k, part in enumerate(split3(amount)):
            out = jnp.where(row == 3 * i + k, part.astype(F32), out)
    return out.astype(BF)


def decays(ref, at):
    rows = ref[at, GR:, :].astype(F32)
    return [rows[3 * i : 3 * i + 1] + rows[3 * i + 1 : 3 * i + 2] + rows[3 * i + 2 : 3 * i + 3] for i in range(GH)]


def sums_of(ref, at, i):
    return ref[at, i * HP : (i + 1) * HP, :].astype(F32)


def project_kernel(z_ref, rows_hbm, dout_hbm, decay_hbm, w_up_hbm, w_in_hbm, w_out_hbm,
                   u_ref, c_ref, dy_ref, cum_ref, cumt_ref, g0_ref, g1_ref, g2_ref, g3_ref,
                   rows_ref, dout_ref, decay_ref, w_up_ref, w_c_ref, w_out_ref, all_ref, sems):
    pairs = (
        (rows_hbm, rows_ref), (w_up_hbm, w_up_ref), (w_in_hbm.at[:, INNER + N :], w_c_ref),
        (dout_hbm, dout_ref), (w_out_hbm, w_out_ref), (decay_hbm, decay_ref),
    )
    copies = [pltpu.make_async_copy(a, b, sems.at[i]) for i, (a, b) in enumerate(pairs)]
    for copy in copies:
        copy.start()
    copies[0].wait()
    copies[1].wait()
    u_ref[...] = dot(rows_ref[...], w_up_ref[...]).astype(BF)
    copies[2].wait()
    c_ref[...] = dot(u_ref[...], w_c_ref[...]).astype(BF)
    copies[3].wait()
    copies[4].wait()
    dy_ref[...] = dot(w_out_ref[...], dout_ref[...], NT).astype(BF)
    copies[5].wait()
    logs = split3(jnp.log(decay_ref[...]))
    r = lax.broadcasted_iota(jnp.int32, (T, T), 0)
    c = lax.broadcasted_iota(jnp.int32, (T, T), 1)
    upper = (r <= c).astype(F32).astype(BF)
    lower = (c <= r).astype(F32).astype(BF)
    cum = sum(dot(p, upper) for p in logs)
    cum_ref[...] = cum
    cumt_ref[...] = sum(dot(lower, p, NT) for p in logs)
    start = jnp.exp(cum)
    scaled = jnp.concatenate(
        [
            (dy_ref[h * HP : (h + 1) * HP, :].astype(F32) * (SC * start[h : h + 1, :])).astype(BF)
            for h in range(H)
        ],
        axis=0,
    )
    sums = dot(scaled, c_ref[...]).astype(BF)
    amount = jnp.exp(cum[:, T - 1 : T])
    for q in range(H // GH):
        all_ref[q, :GR, :] = sums[q * GR : (q + 1) * GR, :]
        all_ref[q, GR:, :] = decay_rows([jnp.broadcast_to(amount[h : h + 1, :], (1, N)) for h in range(q * GH, (q + 1) * GH)])
    for k, ref in enumerate((g0_ref, g1_ref, g2_ref, g3_ref)):
        ref[...] = all_ref[(z_ref[0] + k) & 3]


def place(at, refs, out_ref):
    for k, ref in enumerate(refs):
        out_ref[(at + 4 - k) & 3] = ref[...]


def inner_kernel(z_ref, a_ref, b_ref, c_ref, d_ref, out_ref, st_ref):
    place(z_ref[0], (a_ref, b_ref, c_ref, d_ref), st_ref)
    amounts = [decays(st_ref, zz) for zz in range(4)]
    for i in range(GH):
        carry = sums_of(st_ref, 3, i)
        for zz in (2, 1, 0):
            carry = sums_of(st_ref, zz, i) + amounts[zz][i] * carry
        out_ref[i * HP : (i + 1) * HP, :] = carry.astype(BF)
    out_ref[GR:, :] = decay_rows([amounts[0][i] * amounts[1][i] * amounts[2][i] * amounts[3][i] for i in range(GH)])


def outer_kernel(y_ref, z_ref, a_ref, b_ref, c_ref, d_ref, ta_ref, tb_ref, tc_ref, td_ref,
                 g0_ref, g1_ref, g2_ref, g3_ref, st_ref, tt_ref, ct_ref):
    y, z = y_ref[0], z_ref[0]
    place(z, (a_ref, b_ref, c_ref, d_ref), st_ref)
    place(y, (ta_ref, tb_ref, tc_ref, td_ref), tt_ref)
    inner = [decays(st_ref, zz) for zz in range(4)]
    outer = [decays(tt_ref, yy) for yy in range(4)]
    for i in range(GH):
        carry = jnp.zeros((HP, N), F32)
        for yy in (3, 2, 1):
            carry = jnp.where(yy > y, sums_of(tt_ref, yy, i) + outer[yy][i] * carry, carry)
        for zz in (3, 2, 1, 0):
            ct_ref[zz, i * HP : (i + 1) * HP, :] = carry.astype(BF)
            if zz:
                carry = sums_of(st_ref, zz, i) + inner[zz][i] * carry
    for k, ref in enumerate((g0_ref, g1_ref, g2_ref, g3_ref)):
        ref[...] = ct_ref[(z + k) & 3]


def local_kernel(u_ref, c_ref, w_in_ref, dy_ref, cum_ref, cumt_ref, h0_ref, skip_ref,
                 yt_ref, dx_ref, tx_ref, bt_ref, dbt_ref, dct_ref, extra_ref, x_ref, y_ref, sdy_ref, h0t_ref, sum_ref):
    x_ref[...] = dot(u_ref[...], w_in_ref[:, : INNER + N]).astype(BF)
    proj_t = jnp.transpose(x_ref[...])
    bt = proj_t[INNER:, :]
    c_nat = c_ref[...]
    ct = jnp.transpose(c_nat)
    b_nat = x_ref[:, INNER:]
    pair = (SC * DT) * dot(b_nat, c_nat, NT)
    r = lax.broadcasted_iota(jnp.int32, (N, N), 0)
    c = lax.broadcasted_iota(jnp.int32, (N, N), 1)
    causal = r <= c
    cum = cum_ref[...]
    cumt = cumt_ref[...]
    start = jnp.exp(cum)
    tail = DT * jnp.exp(cum[:, T - 1 : T] - cum)
    bt_ref[...] = bt
    h0t_ref[...] = h0_ref[...].astype(BF)
    y_ref[...] = dot(h0t_ref[...], ct)
    skip_sums = []
    a00 = jnp.zeros((N, N), F32)
    a01 = jnp.zeros((N, N), F32)
    a11 = jnp.zeros((N, N), F32)
    zero = jnp.zeros((N, N), BF)
    zrow = jnp.zeros((HP, T), BF)
    for h in range(H):
        lo, hi = h * HP, (h + 1) * HP
        row0, row1 = cum[h : h + 1, :N], cum[h : h + 1, N:]
        col0, col1 = cumt[:N, h : h + 1], cumt[N:, h : h + 1]
        m00 = jnp.exp(jnp.where(causal, row0 - col0, -1e30))
        m01 = jnp.exp(row1 - col0)
        m11 = jnp.exp(jnp.where(causal, row1 - col1, -1e30))
        weights = jnp.concatenate(
            [
                jnp.concatenate([(m00 * pair[:N, :N]).astype(BF), (m01 * pair[:N, N:]).astype(BF)], axis=1),
                jnp.concatenate([zero, (m11 * pair[N:, N:]).astype(BF)], axis=1),
            ],
            axis=0,
        )
        x_h = proj_t[lo:hi, :]
        dy_h = dy_ref[lo:hi, :]
        x_f, dy_f = x_h.astype(F32), dy_h.astype(F32)
        st = start[h : h + 1, :]
        skip = skip_ref[h]
        y_ref[lo:hi, :] = dot(x_h, weights) + SC * st * y_ref[lo:hi, :] + skip * x_f
        dx_ref[lo:hi, :] = (dot(dy_h, weights, NT) + skip * dy_f).astype(BF)
        sdy_ref[lo:hi, :] = (st * dy_f).astype(BF)
        tx_ref[lo:hi, :] = (tail[h : h + 1, :] * x_f).astype(BF)
        x_pair = x_ref[:, (h // 2) * N : (h // 2 + 1) * N]
        dy_z = jnp.concatenate([dy_h, zrow] if h % 2 == 0 else [zrow, dy_h], axis=0)
        q0 = dot(x_pair[:N, :], dy_z)
        q11 = dot(x_pair[N:, :], dy_z[:, N:])
        a00 += m00 * q0[:, :N]
        a01 += m01 * q0[:, N:]
        a11 += m11 * q11
        skip_sums.append(jnp.sum(x_f * dy_f, keepdims=True))
    yt_ref[...] = y_ref[...].astype(BF)
    sum_ref[:N, :N] = a00.astype(BF)
    sum_ref[:N, N:] = a01.astype(BF)
    sum_ref[N:, :N] = zero
    sum_ref[N:, N:] = a11.astype(BF)
    a = sum_ref[...]
    dct_ref[...] = (SC * (DT * dot(bt, a) + dot(h0t_ref[...], sdy_ref[...], TN))).astype(BF)
    dbt_ref[...] = (DT * SC) * dot(ct, a, NT)
    lane = lax.broadcasted_iota(jnp.int32, (1, T), 1)
    extra = jnp.zeros((1, T), F32)
    for h in range(H):
        whole = skip_sums[h]
        top = whole.astype(BF).astype(F32)
        extra = extra + jnp.where(lane == 128 + h, top, 0.0) + jnp.where(lane == 160 + h, whole - top, 0.0)
    extra_ref[...] = extra


def out_kernel(core_ref, y_ref, dout_ref, keep_ref, give_ref):
    core = core_ref[0]
    half = INNER // 2
    mine = pl.ds(pl.multiple_of(core * half, half), half)
    other = pl.ds(pl.multiple_of((1 - core) * half, half), half)
    give_ref[...] = dot(y_ref[other, :], dout_ref[...]).astype(BF)
    keep_ref[...] = dot(y_ref[mine, :], dout_ref[...]).astype(BF)


def slot_kernel(index_ref, extra_ref, misc_ref, hits_ref):
    index = index_ref[...]
    owner_row = lax.shift_right_logical(index, 9)
    rr = lax.broadcasted_iota(jnp.int32, (T, T), 0)
    cc = lax.broadcasted_iota(jnp.int32, (T, T), 1)
    index_col = jnp.sum(jnp.where(rr == cc, index.astype(F32), 0.0), axis=1, keepdims=True)
    index_col = index_col.astype(jnp.int32)
    owner_col = lax.shift_right_logical(index_col, 9)
    same = owner_col == owner_row
    rank_row = jnp.sum(jnp.where(same & (rr < cc), 1.0, 0.0), axis=0, keepdims=True).astype(jnp.int32)
    rank_col = jnp.sum(jnp.where(same & (cc < rr), 1.0, 0.0), axis=1, keepdims=True).astype(jnp.int32)
    local_col = index_col - owner_col * ROWS_DEV
    id_hi = lax.shift_right_logical(local_col, 1)
    id_lo = local_col - 2 * id_hi
    v = jnp.where(cc == rank_col, id_hi, jnp.where(cc == rank_col + 64, id_lo, 0))
    row_id = lax.broadcasted_iota(jnp.int32, (8 * DEV, T), 0)
    hits_ref[...] = jnp.where(row_id == owner_row * 8 + 2 + rank_row, 1.0, 0.0).astype(BF)
    heads = jnp.where(row_id == owner_row * 8 + 6, 1.0, 0.0).astype(BF)
    misc = dot(heads, v.astype(F32).astype(BF))
    misc_ref[...] = (misc + jnp.where((row_id & 7) == 6, extra_ref[...], 0.0)).astype(BF)


def finish_kernel(z_ref, c0_ref, c1_ref, c2_ref, c3_ref, outer_ref, bt_ref, cum_ref, tx_ref, dbt_ref, dct_ref,
                  rows_ref, w_up_ref, hits_ref, misc_ref, dx_ref, w_in_ref, out_ref, carry_ref, d_ref):
    out_ref[:, 2 * E :] = outer_ref[...]
    for k, ref in enumerate((c0_ref, c1_ref, c2_ref, c3_ref)):
        carry_ref[pl.ds(pl.multiple_of(((z_ref[0] + 4 - k) & 3) * GR, GR), GR), :] = ref[...]
    cum = cum_ref[...]
    tail = DT * jnp.exp(cum[:, T - 1 : T] - cum)
    carry = carry_ref[...]
    entering = dot(carry, bt_ref[...])
    for h in range(H):
        lo, hi = h * HP, (h + 1) * HP
        d_ref[lo:hi, :] = (dx_ref[lo:hi, :].astype(F32) + tail[h : h + 1, :] * entering[lo:hi, :]).astype(BF)
    d_ref[INNER + N :, :] = dct_ref[...]
    d_ref[INNER : INNER + N, :] = (dbt_ref[...] + dot(carry, tx_ref[...], TN)).astype(BF)
    d = d_ref[...]
    g = dot(d, rows_ref[...]).astype(BF)
    out_ref[:, :E] = g[:INNER, :]
    du = dot(w_in_ref[...], d).astype(BF)
    de = dot(w_up_ref[...], du).astype(BF)
    r = lax.broadcasted_iota(jnp.int32, (8 * DEV, 2 * N), 0)
    j = lax.broadcasted_iota(jnp.int32, (1, 2 * N), 1)
    place = jnp.where(r == 8 * lax.shift_right_logical(j, 1) + (j & 1), 1.0, 0.0).astype(BF)
    misc = misc_ref[...].astype(F32) + dot(hits_ref[...], de, NT) + dot(place, g[INNER:, :])
    out_ref[:, E : 2 * E] = misc.astype(BF)


def pair_kernel(keep_ref, got_ref, tx_ref, out_ref, tx_out_ref):
    tx_out_ref[...] = tx_ref[...]
    total = (keep_ref[...].astype(F32) + got_ref[...].astype(F32)).astype(BF)
    out_ref[: INNER // 2, :] = total[:, :E]
    out_ref[INNER // 2 :, :] = total[:, E:]


def sum_kernel(got_ref, chunk_ref, skip_ref):
    total = jnp.sum(got_ref[:, :, : 2 * E].astype(F32), axis=0)
    side = jnp.concatenate([total[0:2, E : E + N], total[0:2, E + N :], jnp.zeros((4, N), F32)], axis=0)
    outer = got_ref[:, :, 2 * E :].reshape(4, 2, CTX, 8, E)
    halves = [jnp.sum(outer[:, c].reshape(DEV // 2, 8, E).astype(F32), axis=0) for c in range(2)]
    chunk = jnp.concatenate([total[:, :E], side] + halves, axis=1)
    chunk_ref[...] = jnp.broadcast_to(chunk[None], chunk_ref.shape).astype(BF)
    skip_ref[...] = total[6:7, E + 128 : E + 256]


def table_kernel(got_ref, table_ref):
    misc = got_ref[:, :, E : 2 * E]
    ids = misc[:, 6:7, 0:128].astype(F32)
    sub = lax.broadcasted_iota(jnp.int32, (DEV, 8, 128), 1) - 2
    lane = lax.broadcasted_iota(jnp.int32, (DEV, 8, 128), 2)
    want = jnp.where(lane == sub, 2.0, jnp.where(lane == sub + 64, 1.0, 0.0))
    row = jnp.sum(ids * want, axis=2, keepdims=True)
    row = jnp.where((sub[:, :, :1] >= 0) & (sub[:, :, :1] < CAP), row, -1.0)
    rid = lax.broadcasted_iota(jnp.int32, (DEV, 8, ROWS_DEV), 2).astype(F32)
    hits = jnp.where(rid == row, 1.0, 0.0).reshape(DEV * 8, ROWS_DEV).astype(BF)
    table_ref[...] = dot(hits, misc.reshape(DEV * 8, E), TN)


def last_kernel(core_ref, own_ref, other_ref, w_up_ref, w_in_ref, up_ref, in_ref, go_ref, g_ref, side_ref):
    step = pl.program_id(0)
    core = core_ref[0]
    sources = ((core, own_ref), (1 - core, other_ref))

    @pl.when(step == 0)
    def _():
        for x in range(4):
            for at, ref in sources:
                rows = pl.ds(pl.multiple_of((2 * x + at) * N, N), N)
                g_ref[rows, :] = ref[x * N : (x + 1) * N, :E]
                side_ref[rows, :] = ref[x * N : (x + 1) * N, E : E + N]
        j = lax.broadcasted_iota(jnp.int32, (2 * N, 8 * DEV), 0)
        r = lax.broadcasted_iota(jnp.int32, (2 * N, 8 * DEV), 1)
        first = r - (8 * lax.shift_right_logical(j, 1) + (j & 1))
        for m in range(2):
            pick = jnp.where(first == 2 * m, 1.0, 0.0).astype(BF)
            g_ref[INNER:, m * N : (m + 1) * N] = dot(pick, side_ref[...]).astype(BF)

    g = g_ref[...]
    part = pl.ds(pl.multiple_of(step * E, E), E)
    in_ref[...] = lax.dot_general(w_up_ref[:, part], g, (((0,), (1,)), ((), ())), preferred_element_type=F32)
    up_ref[...] = jnp.transpose(dot(w_in_ref[part, :], g))
    lanes = pl.ds(pl.multiple_of(E + N + E * step, N), E)
    for x in range(4):
        for at, ref in sources:
            rows = pl.ds(pl.multiple_of((x & 1) * E + at * N, N), N)
            go_ref[rows, (x >> 1) * E : (x >> 1) * E + E] = ref[x * N : (x + 1) * N, lanes].astype(F32)


def hop(value, axis, step):
    return lax.ppermute(value, axis, [(i, (i + step) % 4) for i in range(4)])


def local(event_rows, event_index, decay, saved_state, dout, w_up, w_in, w_out, skip):
    every = ("x", "core", "y", "z")
    rows, d_out = event_rows[0], dout[0]
    core, y, z = (lax.axis_index(a).reshape(1) for a in ("core", "y", "z"))
    u, c_nat, dy, cum, cumt, *sums = call(
        project_kernel,
        [((T, D), BF), ((T, N), BF), ((INNER, T), BF), ((H, T), F32), ((T, H), F32)] + [((MR, N), BF)] * 4,
        BIG, 750_000_000, 4_500_000,
        in_specs=[SM] + [HBM] * 6, out_specs=(VM,) * 9,
        scratch_shapes=[
            pltpu.VMEM((T, E), BF), pltpu.VMEM((T, D), BF), pltpu.VMEM((H, T), F32),
            pltpu.VMEM((E, D), BF), pltpu.VMEM((D, N), BF), pltpu.VMEM((INNER, D), BF),
            pltpu.VMEM((4, MR, N), BF), pltpu.SemaphoreType.DMA((6,)),
        ],
    )(z, rows, d_out, decay[0], w_up, w_in, w_out)
    sums = sums[:1] + [hop(v, "z", k + 1) for k, v in enumerate(sums[1:])]
    yt, dx, tx, bt, dbt, dct, extra = call(
        local_kernel,
        [((INNER, T), BF), ((INNER, T), BF), ((INNER, T), BF), ((N, T), BF),
         ((N, T), F32), ((N, T), BF), ((1, T), F32)],
        BIG, 2_500_000_000, 6_000_000,
        in_specs=[VM] * 7 + [SM], out_specs=(VM,) * 7,
        scratch_shapes=[
            pltpu.VMEM((T, INNER + N), BF),
            pltpu.VMEM((INNER, T), F32), pltpu.VMEM((INNER, T), BF),
            pltpu.VMEM((INNER, N), BF), pltpu.VMEM((T, T), BF),
        ],
    )(u, c_nat, w_in, dy, cum, cumt, jnp.swapaxes(saved_state[0, 0], 1, 2).reshape(INNER, N), skip)
    sums, yt = lax.optimization_barrier((sums, yt))
    (total,) = call(
        inner_kernel, [((MR, N), BF)], 8, 2_000_000, 400_000,
        in_specs=[SM] + [VM] * 4, out_specs=(VM,), scratch_shapes=[pltpu.VMEM((4, MR, N), BF)],
    )(z, *sums)
    total, yt = lax.optimization_barrier((total, yt))
    totals = [total] + [hop(total, "y", k) for k in range(1, 4)]
    keep, give = call(
        out_kernel, [((INNER // 2, D), BF), ((INNER // 2, D), BF)], BIG, 270_000_000, 2_000_000,
        in_specs=[SM] + [VM] * 2, out_specs=(VM,) * 2,
    )(core, yt, d_out)
    totals, give, extra = lax.optimization_barrier((totals, give, extra))
    carries = call(
        outer_kernel, [((GR, N), BF)] * 4, 8, 4_000_000, 800_000,
        in_specs=[SM] * 2 + [VM] * 8, out_specs=(VM,) * 4,
        scratch_shapes=[pltpu.VMEM((4, MR, N), BF)] * 2 + [pltpu.VMEM((4, GR, N), BF)],
    )(y, z, *sums, *totals)
    carries = [carries[0]] + [hop(v, "z", k + 1) for k, v in enumerate(carries[1:])]
    outer, tx = call(
        pair_kernel, [((8 * DEV, E), BF), ((INNER, T), BF)], 8, 300_000, 3_000_000, in_specs=[VM] * 3, out_specs=(VM,) * 2
    )(keep, lax.ppermute(give, "core", [(0, 1), (1, 0)]), tx)
    misc, hits = call(
        slot_kernel, [((8 * DEV, E), BF), ((8 * DEV, T), BF)], 16, 300_000_000, 1_500_000,
        in_specs=[VM] * 2, out_specs=(VM,) * 2,
    )(event_index, extra)
    carries, outer, hits = lax.optimization_barrier((carries, outer, hits))
    (pay,) = call(
        finish_kernel, [((8 * DEV, 3 * E), BF)], 36, 1_400_000_000, 6_000_000,
        in_specs=[SM] + [VM] * 16, out_specs=(VM,),
        scratch_shapes=[pltpu.VMEM((INNER, N), BF), pltpu.VMEM((PROJ, T), BF)],
    )(z, *carries, outer, bt, cum, tx, dbt, dct, rows, w_up, hits, misc, dx, w_in)
    pay_got = lax.all_to_all(pay.reshape(DEV, 8, 3 * E), every, 0, 0, tiled=True)
    chunk, skip_sum = call(
        sum_kernel, [((DEV // 2, 8, 7 * N), BF), ((1, 128), F32)], 12, 2_000_000, 3_000_000,
        in_specs=[VM], out_specs=(VM,) * 2,
    )(pay_got)
    whole = lax.all_to_all(chunk, ("x", "y", "z"), 0, 0, tiled=True).reshape(DEV * 4, 7 * N)
    other = lax.ppermute(whole, "core", [(0, 1), (1, 0)])
    (table,) = call(
        table_kernel, [((ROWS_DEV, E), F32)], 12, 400_000_000, 2_000_000, in_specs=[VM], out_specs=(VM,)
    )(pay_got)
    column = pl.BlockSpec((E, D // 2), lambda i: (0, i))
    row = pl.BlockSpec((D // 2, PROJ), lambda i: (i, 0))
    grad_up, grad_in, grad_out = pl.pallas_call(
        last_kernel,
        grid=(2,),
        out_shape=tuple(jax.ShapeDtypeStruct(s, F32) for s in ((E, D), (D, PROJ), (INNER, D))),
        in_specs=[SM] + [VM] * 4,
        out_specs=(column, row, pl.BlockSpec((INNER // 2, D), lambda i: (i, 0))),
        scratch_shapes=[pltpu.VMEM((PROJ, E), BF), pltpu.VMEM((8 * DEV, N), BF)],
        compiler_params=pltpu.CompilerParams(vmem_limit_bytes=28 * MB),
        cost_estimate=pl.CostEstimate(flops=700_000_000, bytes_accessed=8_000_000, transcendentals=0),
    )(core, whole, other, w_up, w_in)
    grad_skip = skip_sum[0, :H] + skip_sum[0, 32 : 32 + H]
    return (grad_up, grad_in, grad_out, grad_skip, table)


def solution(mesh):
    mesh = Mesh(mesh.devices.reshape(4, 2, 4, 4), ("x", "core", "y", "z"))
    batch, ctx = ("x", "core"), ("y", "z")
    in_specs = (
        P(batch, ctx, None),
        P(batch, ctx),
        P(batch, None, ctx),
        P(batch, ctx, None, None, None),
        P(batch, ctx, None),
        P(),
        P(),
        P(),
        P(),
    )
    out_specs = (P(), P(), P(), P(), P(batch + ctx, None))
    return jax.shard_map(local, mesh=mesh, in_specs=in_specs, out_specs=out_specs, check_vma=False)
```

```python
from functools import partial

import jax
import jax.numpy as jnp
from jax import lax
from jax.experimental import pallas as pl
from jax.experimental.pallas import tpu as pltpu
from jax.sharding import Mesh, PartitionSpec as P

T = 256
E = 256
D = 512
H = 16
HP = 64
N = 128
INNER = H * HP
PROJ = INNER + 2 * N
ROWS_DEV = 512
CAP = 4
DEV = 128
CTX = 16
GH = 4
GR = GH * HP
MR = GR + 16

DT = 0.0625
SC = 128.0**-0.5
F32 = jnp.float32
BF = jnp.bfloat16
NN = (((1,), (0,)), ((), ()))
NT = (((1,), (1,)), ((), ()))
TN = (((0,), (0,)), ((), ()))
MB = 1 << 20
BIG = 60


def dot(a, b, dims=NN):
    return lax.dot_general(a, b, dims, preferred_element_type=F32)


def split3(v):
    hi = v.astype(BF)
    rest = v - hi.astype(F32)
    mid = rest.astype(BF)
    return hi, mid, (rest - mid.astype(F32)).astype(BF)


def call(kernel, outs, vmem, flops, nbytes, **kw):
    return pl.pallas_call(
        kernel,
        out_shape=tuple(jax.ShapeDtypeStruct(s, d) for s, d in outs),
        compiler_params=pltpu.CompilerParams(vmem_limit_bytes=vmem * MB),
        cost_estimate=pl.CostEstimate(flops=flops, bytes_accessed=nbytes, transcendentals=0),
        **kw,
    )


VM = pl.BlockSpec(memory_space=pltpu.VMEM)
HBM = pl.BlockSpec(memory_space=pltpu.HBM)
SM = pl.BlockSpec(memory_space=pltpu.SMEM)


def decay_rows(amounts):
    row = lax.broadcasted_iota(jnp.int32, (MR - GR, N), 0)
    out = jnp.zeros((MR - GR, N), F32)
    for i, amount in enumerate(amounts):
        for k, part in enumerate(split3(amount)):
            out = jnp.where(row == 3 * i + k, part.astype(F32), out)
    return out.astype(BF)


def decays(ref, at):
    rows = ref[at, GR:, :].astype(F32)
    return [rows[3 * i : 3 * i + 1] + rows[3 * i + 1 : 3 * i + 2] + rows[3 * i + 2 : 3 * i + 3] for i in range(GH)]


def sums_of(ref, at, i):
    return ref[at, i * HP : (i + 1) * HP, :].astype(F32)


def project_kernel(z_ref, rows_hbm, dout_hbm, decay_hbm, w_up_hbm, w_in_hbm, w_out_hbm,
                   u_ref, c_ref, dy_ref, cum_ref, cumt_ref, g0_ref, g1_ref, g2_ref, g3_ref,
                   rows_ref, dout_ref, decay_ref, w_up_ref, w_c_ref, w_out_ref, all_ref, sems):
    pairs = (
        (rows_hbm, rows_ref), (w_up_hbm, w_up_ref), (w_in_hbm.at[:, INNER + N :], w_c_ref),
        (dout_hbm, dout_ref), (w_out_hbm, w_out_ref), (decay_hbm, decay_ref),
    )
    copies = [pltpu.make_async_copy(a, b, sems.at[i]) for i, (a, b) in enumerate(pairs)]
    for copy in copies:
        copy.start()
    copies[0].wait()
    copies[1].wait()
    u_ref[...] = dot(rows_ref[...], w_up_ref[...]).astype(BF)
    copies[2].wait()
    c_ref[...] = dot(u_ref[...], w_c_ref[...]).astype(BF)
    copies[3].wait()
    copies[4].wait()
    dy_ref[...] = dot(w_out_ref[...], dout_ref[...], NT).astype(BF)
    copies[5].wait()
    logs = split3(jnp.log(decay_ref[...]))
    r = lax.broadcasted_iota(jnp.int32, (T, T), 0)
    c = lax.broadcasted_iota(jnp.int32, (T, T), 1)
    upper = (r <= c).astype(F32).astype(BF)
    lower = (c <= r).astype(F32).astype(BF)
    cum = sum(dot(p, upper) for p in logs)
    cum_ref[...] = cum
    cumt_ref[...] = sum(dot(lower, p, NT) for p in logs)
    start = jnp.exp(cum)
    scaled = jnp.concatenate(
        [
            (dy_ref[h * HP : (h + 1) * HP, :].astype(F32) * (SC * start[h : h + 1, :])).astype(BF)
            for h in range(H)
        ],
        axis=0,
    )
    sums = dot(scaled, c_ref[...]).astype(BF)
    amount = jnp.exp(cum[:, T - 1 : T])
    for q in range(H // GH):
        all_ref[q, :GR, :] = sums[q * GR : (q + 1) * GR, :]
        all_ref[q, GR:, :] = decay_rows([jnp.broadcast_to(amount[h : h + 1, :], (1, N)) for h in range(q * GH, (q + 1) * GH)])
    for k, ref in enumerate((g0_ref, g1_ref, g2_ref, g3_ref)):
        ref[...] = all_ref[(z_ref[0] + k) & 3]


def place(at, refs, out_ref):
    for k, ref in enumerate(refs):
        out_ref[(at + 4 - k) & 3] = ref[...]


def inner_kernel(z_ref, a_ref, b_ref, c_ref, d_ref, out_ref, st_ref):
    place(z_ref[0], (a_ref, b_ref, c_ref, d_ref), st_ref)
    amounts = [decays(st_ref, zz) for zz in range(4)]
    for i in range(GH):
        carry = sums_of(st_ref, 3, i)
        for zz in (2, 1, 0):
            carry = sums_of(st_ref, zz, i) + amounts[zz][i] * carry
        out_ref[i * HP : (i + 1) * HP, :] = carry.astype(BF)
    out_ref[GR:, :] = decay_rows([amounts[0][i] * amounts[1][i] * amounts[2][i] * amounts[3][i] for i in range(GH)])


def outer_kernel(y_ref, z_ref, a_ref, b_ref, c_ref, d_ref, ta_ref, tb_ref, tc_ref, td_ref,
                 g0_ref, g1_ref, g2_ref, g3_ref, st_ref, tt_ref, ct_ref):
    y, z = y_ref[0], z_ref[0]
    place(z, (a_ref, b_ref, c_ref, d_ref), st_ref)
    place(y, (ta_ref, tb_ref, tc_ref, td_ref), tt_ref)
    inner = [decays(st_ref, zz) for zz in range(4)]
    outer = [decays(tt_ref, yy) for yy in range(4)]
    for i in range(GH):
        carry = jnp.zeros((HP, N), F32)
        for yy in (3, 2, 1):
            carry = jnp.where(yy > y, sums_of(tt_ref, yy, i) + outer[yy][i] * carry, carry)
        for zz in (3, 2, 1, 0):
            ct_ref[zz, i * HP : (i + 1) * HP, :] = carry.astype(BF)
            if zz:
                carry = sums_of(st_ref, zz, i) + inner[zz][i] * carry
    for k, ref in enumerate((g0_ref, g1_ref, g2_ref, g3_ref)):
        ref[...] = ct_ref[(z + k) & 3]


def local_kernel(u_ref, c_ref, w_in_ref, dy_ref, cum_ref, cumt_ref, h0_ref, skip_ref,
                 yt_ref, dx_ref, tx_ref, bt_ref, dbt_ref, dct_ref, extra_ref, x_ref, y_ref, sdy_ref, h0t_ref, sum_ref):
    x_ref[...] = dot(u_ref[...], w_in_ref[:, : INNER + N]).astype(BF)
    proj_t = jnp.transpose(x_ref[...])
    bt = proj_t[INNER:, :]
    c_nat = c_ref[...]
    ct = jnp.transpose(c_nat)
    b_nat = x_ref[:, INNER:]
    pair = (SC * DT) * dot(b_nat, c_nat, NT)
    r = lax.broadcasted_iota(jnp.int32, (N, N), 0)
    c = lax.broadcasted_iota(jnp.int32, (N, N), 1)
    causal = r <= c
    cum = cum_ref[...]
    cumt = cumt_ref[...]
    start = jnp.exp(cum)
    tail = DT * jnp.exp(cum[:, T - 1 : T] - cum)
    bt_ref[...] = bt
    h0t_ref[...] = h0_ref[...].astype(BF)
    y_ref[...] = dot(h0t_ref[...], ct)
    skip_sums = []
    a00 = jnp.zeros((N, N), F32)
    a01 = jnp.zeros((N, N), F32)
    a11 = jnp.zeros((N, N), F32)
    zero = jnp.zeros((N, N), BF)
    zrow = jnp.zeros((HP, T), BF)
    for h in range(H):
        lo, hi = h * HP, (h + 1) * HP
        row0, row1 = cum[h : h + 1, :N], cum[h : h + 1, N:]
        col0, col1 = cumt[:N, h : h + 1], cumt[N:, h : h + 1]
        m00 = jnp.exp(jnp.where(causal, row0 - col0, -1e30))
        m01 = jnp.exp(row1 - col0)
        m11 = jnp.exp(jnp.where(causal, row1 - col1, -1e30))
        weights = jnp.concatenate(
            [
                jnp.concatenate([(m00 * pair[:N, :N]).astype(BF), (m01 * pair[:N, N:]).astype(BF)], axis=1),
                jnp.concatenate([zero, (m11 * pair[N:, N:]).astype(BF)], axis=1),
            ],
            axis=0,
        )
        x_h = proj_t[lo:hi, :]
        dy_h = dy_ref[lo:hi, :]
        x_f, dy_f = x_h.astype(F32), dy_h.astype(F32)
        st = start[h : h + 1, :]
        skip = skip_ref[h]
        y_ref[lo:hi, :] = dot(x_h, weights) + SC * st * y_ref[lo:hi, :] + skip * x_f
        dx_ref[lo:hi, :] = (dot(dy_h, weights, NT) + skip * dy_f).astype(BF)
        sdy_ref[lo:hi, :] = (st * dy_f).astype(BF)
        tx_ref[lo:hi, :] = (tail[h : h + 1, :] * x_f).astype(BF)
        x_pair = x_ref[:, (h // 2) * N : (h // 2 + 1) * N]
        dy_z = jnp.concatenate([dy_h, zrow] if h % 2 == 0 else [zrow, dy_h], axis=0)
        q0 = dot(x_pair[:N, :], dy_z)
        q11 = dot(x_pair[N:, :], dy_z[:, N:])
        a00 += m00 * q0[:, :N]
        a01 += m01 * q0[:, N:]
        a11 += m11 * q11
        skip_sums.append(jnp.sum(x_f * dy_f, keepdims=True))
    yt_ref[...] = y_ref[...].astype(BF)
    sum_ref[:N, :N] = a00.astype(BF)
    sum_ref[:N, N:] = a01.astype(BF)
    sum_ref[N:, :N] = zero
    sum_ref[N:, N:] = a11.astype(BF)
    a = sum_ref[...]
    dct_ref[...] = (SC * (DT * dot(bt, a) + dot(h0t_ref[...], sdy_ref[...], TN))).astype(BF)
    dbt_ref[...] = (DT * SC) * dot(ct, a, NT)
    lane = lax.broadcasted_iota(jnp.int32, (1, T), 1)
    extra = jnp.zeros((1, T), F32)
    for h in range(H):
        whole = skip_sums[h]
        top = whole.astype(BF).astype(F32)
        extra = extra + jnp.where(lane == 128 + h, top, 0.0) + jnp.where(lane == 160 + h, whole - top, 0.0)
    extra_ref[...] = extra


def out_kernel(core_ref, y_ref, dout_ref, keep_ref, give_ref):
    core = core_ref[0]
    half = INNER // 2
    mine = pl.ds(pl.multiple_of(core * half, half), half)
    other = pl.ds(pl.multiple_of((1 - core) * half, half), half)
    give_ref[...] = dot(y_ref[other, :], dout_ref[...]).astype(BF)
    keep_ref[...] = dot(y_ref[mine, :], dout_ref[...]).astype(BF)


def slot_kernel(index_ref, extra_ref, misc_ref, hits_ref):
    index = index_ref[...]
    owner_row = lax.shift_right_logical(index, 9)
    rr = lax.broadcasted_iota(jnp.int32, (T, T), 0)
    cc = lax.broadcasted_iota(jnp.int32, (T, T), 1)
    index_col = jnp.sum(jnp.where(rr == cc, index.astype(F32), 0.0), axis=1, keepdims=True)
    index_col = index_col.astype(jnp.int32)
    owner_col = lax.shift_right_logical(index_col, 9)
    same = owner_col == owner_row
    rank_row = jnp.sum(jnp.where(same & (rr < cc), 1.0, 0.0), axis=0, keepdims=True).astype(jnp.int32)
    rank_col = jnp.sum(jnp.where(same & (cc < rr), 1.0, 0.0), axis=1, keepdims=True).astype(jnp.int32)
    local_col = index_col - owner_col * ROWS_DEV
    id_hi = lax.shift_right_logical(local_col, 1)
    id_lo = local_col - 2 * id_hi
    v = jnp.where(cc == rank_col, id_hi, jnp.where(cc == rank_col + 64, id_lo, 0))
    row_id = lax.broadcasted_iota(jnp.int32, (8 * DEV, T), 0)
    hits_ref[...] = jnp.where(row_id == owner_row * 8 + 2 + rank_row, 1.0, 0.0).astype(BF)
    heads = jnp.where(row_id == owner_row * 8 + 6, 1.0, 0.0).astype(BF)
    misc = dot(heads, v.astype(F32).astype(BF))
    misc_ref[...] = (misc + jnp.where((row_id & 7) == 6, extra_ref[...], 0.0)).astype(BF)


def finish_kernel(z_ref, c0_ref, c1_ref, c2_ref, c3_ref, outer_ref, bt_ref, cum_ref, tx_ref, dbt_ref, dct_ref,
                  rows_ref, w_up_ref, hits_ref, misc_ref, dx_ref, w_in_ref, out_ref, carry_ref, d_ref):
    out_ref[:, 2 * E :] = outer_ref[...]
    for k, ref in enumerate((c0_ref, c1_ref, c2_ref, c3_ref)):
        carry_ref[pl.ds(pl.multiple_of(((z_ref[0] + 4 - k) & 3) * GR, GR), GR), :] = ref[...]
    cum = cum_ref[...]
    tail = DT * jnp.exp(cum[:, T - 1 : T] - cum)
    carry = carry_ref[...]
    entering = dot(carry, bt_ref[...])
    for h in range(H):
        lo, hi = h * HP, (h + 1) * HP
        d_ref[lo:hi, :] = (dx_ref[lo:hi, :].astype(F32) + tail[h : h + 1, :] * entering[lo:hi, :]).astype(BF)
    d_ref[INNER + N :, :] = dct_ref[...]
    d_ref[INNER : INNER + N, :] = (dbt_ref[...] + dot(carry, tx_ref[...], TN)).astype(BF)
    d = d_ref[...]
    g = dot(d, rows_ref[...]).astype(BF)
    out_ref[:, :E] = g[:INNER, :]
    du = dot(w_in_ref[...], d).astype(BF)
    de = dot(w_up_ref[...], du).astype(BF)
    r = lax.broadcasted_iota(jnp.int32, (8 * DEV, 2 * N), 0)
    j = lax.broadcasted_iota(jnp.int32, (1, 2 * N), 1)
    place = jnp.where(r == 8 * lax.shift_right_logical(j, 1) + (j & 1), 1.0, 0.0).astype(BF)
    misc = misc_ref[...].astype(F32) + dot(hits_ref[...], de, NT) + dot(place, g[INNER:, :])
    out_ref[:, E : 2 * E] = misc.astype(BF)


def pair_kernel(keep_ref, got_ref, tx_ref, out_ref, tx_out_ref):
    tx_out_ref[...] = tx_ref[...]
    total = (keep_ref[...].astype(F32) + got_ref[...].astype(F32)).astype(BF)
    out_ref[: INNER // 2, :] = total[:, :E]
    out_ref[INNER // 2 :, :] = total[:, E:]


def sum_kernel(got_ref, chunk_ref, skip_ref):
    total = jnp.sum(got_ref[:, :, : 2 * E].astype(F32), axis=0)
    side = jnp.concatenate([total[0:2, E : E + N], total[0:2, E + N :], jnp.zeros((4, N), F32)], axis=0)
    outer = got_ref[:, :, 2 * E :].reshape(4, 2, CTX, 8, E)
    halves = [jnp.sum(outer[:, c].reshape(DEV // 2, 8, E).astype(F32), axis=0) for c in range(2)]
    chunk = jnp.concatenate([total[:, :E], side] + halves, axis=1)
    chunk_ref[...] = jnp.broadcast_to(chunk[None], chunk_ref.shape).astype(BF)
    skip_ref[...] = total[6:7, E + 128 : E + 256]


def table_kernel(got_ref, table_ref):
    misc = got_ref[:, :, E : 2 * E]
    ids = misc[:, 6:7, 0:128].astype(F32)
    sub = lax.broadcasted_iota(jnp.int32, (DEV, 8, 128), 1) - 2
    lane = lax.broadcasted_iota(jnp.int32, (DEV, 8, 128), 2)
    want = jnp.where(lane == sub, 2.0, jnp.where(lane == sub + 64, 1.0, 0.0))
    row = jnp.sum(ids * want, axis=2, keepdims=True)
    row = jnp.where((sub[:, :, :1] >= 0) & (sub[:, :, :1] < CAP), row, -1.0)
    rid = lax.broadcasted_iota(jnp.int32, (DEV, 8, ROWS_DEV), 2).astype(F32)
    hits = jnp.where(rid == row, 1.0, 0.0).reshape(DEV * 8, ROWS_DEV).astype(BF)
    table_ref[...] = dot(hits, misc.reshape(DEV * 8, E), TN)


def last_kernel(core_ref, own_ref, other_ref, w_up_ref, w_in_ref, up_ref, in_ref, go_ref, g_ref, side_ref):
    step = pl.program_id(0)
    core = core_ref[0]
    sources = ((core, own_ref), (1 - core, other_ref))

    @pl.when(step == 0)
    def _():
        for x in range(4):
            for at, ref in sources:
                rows = pl.ds(pl.multiple_of((2 * x + at) * N, N), N)
                g_ref[rows, :] = ref[x * N : (x + 1) * N, :E]
                side_ref[rows, :] = ref[x * N : (x + 1) * N, E : E + N]
        j = lax.broadcasted_iota(jnp.int32, (2 * N, 8 * DEV), 0)
        r = lax.broadcasted_iota(jnp.int32, (2 * N, 8 * DEV), 1)
        first = r - (8 * lax.shift_right_logical(j, 1) + (j & 1))
        for m in range(2):
            pick = jnp.where(first == 2 * m, 1.0, 0.0).astype(BF)
            g_ref[INNER:, m * N : (m + 1) * N] = dot(pick, side_ref[...]).astype(BF)

    g = g_ref[...]
    part = pl.ds(pl.multiple_of(step * E, E), E)
    in_ref[...] = lax.dot_general(w_up_ref[:, part], g, (((0,), (1,)), ((), ())), preferred_element_type=F32)
    up_ref[...] = jnp.transpose(dot(w_in_ref[part, :], g))
    lanes = pl.ds(pl.multiple_of(E + N + E * step, N), E)
    for x in range(4):
        for at, ref in sources:
            rows = pl.ds(pl.multiple_of((x & 1) * E + at * N, N), N)
            go_ref[rows, (x >> 1) * E : (x >> 1) * E + E] = ref[x * N : (x + 1) * N, lanes].astype(F32)


def hop(value, axis, step):
    return lax.ppermute(value, axis, [(i, (i + step) % 4) for i in range(4)])


def local(event_rows, event_index, decay, saved_state, dout, w_up, w_in, w_out, skip):
    every = ("x", "core", "y", "z")
    rows, d_out = event_rows[0], dout[0]
    core, y, z = (lax.axis_index(a).reshape(1) for a in ("core", "y", "z"))
    u, c_nat, dy, cum, cumt, *sums = call(
        project_kernel,
        [((T, D), BF), ((T, N), BF), ((INNER, T), BF), ((H, T), F32), ((T, H), F32)] + [((MR, N), BF)] * 4,
        BIG, 750_000_000, 4_500_000,
        in_specs=[SM] + [HBM] * 6, out_specs=(VM,) * 9,
        scratch_shapes=[
            pltpu.VMEM((T, E), BF), pltpu.VMEM((T, D), BF), pltpu.VMEM((H, T), F32),
            pltpu.VMEM((E, D), BF), pltpu.VMEM((D, N), BF), pltpu.VMEM((INNER, D), BF),
            pltpu.VMEM((4, MR, N), BF), pltpu.SemaphoreType.DMA((6,)),
        ],
    )(z, rows, d_out, decay[0], w_up, w_in, w_out)
    sums = sums[:1] + [hop(v, "z", k + 1) for k, v in enumerate(sums[1:])]
    yt, dx, tx, bt, dbt, dct, extra = call(
        local_kernel,
        [((INNER, T), BF), ((INNER, T), BF), ((INNER, T), BF), ((N, T), BF),
         ((N, T), F32), ((N, T), BF), ((1, T), F32)],
        BIG, 2_500_000_000, 6_000_000,
        in_specs=[VM] * 7 + [SM], out_specs=(VM,) * 7,
        scratch_shapes=[
            pltpu.VMEM((T, INNER + N), BF),
            pltpu.VMEM((INNER, T), F32), pltpu.VMEM((INNER, T), BF),
            pltpu.VMEM((INNER, N), BF), pltpu.VMEM((T, T), BF),
        ],
    )(u, c_nat, w_in, dy, cum, cumt, jnp.swapaxes(saved_state[0, 0], 1, 2).reshape(INNER, N), skip)
    sums, yt = lax.optimization_barrier((sums, yt))
    (total,) = call(
        inner_kernel, [((MR, N), BF)], 8, 2_000_000, 400_000,
        in_specs=[SM] + [VM] * 4, out_specs=(VM,), scratch_shapes=[pltpu.VMEM((4, MR, N), BF)],
    )(z, *sums)
    total, yt = lax.optimization_barrier((total, yt))
    totals = [total] + [hop(total, "y", k) for k in range(1, 4)]
    keep, give = call(
        out_kernel, [((INNER // 2, D), BF), ((INNER // 2, D), BF)], BIG, 270_000_000, 2_000_000,
        in_specs=[SM] + [VM] * 2, out_specs=(VM,) * 2,
    )(core, yt, d_out)
    totals, keep, extra = lax.optimization_barrier((totals, keep, extra))
    carries = call(
        outer_kernel, [((GR, N), BF)] * 4, 8, 4_000_000, 800_000,
        in_specs=[SM] * 2 + [VM] * 8, out_specs=(VM,) * 4,
        scratch_shapes=[pltpu.VMEM((4, MR, N), BF)] * 2 + [pltpu.VMEM((4, GR, N), BF)],
    )(y, z, *sums, *totals)
    carries, give = lax.optimization_barrier((carries, give))
    carries = [carries[0]] + [hop(v, "z", k + 1) for k, v in enumerate(carries[1:])]
    outer, tx = call(
        pair_kernel, [((8 * DEV, E), BF), ((INNER, T), BF)], 8, 300_000, 3_000_000, in_specs=[VM] * 3, out_specs=(VM,) * 2
    )(keep, lax.ppermute(give, "core", [(0, 1), (1, 0)]), tx)
    misc, hits = call(
        slot_kernel, [((8 * DEV, E), BF), ((8 * DEV, T), BF)], 16, 300_000_000, 1_500_000,
        in_specs=[VM] * 2, out_specs=(VM,) * 2,
    )(event_index, extra)
    carries, outer, hits = lax.optimization_barrier((carries, outer, hits))
    (pay,) = call(
        finish_kernel, [((8 * DEV, 3 * E), BF)], 36, 1_400_000_000, 6_000_000,
        in_specs=[SM] + [VM] * 16, out_specs=(VM,),
        scratch_shapes=[pltpu.VMEM((INNER, N), BF), pltpu.VMEM((PROJ, T), BF)],
    )(z, *carries, outer, bt, cum, tx, dbt, dct, rows, w_up, hits, misc, dx, w_in)
    pay_got = lax.all_to_all(pay.reshape(DEV, 8, 3 * E), every, 0, 0, tiled=True)
    chunk, skip_sum = call(
        sum_kernel, [((DEV // 2, 8, 7 * N), BF), ((1, 128), F32)], 12, 2_000_000, 3_000_000,
        in_specs=[VM], out_specs=(VM,) * 2,
    )(pay_got)
    whole = lax.all_to_all(chunk, ("x", "y", "z"), 0, 0, tiled=True).reshape(DEV * 4, 7 * N)
    other = lax.ppermute(whole, "core", [(0, 1), (1, 0)])
    (table,) = call(
        table_kernel, [((ROWS_DEV, E), F32)], 12, 400_000_000, 2_000_000, in_specs=[VM], out_specs=(VM,)
    )(pay_got)
    column = pl.BlockSpec((E, D // 2), lambda i: (0, i))
    row = pl.BlockSpec((D // 2, PROJ), lambda i: (i, 0))
    grad_up, grad_in, grad_out = pl.pallas_call(
        last_kernel,
        grid=(2,),
        out_shape=tuple(jax.ShapeDtypeStruct(s, F32) for s in ((E, D), (D, PROJ), (INNER, D))),
        in_specs=[SM] + [VM] * 4,
        out_specs=(column, row, pl.BlockSpec((INNER // 2, D), lambda i: (i, 0))),
        scratch_shapes=[pltpu.VMEM((PROJ, E), BF), pltpu.VMEM((8 * DEV, N), BF)],
        compiler_params=pltpu.CompilerParams(vmem_limit_bytes=28 * MB),
        cost_estimate=pl.CostEstimate(flops=700_000_000, bytes_accessed=8_000_000, transcendentals=0),
    )(core, whole, other, w_up, w_in)
    grad_skip = skip_sum[0, :H] + skip_sum[0, 32 : 32 + H]
    return (grad_up, grad_in, grad_out, grad_skip, table)


def solution(mesh):
    mesh = Mesh(mesh.devices.reshape(4, 2, 4, 4), ("x", "core", "y", "z"))
    batch, ctx = ("x", "core"), ("y", "z")
    in_specs = (
        P(batch, ctx, None),
        P(batch, ctx),
        P(batch, None, ctx),
        P(batch, ctx, None, None, None),
        P(batch, ctx, None),
        P(),
        P(),
        P(),
        P(),
    )
    out_specs = (P(), P(), P(), P(), P(batch + ctx, None))
    return jax.shard_map(local, mesh=mesh, in_specs=in_specs, out_specs=out_specs, check_vma=False)
```
